32 devices in a mesh: dp: 2 (over core), ctx: 4 (over y, x), tp: 4 (over z).
Axes of the slice: x: 2, y: 2, z: 4, core: 2. Of those that a mesh axis runs over, the one named last changes fastest.
Arguments:
- tokens: bfloat16 [4, 1024, 768], P('dp', ('ctx', 'tp')), may hold values from -6 to 6
- timesteps: int32 [4, 4], P('dp', 'ctx'), may hold values from 0 to 999
- query_weight: bfloat16 [768, 768], P('dp', 'tp'), may hold values from -0.21875 to 0.21875
- key_weight: bfloat16 [768, 768], P('dp', 'tp'), may hold values from -0.21875 to 0.21875
- value_weight: bfloat16 [768, 768], P('dp', 'tp'), may hold values from -0.21875 to 0.21875
- out_weight: bfloat16 [768, 768], P('dp', 'tp'), may hold values from -6 to 6
- up_weight: bfloat16 [768, 3072], P('dp', 'tp'), may hold values from -0.21875 to 0.21875
- down_weight: bfloat16 [768, 3072], P('dp', 'tp'), may hold values from -0.21875 to 0.21875
- modulation_weight: bfloat16 [768, 4608], P('dp'), may hold values from -0.4375 to 0.4375
- cotangent: bfloat16 [4, 1024, 768], P('dp', ('ctx', 'tp')), may hold values from -6 to 6
Outputs:
- result: bfloat16 [4, 1024, 768], P('dp', ('ctx', 'tp'))
- grad_tokens: float32 [4, 1024, 768], P('dp', ('ctx', 'tp'))
- grad_query: float32 [768, 768], P('dp', 'tp')
- grad_key: float32 [768, 768], P('dp', 'tp')
- grad_value: float32 [768, 768], P('dp', 'tp')
- grad_out: float32 [768, 768], P('dp', 'tp')
- grad_up: float32 [768, 3072], P('dp', 'tp')
- grad_down: float32 [768, 3072], P('dp', 'tp')
- grad_modulation: float32 [768, 4608], P('dp', 'tp')
The draws below stay inside these ranges and needn't reach their ends.
All inputs are finite; a program needn't handle non-finite values.
Results may differ from the reference program's by a relative error of at most 0.019.
Values may be sent and summed in bfloat16 or wider, within the bound.
A program may use at most 128 MiB of HBM per device.

```python
import math
import jax
import jax.numpy as jnp
from jax import lax

D = 768
HEADS = 12
HEAD_DIM = 64
FF = 3072
BLK = 256
TSTEPS = 1000
LENGTH = 1024
SEQS = 4
N_CTX = 4


def touch_ends(entries, key, least, largest):
    spot = [jax.random.randint(jax.random.fold_in(key, axis), (), 0, length) for axis, length in enumerate(entries.shape)]
    longest = entries.shape.index(max(entries.shape))
    neighbour = spot[:longest] + [(spot[longest] + 1) % entries.shape[longest]] + spot[longest + 1:]
    return entries.at[tuple(spot)].set(least).at[tuple(neighbour)].set(largest)


def shard_levels(stream_key, extent, pieces, smallest, largest):
    level = 1.0
    for dim, blocks in pieces:
        heights = jax.random.uniform(jax.random.fold_in(jax.random.fold_in(stream_key, 6), dim), (blocks,), jnp.float32, smallest / len(pieces), largest / len(pieces))
        level = level * jnp.repeat(jnp.exp(heights), extent[dim] // blocks).reshape((-1,) + (1,) * (len(extent) - 1 - dim))
    return level


def normal_values(rng, dims, scale, bound, shards=(), kind=jnp.bfloat16):
    level = shard_levels(rng, dims, shards, -0.22, 0.18) if shards else 1.0
    drawn = jax.random.normal(rng, dims, jnp.float32) * scale * level
    return jnp.minimum(jnp.maximum(drawn, -bound), bound).astype(kind)


def setup_inputs(seed: int = 0) -> dict:
    arg_keys = jax.random.split(jax.random.key(seed), 11)
    tokens = normal_values(arg_keys[0], (SEQS, LENGTH, D), 1.0, 6.0, ((0, 2), (1, 16)))
    timesteps = touch_ends(jax.random.randint(arg_keys[1], (SEQS, N_CTX), 0, TSTEPS), jax.random.fold_in(arg_keys[1], 1), 0, TSTEPS - 1).astype(jnp.int32)
    query_weight = normal_values(arg_keys[2], (D, D), D ** -0.5, 0.21875, ((0, 2), (1, 4)))
    key_weight = normal_values(arg_keys[3], (D, D), D ** -0.5, 0.21875, ((0, 2), (1, 4)))
    value_weight = normal_values(arg_keys[4], (D, D), D ** -0.5, 0.21875, ((0, 2), (1, 4)))
    out_weight = normal_values(arg_keys[5], (D, D), 1 ** -0.5, 6.0, ((0, 2), (1, 4)))
    up_weight = normal_values(arg_keys[6], (D, FF), D ** -0.5, 0.21875, ((0, 2), (1, 4)))
    down_weight = normal_values(arg_keys[7], (D, FF), (FF // 4) ** -0.5, 0.21875, ((0, 2), (1, 4)))
    modulation_weight = normal_values(arg_keys[8], (D, 6 * D), (D // 4) ** -0.5, 0.4375, ((0, 2),))
    cotangent = normal_values(arg_keys[9], (SEQS, LENGTH, D), 1.0, 6.0, ((0, 2), (1, 16)))
    return dict(tokens=tokens, timesteps=timesteps, query_weight=query_weight, key_weight=key_weight, value_weight=value_weight, out_weight=out_weight, up_weight=up_weight, down_weight=down_weight, modulation_weight=modulation_weight, cotangent=cotangent)


norm_eps = 1e-06
highest = lax.Precision.HIGHEST

@jax.custom_vjp
def low(v):
    return lax.optimization_barrier(v.astype(jnp.bfloat16)).astype(jnp.float32)

@jax.custom_vjp
def low_back(v):
    return v

def low_keep(v):
    return (low(v), None)

def low_pass(kept, grad):
    return (grad,)

def back_keep(v):
    return (v, None)

def back_low(kept, grad):
    return (low(grad),)
low.defvjp(low_keep, low_pass)
low_back.defvjp(back_keep, back_low)

def norm_rows(row_data):
    center = row_data - lax.optimization_barrier(jnp.mean(row_data, axis=-1, keepdims=True))
    spread = lax.optimization_barrier(jnp.mean(center * center, axis=-1, keepdims=True))
    return center * lax.rsqrt(spread + norm_eps)

def rotate(row_data, places, turn_sign):
    half_dim = row_data.shape[-1] // 2
    freq_rates = jnp.exp(jnp.arange(half_dim, dtype=jnp.float32) * (-2.0 * math.log(10000.0) / row_data.shape[-1]))
    angles = places.astype(jnp.float32)[:, None] * freq_rates[None, :]
    cosine = jnp.cos(angles)[:, None, :]
    sine_part = turn_sign * jnp.sin(angles)[:, None, :]
    first_half = row_data[..., :half_dim]
    second_half = row_data[..., half_dim:]
    return jnp.concatenate([first_half * cosine - second_half * sine_part, first_half * sine_part + second_half * cosine], axis=-1)

def time_embed(step_ids, model_width):
    half_dim = model_width // 2
    freq_rates = jnp.exp(jnp.arange(half_dim, dtype=jnp.float32) * (-math.log(10000.0) / half_dim))
    angles = step_ids.astype(jnp.float32)[..., None] * freq_rates
    return jnp.concatenate([jnp.sin(angles), jnp.cos(angles)], axis=-1)

def attend(queries, key_rows, values):
    length = queries.shape[1]
    query_len = min(512, length)
    score_scale = HEAD_DIM ** (-0.5)
    key_block = jnp.arange(length).astype(jnp.int32) // BLK

    def one_block(block_idx):
        first_row = (block_idx * query_len).astype(jnp.int32)
        query_part = lax.dynamic_slice_in_dim(queries, first_row, query_len, 1)
        raw_scores = low_back(jnp.einsum('gqhd,gkhd->ghqk', query_part, key_rows, precision=highest))
        scores = raw_scores * score_scale
        query_block = (first_row + jnp.arange(query_len).astype(jnp.int32)) // BLK
        allowed = key_block[None, :] <= query_block[:, None]
        scores = jnp.where(allowed, scores, -1e+30)
        log_norm = jax.nn.logsumexp(scores, axis=-1, keepdims=True)
        prob_tile = low(jnp.exp(scores - log_norm))
        return jnp.einsum('ghqk,gkhd->gqhd', prob_tile, values, precision=highest)
    blocks = lax.map(jax.checkpoint(one_block), jnp.arange(length // query_len).astype(jnp.int32))
    return jnp.transpose(blocks, (1, 0, 2, 3, 4)).reshape(queries.shape)

def block_layer(row_in, embed_in, query_weight, key_weight, value_weight, out_weight, up_weight, down_weight, modulation_weight):
    group_size, length, model_width = row_in.shape
    block_count = length // BLK
    modulation = jnp.einsum('gbd,de->gbe', embed_in, modulation_weight, precision=highest).reshape(group_size, block_count, 6, 1, model_width)
    shift_one, scale_one, gate_one, shift_two, scale_two, gate_two = [modulation[:, :, slot_idx] for slot_idx in range(6)]
    residual = row_in.reshape(group_size, block_count, BLK, model_width)
    normed = low(norm_rows(residual) * (1.0 + scale_one) + shift_one).reshape(group_size * length, model_width)
    places = jnp.arange(length).astype(jnp.int32)
    head_shape = (group_size, length, HEADS, HEAD_DIM)
    query_pre = low_back(jnp.dot(normed, query_weight, precision=highest)).reshape(head_shape)
    key_pre = low_back(jnp.dot(normed, key_weight, precision=highest)).reshape(head_shape)
    queries = low(rotate(query_pre, places, 1.0))
    key_rows = low(rotate(key_pre, places, 1.0))
    values = low(low_back(jnp.dot(normed, value_weight, precision=highest))).reshape(head_shape)
    attended = low(low_back(attend(queries, key_rows, values))).reshape(group_size * length, model_width)
    branch = low_back(jnp.dot(attended, out_weight.T, precision=highest)).reshape(group_size, block_count, BLK, model_width)
    middle = residual + gate_one * branch
    normed_two = low(norm_rows(middle) * (1.0 + scale_two) + shift_two).reshape(group_size * length, model_width)
    hidden = low_back(jnp.dot(normed_two, up_weight, precision=highest))
    active = low(jax.nn.gelu(hidden))
    mlp_branch = low_back(jnp.dot(active, down_weight.T, precision=highest)).reshape(group_size, block_count, BLK, model_width)
    return (middle + gate_two * mlp_branch).reshape(group_size, length, model_width)

def reference(tokens, timesteps, query_weight, key_weight, value_weight, out_weight, up_weight, down_weight, modulation_weight, cotangent):
    group_size = math.gcd(SEQS, max(1, 4096 // LENGTH))
    rounds = SEQS // group_size
    params = (query_weight.astype(jnp.float32), key_weight.astype(jnp.float32), value_weight.astype(jnp.float32), out_weight.astype(jnp.float32), up_weight.astype(jnp.float32), down_weight.astype(jnp.float32), modulation_weight.astype(jnp.float32))
    embed_low = low(jax.nn.silu(time_embed(timesteps, D)))
    token_all = tokens.astype(jnp.float32).reshape(rounds, group_size, LENGTH, D)
    embed_all = embed_low.reshape(rounds, group_size, N_CTX, D)
    cot_all = cotangent.astype(jnp.float32).reshape(rounds, group_size, LENGTH, D)

    def one_round(totals, round_in):
        row_in, embed_in, cot_in = round_in

        def forward(row_data, *weight_list):
            return block_layer(row_data, embed_in, *weight_list)
        output, pull = jax.vjp(forward, row_in, *params)
        gradients = pull(cot_in)
        totals = tuple((running_sum + grad_part for running_sum, grad_part in zip(totals, gradients[1:])))
        return (totals, (output.astype(jnp.bfloat16), gradients[0]))
    zero_start = tuple((jnp.zeros(weight.shape, jnp.float32) for weight in params))
    totals, (outputs, input_grads) = lax.scan(one_round, zero_start, (token_all, embed_all, cot_all))
    return (outputs.reshape(SEQS, LENGTH, D), input_grads.reshape(SEQS, LENGTH, D), totals[0], totals[1], totals[2], totals[3], totals[4], totals[5], totals[6])
```

```python
import functools
import math

import jax
import jax.numpy as jnp
from jax import lax
from jax.experimental import pallas as pl
from jax.experimental.pallas import tpu as pltpu
from jax.sharding import PartitionSpec as P

MESH = pl.DeviceIdType.MESH
HEAD_DIM = 64
WIN = 256
LANES = 128
EPS = 1e-06
NEG = -1e30
GELU_C = 0.7978845608028654
GELU_A = 0.044715
F32 = jnp.float32
BF16 = jnp.bfloat16
VMEM_BYTES = 62 * 1024 * 1024

NN = (((1,), (0,)), ((), ()))
NT = (((1,), (1,)), ((), ()))
TN = (((0,), (0,)), ((), ()))


def mm(a, b, dims=NN):
    return lax.dot_general(a, b, dims, preferred_element_type=F32)


def norm_parts(x):
    center = x - jnp.mean(x, axis=-1, keepdims=True)
    rstd = lax.rsqrt(jnp.mean(center * center, axis=-1, keepdims=True) + EPS)
    return center * rstd, rstd


def norm_back(grad, unit, rstd, scale):
    dn = grad * (1.0 + scale)
    return rstd * (
        dn
        - jnp.mean(dn, axis=-1, keepdims=True)
        - unit * jnp.mean(dn * unit, axis=-1, keepdims=True)
    )


def remote(src, dst, send, recv, **dev):
    return pltpu.make_async_remote_copy(
        src_ref=src, dst_ref=dst, send_sem=send, recv_sem=recv, device_id=dev, device_id_type=MESH
    )


def chunk_rows(count, devices):
    return 16 * -(-(count // 16) // devices)


class Dims:
    def __init__(self, mesh, tokens, query, up, mod):
        self.nc = mesh.shape["ctx"]
        self.nt = mesh.shape["tp"]
        self.seqs, self.rows, self.width = tokens
        self.block = self.rows * self.nt
        self.hw, self.half = query
        self.heads = self.hw // HEAD_DIM
        self.ff = up[1]
        self.mod = mod[1]
        self.kvw = 2 * self.hw
        self.vlo = self.kvw - WIN
        self.voff = self.hw - self.vlo
        self.wide = 2 * self.ff
        self.heads_rows = 4 * self.hw
        self.mcols = self.mod // self.nt


def scratch_table(z):
    vm = lambda shape, dtype=BF16: pltpu.VMEM(shape, dtype)
    sem = lambda *shape: pltpu.SemaphoreType.DMA(shape)
    full = (z.seqs, z.block, z.width)
    own = (z.seqs, z.rows, z.width)
    parts = (z.nt,) + own
    return dict(
        tok=vm(full),
        cot=vm(full),
        wqt=vm((WIN, z.width)),
        wkvt=vm((z.kvw, z.width)),
        wot=vm((WIN, z.width)),
        wu=vm((z.width, z.ff)),
        wd=vm((z.width, z.ff)),
        wm=vm((z.half, z.mod)),
        emb_s=vm((8, z.half), F32),
        emb_r=vm((8, z.half), F32),
        emb=vm((z.nc, 8, z.half), F32),
        mod_s=vm((8, z.mod), F32),
        mod_r=vm((8, z.mod), F32),
        mod=vm((8, z.mod), F32),
        cosine=vm((z.block, LANES), F32),
        sine=vm((z.block, LANES), F32),
        nrm=vm(full),
        q=vm((z.seqs, z.block, WIN)),
        kv=vm((z.nc, z.seqs, z.block, z.kvw)),
        vt=vm((WIN, z.block)),
        stat=vm((2, 8, z.block), F32),
        acc=vm((z.hw, z.block), F32),
        att=vm((z.seqs, z.hw, z.block), F32),
        attl=vm((z.seqs, z.block, WIN)),
        lse=vm((z.seqs, 8, z.block), F32),
        delta=vm((z.seqs, 8, z.block), F32),
        part=vm(full),
        br_r=vm(parts),
        branch=vm(own, F32),
        middle=vm(own, F32),
        n2=vm(full),
        act=vm((z.seqs, z.block, z.ff)),
        hgrad=vm((z.seqs, z.block, z.ff)),
        mgrad=vm(full),
        g2p=vm(full),
        g2_r=vm(parts),
        mlp=vm(full),
        ml_r=vm(parts),
        midg=vm(own, F32),
        bg=vm(full),
        do=vm((z.seqs, z.block, WIN)),
        dot=vm((WIN, z.block)),
        dqt=vm((z.hw, z.block), F32),
        dq=vm((z.seqs, z.block, WIN), F32),
        dkv=vm((z.seqs, z.block, z.kvw), F32),
        dkv_r=vm((z.nc, z.seqs, z.block, z.kvw)),
        qb=vm((z.seqs, z.block, WIN)),
        kvb=vm((z.seqs, z.block, z.kvw)),
        n1_r=vm(parts),
        ga_s=vm((z.half, z.wide)),
        ga_o=vm((z.half, z.wide)),
        ga_r=vm((z.half, z.wide)),
        ga_c=vm((z.nc, chunk_rows(z.half, z.nc), z.wide)),
        ga_t=vm((z.half, z.wide)),
        gb_s=vm((z.heads_rows, z.half)),
        gb_o=vm((z.heads_rows, z.half)),
        gb_r=vm((z.heads_rows, z.half)),
        gb_c=vm((z.nc, chunk_rows(z.heads_rows, z.nc), z.half)),
        gb_t=vm((z.heads_rows, z.half)),
        msum=vm((8, z.mod), F32),
        mt_r=vm((z.nt, 8, z.mcols), F32),
        md_s=vm((8, z.mcols), F32),
        md_r=vm((8, z.mcols), F32),
        mg=vm((z.nc, 8, z.mcols), F32),
        res=vm(own),
        gtok=vm(own, F32),
        s_loc=sem(16),
        s_w=sem(2, 6),
        s_e=sem(2),
        s_ec=sem(2, z.nc),
        s_m=sem(2, 2),
        s_tok=sem(2, z.nt),
        r_tok=sem(z.nt),
        s_cot=sem(2, z.nt),
        s_kv=sem(z.nc, z.nt),
        r_kv=sem(z.nc, z.nt),
        s_br=sem(z.seqs, z.nt),
        r_br=sem(z.seqs, z.nt),
        s_n2=sem(2, z.nt),
        r_n2=sem(z.nt),
        s_g2=sem(2, z.nt),
        s_ml=sem(2, z.nt),
        s_bg=sem(2, z.nt),
        r_bg=sem(z.nt),
        s_dk=sem(z.nc, z.seqs),
        r_dk=sem(z.nc, z.seqs),
        s_n1=sem(2, z.nt),
        s_ga=sem(2),
        s_gac=sem(2, z.nc),
        s_gag=sem(2, z.nc),
        s_gb=sem(2),
        s_gbc=sem(2, z.nc),
        s_gbg=sem(2, z.nc),
        s_mt=sem(2, z.nt),
        s_md=sem(2),
        s_mc=sem(2, z.nc),
    )


class Box:
    pass


def layer_kernel(z, names, *refs):
    r = Box()
    for name, ref in zip(names, refs):
        setattr(r, name, ref)
    d, c, t = lax.axis_index("dp"), lax.axis_index("ctx"), lax.axis_index("tp")
    other = 1 - d
    nt, nc, rows, block, width, hw = z.nt, z.nc, z.rows, z.block, z.width, z.hw
    seqs, half = z.seqs, z.half

    def each(count, body, first=0):
        def step(i, carry):
            body(i)
            return carry

        lax.fori_loop(first, count, step, 0)

    def span(idx):
        return pl.ds(pl.multiple_of(idx * rows, rows), rows)

    def slot(ref, idx):
        return ref.at[:, span(idx), :]

    def flat(x):
        return x.reshape(x.shape[0] * x.shape[1], x.shape[2])

    def lanes_of(shape, axis=1):
        return lax.broadcasted_iota(jnp.int32, shape, axis)

    local = []

    def fetch(src, dst):
        cp = pltpu.make_async_copy(src, dst, r.s_loc.at[len(local)])
        cp.start()
        local.append(cp)
        return cp

    my_half = pl.ds(pl.multiple_of(d * half, LANES), half)
    weights = [
        (r.wq_in, r.wqt.at[0:hw, my_half]),
        (r.wk_in, r.wkvt.at[0:hw, my_half]),
        (r.wv_in, r.wkvt.at[hw : z.kvw, my_half]),
        (r.wo_in, r.wot.at[z.voff : z.voff + hw, my_half]),
        (r.wu_in, r.wu.at[my_half, :]),
        (r.wd_in, r.wd.at[my_half, :]),
    ]
    first_cols = 2 * width
    cp_tok = fetch(r.tok_in, slot(r.tok, t))
    cp_wm1 = fetch(r.wm_in.at[:, 0:first_cols], r.wm.at[:, 0:first_cols])
    cp_w = [fetch(src, dst) for src, dst in weights]
    cp_wm2 = fetch(r.wm_in.at[:, first_cols : z.mod], r.wm.at[:, first_cols : z.mod])
    cp_cot = fetch(r.cot_in, slot(r.cot, t))

    r.wqt[hw:WIN, :] = jnp.zeros((WIN - hw, width), BF16)
    r.wot[0 : z.voff, :] = jnp.zeros((z.voff, width), BF16)

    bar = pltpu.get_barrier_semaphore()
    pl.semaphore_signal(bar, inc=1, device_id={"dp": other}, device_id_type=MESH)
    for k in range(1, nt):
        pl.semaphore_signal(bar, inc=1, device_id={"tp": (t + k) % nt}, device_id_type=MESH)

    def greet(k):
        pl.semaphore_signal(bar, inc=1, device_id={"ctx": (c + k) % nc}, device_id_type=MESH)

    each(nc, greet, 1)

    row8 = lanes_of((8, half), 0)
    step_of = jnp.where(
        row8 % 2 == 0, r.ts_in[0, 0].astype(F32), r.ts_in[1, 0].astype(F32)
    )
    angle = step_of * r.rate_in[...]
    sin_e, cos_e = jnp.sin(angle), jnp.cos(angle)

    def silu_low(v):
        return (v / (1.0 + jnp.exp(-v))).astype(BF16).astype(F32)

    sin_e, cos_e = silu_low(sin_e), silu_low(cos_e)
    first = d == 0
    own_half = jnp.where(row8 < 2, jnp.where(first, sin_e, cos_e), 0.0)
    r.emb_s[...] = jnp.where(
        (row8 >= 2) & (row8 < 4), jnp.where(first, cos_e, sin_e), 0.0
    )
    pl.semaphore_wait(bar, 1 + (nt - 1) + (nc - 1))

    def line_send(src, buf, send, recv, idx, side):
        to = t + 1 - 2 * side

        @pl.when((to >= 0) & (to < nt))
        def _():
            remote(src, slot(buf, idx), send.at[side, idx], recv.at[idx], tp=to).start()

    def line_open(src, buf, send, recv):
        line_send(src, buf, send, recv, t, 0)
        line_send(src, buf, send, recv, t, 1)

    def line_rest(buf, send, recv, work):
        def far(dist):
            def take(side):
                idx = t + (2 * side - 1) * dist

                @pl.when((idx >= 0) & (idx < nt))
                def _():
                    here = slot(buf, idx)
                    remote(here, here, send.at[side, idx], recv.at[idx], tp=idx).wait_recv()
                    line_send(here, buf, send, recv, idx, side)

            def run(side):
                idx = t + (2 * side - 1) * dist

                @pl.when((idx >= 0) & (idx < nt))
                def _():
                    work(idx)

            each(2, take)
            each(2, run)

        each(nt, far, 1)

    def line_close(buf, send, recv):
        def one(j):
            idx, side = j // 2, j % 2
            to = t + 1 - 2 * side
            passed = ((1 - 2 * side) * (t - idx) >= 0) & (to >= 0) & (to < nt)

            @pl.when(passed)
            def _():
                here = slot(buf, idx)
                remote(here, here, send.at[side, idx], recv.at[idx], tp=to).wait_send()

        each(2 * nt, one)

    def push(src_of, buf, sems, idx):
        remote(src_of(idx), buf.at[t], sems.at[0, idx], sems.at[1, t], tp=idx).start()

    def pull(buf, sems, idx):
        remote(buf.at[idx], buf.at[idx], sems.at[0, idx], sems.at[1, idx], tp=idx).wait_recv()

    def push_done(src_of, buf, sems):
        for k in range(1, nt):
            idx = (t + k) % nt
            remote(src_of(idx), buf.at[t], sems.at[0, idx], sems.at[1, t], tp=idx).wait_send()

    def summed(part, buf):
        total = part[:, span(t), :].astype(F32)
        for k in range(1, nt):
            total = total + buf[(t + k) % nt].astype(F32)
        return total

    line_open(r.tok_in, r.tok, r.s_tok, r.r_tok)
    send_emb = remote(r.emb_s, r.emb_r, r.s_e.at[0], r.s_e.at[1], dp=other)
    send_emb.start()
    send_w = [
        remote(src, dst, r.s_w.at[0, i], r.s_w.at[1, i], dp=other)
        for i, (src, dst) in enumerate(weights)
    ]
    for cp in send_w[:3]:
        cp.start()

    send_emb.wait()
    emb4 = own_half + r.emb_r[...]
    r.emb[pl.ds(c, 1)] = emb4[None]
    emb_low = emb4.astype(BF16)

    def mod_part(lo, hi, which, ready):
        ready.wait()
        r.mod_s[:, lo:hi] = mm(emb_low, r.wm[:, lo:hi])
        cp = remote(
            r.mod_s.at[:, lo:hi], r.mod_r.at[:, lo:hi], r.s_m.at[0, which], r.s_m.at[1, which], dp=other
        )
        cp.start()
        return cp

    def mod_take(lo, hi, cp):
        cp.wait()
        for s in range(seqs):
            r.mod[s : s + 1, lo:hi] = r.mod_s[s : s + 1, lo:hi] + r.mod_r[s + 2 : s + 3, lo:hi]

    def vec(slot_idx):
        lo = slot_idx * width
        return r.mod[0:seqs, lo : lo + width][:, None, :]

    mod1 = mod_part(0, first_cols, 0, cp_wm1)
    for cp in send_w[3:]:
        cp.start()

    def send_ctx_emb(k):
        to = (c + k) % nc
        remote(r.emb.at[c], r.emb.at[c], r.s_ec.at[0, to], r.s_ec.at[1, c], ctx=to).start()

    each(nc, send_ctx_emb, 1)

    place = (c * block + lanes_of((block, LANES), 0)).astype(F32)
    turn = place * r.rope_in[...]
    low_lane = lanes_of((block, LANES)) % HEAD_DIM < HEAD_DIM // 2
    r.cosine[...] = jnp.cos(turn)
    r.sine[...] = jnp.where(low_lane, -jnp.sin(turn), jnp.sin(turn))

    def swap(x):
        low = lanes_of(x.shape) % HEAD_DIM < HEAD_DIM // 2
        return jnp.where(
            low,
            pltpu.roll(x, LANES - HEAD_DIM // 2, 1),
            pltpu.roll(x, HEAD_DIM // 2, 1),
        )

    for i in range(3):
        cp_w[i].wait()
        send_w[i].wait_recv()
    mod_take(0, first_cols, mod1)

    def make_qkv(idx):
        at = span(idx)
        unit, _ = norm_parts(r.tok[:, at, :].astype(F32))
        low = (unit * (1.0 + vec(1)) + vec(0)).astype(BF16)
        r.nrm[:, at, :] = low
        low = flat(low)
        cos1, sin1 = r.cosine[at, :], r.sine[at, :]
        cos2 = jnp.concatenate([cos1] * seqs, axis=0)
        sin2 = jnp.concatenate([sin1] * seqs, axis=0)
        q_pre = mm(low, r.wqt[...], NT)
        kv_pre = mm(low, r.wkvt[...], NT)
        shape = (seqs, rows, LANES)
        for j in range(WIN // LANES):
            x = q_pre[:, j * LANES : (j + 1) * LANES]
            x = (x * cos2 + swap(x) * sin2) * (HEAD_DIM ** -0.5)
            r.q[:, at, j * LANES : (j + 1) * LANES] = x.astype(BF16).reshape(shape)
        for j in range(z.kvw // LANES):
            x = kv_pre[:, j * LANES : (j + 1) * LANES]
            keys = min(max(hw - j * LANES, 0), LANES)
            if keys > 0:
                turned = x * cos2 + swap(x) * sin2
                x = turned if keys == LANES else jnp.where(lanes_of(x.shape) < keys, turned, x)
            r.kv[c, :, at, j * LANES : (j + 1) * LANES] = x.astype(BF16).reshape(shape)

        def send_kv(to):
            mine = r.kv.at[c, :, at, :]
            remote(mine, mine, r.s_kv.at[to, idx], r.r_kv.at[c, idx], ctx=to).start()

        each(nc, send_kv, c + 1)

    cp_tok.wait()
    make_qkv(t)
    mod2 = mod_part(first_cols, z.mod, 1, cp_wm2)
    line_rest(r.tok, r.s_tok, r.r_tok, make_qkv)

    cp_cot.wait()
    for k in range(1, nt):
        to = (t + k) % nt
        remote(r.cot_in, slot(r.cot, t), r.s_cot.at[0, to], r.s_cot.at[1, t], tp=to).start()
    mod_take(first_cols, z.mod, mod2)
    for i in range(3, 6):
        cp_w[i].wait()
        send_w[i].wait_recv()

    eye = (lanes_of((WIN, WIN), 0) == lanes_of((WIN, WIN))).astype(BF16)

    def head_of(x, h, off=0):
        lane = lanes_of(x.shape)
        lo = off + h * HEAD_DIM
        return jnp.where((lane >= lo) & (lane < lo + HEAD_DIM), x, jnp.zeros_like(x))

    def attend_seq(s):
        r.stat[0] = jnp.full((8, block), NEG, F32)
        r.stat[1] = jnp.zeros((8, block), F32)
        r.acc[...] = jnp.zeros((hw, block), F32)
        q = r.q[s]

        def one_block(back):
            j = c - back

            @pl.when((back > 0) & (s == 0))
            def _():
                def take(idx):
                    there = r.kv.at[j, :, span(idx), :]
                    remote(there, there, r.s_kv.at[j, idx], r.r_kv.at[j, idx], ctx=j).wait_recv()

                each(nt, take)

            keys = r.kv[j, s, :, 0:WIN]
            r.vt[...] = mm(eye, r.kv[j, s, :, z.vlo : z.vlo + WIN], NT).astype(BF16)
            for h in range(z.heads):
                scores = mm(keys, head_of(q, h), NT)
                old = r.stat[0, h : h + 1, :]
                top = jnp.maximum(old, jnp.max(scores, axis=0, keepdims=True))
                prob = jnp.exp(scores - top)
                fade = jnp.exp(old - top)
                r.stat[0, h : h + 1, :] = top
                r.stat[1, h : h + 1, :] = r.stat[1, h : h + 1, :] * fade + jnp.sum(
                    prob, axis=0, keepdims=True
                )
                lo = h * HEAD_DIM
                vt = r.vt[z.voff + lo : z.voff + lo + HEAD_DIM, :]
                r.acc[lo : lo + HEAD_DIM, :] = r.acc[lo : lo + HEAD_DIM, :] * fade + mm(
                    vt, prob.astype(BF16)
                )

        each(c + 1, one_block)
        for h in range(z.heads):
            lo = h * HEAD_DIM
            denom = r.stat[1, h : h + 1, :]
            r.lse[s, h : h + 1, :] = r.stat[0, h : h + 1, :] + jnp.log(denom)
            r.att[s, lo : lo + HEAD_DIM, :] = r.acc[lo : lo + HEAD_DIM, :] / denom
        low = jnp.transpose(r.att[s]).astype(BF16)
        r.attl[s, :, 0:hw] = low
        r.attl[s, :, hw:WIN] = jnp.zeros((block, WIN - hw), BF16)
        r.part[s] = mm(low, r.wot[z.voff : z.voff + hw, :]).astype(BF16)
        for k in range(1, nt):
            to = (t + k) % nt
            remote(
                r.part.at[s, span(to), :], r.br_r.at[t, s], r.s_br.at[s, to], r.r_br.at[s, t], tp=to
            ).start()

    each(seqs, attend_seq)

    for s in range(seqs):
        for k in range(1, nt):
            fr = (t + k) % nt
            remote(
                r.br_r.at[fr, s], r.br_r.at[fr, s], r.s_br.at[s, fr], r.r_br.at[s, fr], tp=fr
            ).wait_recv()
    branch = summed(r.part, r.br_r)
    r.branch[...] = branch
    middle = r.tok[:, span(t), :].astype(F32) + vec(2) * branch
    r.middle[...] = middle
    unit, _ = norm_parts(middle)
    r.n2[:, span(t), :] = (unit * (1.0 + vec(4)) + vec(3)).astype(BF16)
    line_open(slot(r.n2, t), r.n2, r.s_n2, r.r_n2)

    for k in range(1, nt):
        fr = (t + k) % nt
        there = slot(r.cot, fr)
        remote(there, there, r.s_cot.at[0, fr], r.s_cot.at[1, fr], tp=fr).wait_recv()

    def feed(idx):
        at = span(idx)
        hid = mm(flat(r.n2[:, at, :]), r.wu[...])
        square = hid * hid
        tanh = jnp.tanh(GELU_C * (hid + GELU_A * (hid * square)))
        r.act[:, at, :] = (0.5 * hid * (1.0 + tanh)).astype(BF16).reshape(seqs, rows, z.ff)
        slope = 0.5 * (1.0 + tanh) + 0.5 * hid * (1.0 - tanh * tanh) * (
            GELU_C * (1.0 + 3.0 * GELU_A * square)
        )
        low = (vec(5) * r.cot[:, at, :].astype(F32)).astype(BF16)
        r.mgrad[:, at, :] = low
        hgrad = (slope * mm(flat(low), r.wd[...])).astype(BF16)
        r.hgrad[:, at, :] = hgrad.reshape(seqs, rows, z.ff)
        r.g2p[:, at, :] = mm(hgrad, r.wu[...], NT).astype(BF16).reshape(seqs, rows, width)

    def feed_push(idx):
        feed(idx)
        push(lambda i: slot(r.g2p, i), r.g2_r, r.s_g2, idx)

    feed(t)
    line_rest(r.n2, r.s_n2, r.r_n2, feed_push)

    def mlp_rows(idx):
        at = span(idx)
        r.mlp[:, at, :] = (
            mm(flat(r.act[:, at, :]), r.wd[...], NT).astype(BF16).reshape(seqs, rows, width)
        )

    def mlp_push(k):
        idx = (t + k) % nt
        mlp_rows(idx)
        push(lambda i: slot(r.mlp, i), r.ml_r, r.s_ml, idx)

    each(nt, mlp_push, 1)
    mlp_rows(t)

    r.msum[...] = jnp.zeros((8, z.mod), F32)

    def keep_sum(slot_idx, value):
        lo = slot_idx * width
        r.msum[0:seqs, lo : lo + width] = jnp.sum(value, axis=1)

    for k in range(1, nt):
        pull(r.g2_r, r.s_g2, (t + k) % nt)
    grad2 = summed(r.g2p, r.g2_r)
    unit, rstd = norm_parts(r.middle[...])
    keep_sum(3, grad2)
    keep_sum(4, grad2 * unit)
    mid_grad = r.cot[:, span(t), :].astype(F32) + norm_back(grad2, unit, rstd, vec(4))
    r.midg[...] = mid_grad
    keep_sum(2, mid_grad * r.branch[...])
    r.bg[:, span(t), :] = (vec(2) * mid_grad).astype(BF16)
    line_open(slot(r.bg, t), r.bg, r.s_bg, r.r_bg)

    def pair_grads(lhs, rhs, mine, sent, lo, hi):
        right = flat(rhs[...])
        for which, dst in ((other, sent), (d, mine)):
            cols = pl.ds(pl.multiple_of(which * half, half), half)
            left = flat(lhs[:, :, cols])
            dst[:, lo:hi] = mm(left, right, TN).astype(BF16)

    pair_grads(r.mgrad, r.act, r.ga_o, r.ga_s, z.ff, 2 * z.ff)
    pair_grads(r.n2, r.hgrad, r.ga_o, r.ga_s, 0, z.ff)
    send_ga = remote(r.ga_s, r.ga_r, r.s_ga.at[0], r.s_ga.at[1], dp=other)
    send_ga.start()

    def out_grads(idx):
        at = span(idx)
        r.do[:, at, :] = (
            mm(flat(r.bg[:, at, :]), r.wot[...], NT).astype(BF16).reshape(seqs, rows, WIN)
        )

    out_grads(t)
    line_rest(r.bg, r.s_bg, r.r_bg, out_grads)

    class Reduction:
        def __init__(self, got, mine, theirs, buf, total, sems, sems_all):
            self.got, self.mine, self.theirs, self.buf, self.total = got, mine, theirs, buf, total
            self.sems, self.sems_all = sems, sems_all
            self.chunk = buf.shape[1]
            self.owners = mine.shape[0] // self.chunk

        def rows(self, o):
            return pl.ds(pl.multiple_of(o * self.chunk, 16), self.chunk)

        def part(self, o):
            return remote(
                self.mine.at[self.rows(o), :],
                self.buf.at[c],
                self.sems.at[0, o],
                self.sems.at[1, c],
                ctx=o,
            )

        def share(self, owner, to):
            here = self.total.at[self.rows(owner), :]
            return remote(here, here, self.sems_all.at[0, to], self.sems_all.at[1, owner], ctx=to)

        def to_owners(self, body):
            def one(k):
                o = (c + k) % nc

                @pl.when(o < self.owners)
                def _():
                    body(o)

            each(nc, one, 1)

        def as_owner(self, body):
            @pl.when(c < self.owners)
            def _():
                body()

        def send(self):
            self.got.wait()
            self.mine[...] = (self.mine[...].astype(F32) + self.theirs[...].astype(F32)).astype(
                BF16
            )
            self.to_owners(lambda o: self.part(o).start())

        def sum(self):
            def body():
                def add(k, acc):
                    fr = (c + k) % nc
                    there = self.buf.at[fr]
                    remote(
                        there, there, self.sems.at[0, fr], self.sems.at[1, fr], ctx=fr
                    ).wait_recv()
                    return acc + self.buf[fr].astype(F32)

                acc = self.mine[self.rows(c), :].astype(F32)
                if nc <= 4:
                    for k in range(1, nc):
                        acc = add(k, acc)
                else:
                    acc = lax.fori_loop(1, nc, add, acc)
                self.total[self.rows(c), :] = acc.astype(BF16)
                each(nc, lambda k: self.share(c, (c + k) % nc).start(), 1)

            self.as_owner(body)

        def take(self):
            def one(o):
                self.share(o, o).wait_recv()
                self.part(o).wait_send()

            self.to_owners(one)
            self.as_owner(
                lambda: each(nc, lambda k: self.share(c, (c + k) % nc).wait_send(), 1)
            )

    red_a = Reduction(send_ga, r.ga_o, r.ga_r, r.ga_c, r.ga_t, r.s_gac, r.s_gag)
    red_a.send()

    def back_seq(s):
        do = r.do[s]
        r.dot[...] = mm(eye, do, NT).astype(BF16)
        for h in range(z.heads):
            lo = h * HEAD_DIM
            r.delta[s, h : h + 1, :] = jnp.sum(
                r.dot[z.voff + lo : z.voff + lo + HEAD_DIM, :].astype(F32)
                * r.att[s, lo : lo + HEAD_DIM, :],
                axis=0,
                keepdims=True,
            )
        r.dqt[...] = jnp.zeros((hw, block), F32)
        q = r.q[s]

        def one_block(j):
            keys = r.kv[j, s, :, 0:WIN]
            vals = r.kv[j, s, :, z.vlo : z.vlo + WIN]
            r.vt[...] = mm(eye, keys, NT).astype(BF16)
            dk = jnp.zeros((block, WIN), F32)
            dv = jnp.zeros((block, WIN), F32)
            for h in range(z.heads):
                lo = h * HEAD_DIM
                qh = head_of(q, h)
                doh = head_of(do, h, z.voff)
                prob = jnp.exp(mm(keys, qh, NT) - r.lse[s, h : h + 1, :])
                dprob = mm(vals, doh, NT)
                dsc = (prob * (dprob - r.delta[s, h : h + 1, :])).astype(BF16)
                dv = dv + mm(prob.astype(BF16), doh)
                dk = dk + mm(dsc, qh)
                r.dqt[lo : lo + HEAD_DIM, :] += mm(r.vt[lo : lo + HEAD_DIM, :], dsc)
            over = WIN - z.vlo
            pieces = (
                (0, z.vlo, dk[:, 0 : z.vlo]),
                (z.vlo, WIN, dk[:, z.vlo : WIN] + dv[:, 0:over]),
                (WIN, z.kvw, dv[:, over:WIN]),
            )

            @pl.when(j < c)
            def _():
                for lo, hi, piece in pieces:
                    r.kv[j, s, :, lo:hi] = piece.astype(BF16)
                remote(
                    r.kv.at[j, s], r.dkv_r.at[c, s], r.s_dk.at[j, s], r.r_dk.at[c, s], ctx=j
                ).start()

            @pl.when(j == c)
            def _():
                for lo, hi, piece in pieces:
                    r.dkv[s, :, lo:hi] = piece

        each(c + 1, one_block)
        r.dq[s, :, 0:hw] = jnp.transpose(r.dqt[...]) * (HEAD_DIM ** -0.5)
        r.dq[s, :, hw:WIN] = jnp.zeros((block, WIN - hw), F32)

    def kv_sent(j):
        def one(idx):
            mine = r.kv.at[c, :, span(idx), :]
            remote(mine, mine, r.s_kv.at[j, idx], r.r_kv.at[c, idx], ctx=j).wait_send()

        each(nt, one)

    each(nc, kv_sent, c + 1)
    each(seqs, back_seq)

    def add_dkv(j):
        for s in range(seqs):
            there = r.dkv_r.at[j, s]
            remote(there, there, r.s_dk.at[j, s], r.r_dk.at[j, s], ctx=j).wait_recv()
        r.dkv[...] += r.dkv_r[j].astype(F32)

    each(nc, add_dkv, c + 1)

    cos1, sin1 = r.cosine[...], r.sine[...]
    for s in range(seqs):
        for j in range(WIN // LANES):
            x = r.dq[s, :, j * LANES : (j + 1) * LANES]
            r.qb[s, :, j * LANES : (j + 1) * LANES] = (x * cos1 - swap(x) * sin1).astype(BF16)
        for j in range(z.kvw // LANES):
            x = r.dkv[s, :, j * LANES : (j + 1) * LANES]
            keys = min(max(hw - j * LANES, 0), LANES)
            if keys > 0:
                turned = x * cos1 - swap(x) * sin1
                x = turned if keys == LANES else jnp.where(lanes_of(x.shape) < keys, turned, x)
            r.kvb[s, :, j * LANES : (j + 1) * LANES] = x.astype(BF16)

    def n1_rows(idx):
        at = span(idx)
        r.g2p[:, at, :] = (
            (
                mm(flat(r.qb[:, at, :]), r.wqt[...])
                + mm(flat(r.kvb[:, at, :]), r.wkvt[...])
            )
            .astype(BF16)
            .reshape(seqs, rows, width)
        )

    def n1_push(k):
        idx = (t + k) % nt
        n1_rows(idx)
        push(lambda i: slot(r.g2p, i), r.n1_r, r.s_n1, idx)

    push_done(lambda i: slot(r.g2p, i), r.g2_r, r.s_g2)
    each(nt, n1_push, 1)
    n1_rows(t)

    for which, dst in ((other, r.gb_s), (d, r.gb_o)):
        cols = pl.ds(pl.multiple_of(which * half, LANES), half)
        right = flat(r.nrm[:, :, cols])
        dst[0:hw, :] = mm(flat(r.qb[:, :, 0:hw]), right, TN).astype(BF16)
        dst[hw : 3 * hw, :] = mm(flat(r.kvb[...]), right, TN).astype(BF16)
        right = flat(r.bg[:, :, cols])
        dst[3 * hw : 4 * hw, :] = mm(flat(r.attl[:, :, 0:hw]), right, TN).astype(BF16)
    send_gb = remote(r.gb_s, r.gb_r, r.s_gb.at[0], r.s_gb.at[1], dp=other)
    send_gb.start()
    red_a.sum()

    for k in range(1, nt):
        pull(r.ml_r, r.s_ml, (t + k) % nt)
    mlp = summed(r.mlp, r.ml_r)
    r.res[...] = (r.middle[...] + vec(5) * mlp).astype(BF16)
    keep_sum(5, r.cot[:, span(t), :].astype(F32) * mlp)
    outs = []

    def store(src, dst):
        cp = pltpu.make_async_copy(src, dst, r.s_loc.at[len(local) + len(outs)])
        cp.start()
        outs.append(cp)

    store(r.res, r.res_out)
    red_b = Reduction(send_gb, r.gb_o, r.gb_r, r.gb_c, r.gb_t, r.s_gbc, r.s_gbg)
    red_b.send()

    for k in range(1, nt):
        pull(r.n1_r, r.s_n1, (t + k) % nt)
    grad1 = summed(r.g2p, r.n1_r)
    unit, rstd = norm_parts(r.tok[:, span(t), :].astype(F32))
    keep_sum(0, grad1)
    keep_sum(1, grad1 * unit)

    def mcol(idx):
        return pl.ds(pl.multiple_of(idx * z.mcols, LANES), z.mcols)

    for k in range(1, nt):
        to = (t + k) % nt
        remote(
            r.msum.at[:, mcol(to)], r.mt_r.at[t], r.s_mt.at[0, to], r.s_mt.at[1, t], tp=to
        ).start()
    r.gtok[...] = r.midg[...] + norm_back(grad1, unit, rstd, vec(1))
    store(r.gtok, r.gtok_out)
    red_b.sum()
    total = r.msum[:, mcol(t)]
    for k in range(1, nt):
        fr = (t + k) % nt
        pull(r.mt_r, r.s_mt, fr)
        total = total + r.mt_r[fr]
    r.md_s[...] = total
    send_md = remote(r.md_s, r.md_r, r.s_md.at[0], r.s_md.at[1], dp=other)
    send_md.start()
    send_md.wait()
    r.mg[pl.ds(c, 1), 0:2, :] = total[None, 0:2, :]
    r.mg[pl.ds(c, 1), 2:4, :] = r.md_r[0:2, :][None]
    r.mg[pl.ds(c, 1), 4:8, :] = jnp.zeros((1, 4, z.mcols), F32)

    def send_mg(k):
        to = (c + k) % nc
        remote(r.mg.at[c], r.mg.at[c], r.s_mc.at[0, to], r.s_mc.at[1, c], ctx=to).start()

    each(nc, send_mg, 1)
    red_a.take()
    store(r.ga_t, r.ga_out)
    red_b.take()
    store(r.gb_t, r.gb_out)

    def take_small(k):
        fr = (c + k) % nc
        for buf, sems in ((r.mg, r.s_mc), (r.emb, r.s_ec)):
            remote(buf.at[fr], buf.at[fr], sems.at[0, fr], sems.at[1, fr], ctx=fr).wait_recv()
            remote(buf.at[c], buf.at[c], sems.at[0, fr], sems.at[1, c], ctx=fr).wait_send()

    each(nc, take_small, 1)
    store(r.mg, r.mg_out)
    store(r.emb, r.emb_out)

    for cp in send_w:
        cp.wait_send()
    line_close(r.tok, r.s_tok, r.r_tok)
    line_close(r.n2, r.s_n2, r.r_n2)
    line_close(r.bg, r.s_bg, r.r_bg)
    for k in range(1, nt):
        to = (t + k) % nt
        remote(r.cot_in, slot(r.cot, t), r.s_cot.at[0, to], r.s_cot.at[1, t], tp=to).wait_send()
        for s in range(seqs):
            remote(
                r.part.at[s, span(to), :], r.br_r.at[t, s], r.s_br.at[s, to], r.r_br.at[s, t], tp=to
            ).wait_send()
        remote(
            r.msum.at[:, mcol(to)], r.mt_r.at[t], r.s_mt.at[0, to], r.s_mt.at[1, t], tp=to
        ).wait_send()
    push_done(lambda i: slot(r.mlp, i), r.ml_r, r.s_ml)
    push_done(lambda i: slot(r.g2p, i), r.n1_r, r.s_n1)

    def dkv_sent(j):
        for s in range(seqs):
            remote(
                r.kv.at[j, s], r.dkv_r.at[c, s], r.s_dk.at[j, s], r.r_dk.at[c, s], ctx=j
            ).wait_send()

    each(c, dkv_sent)
    for cp in outs:
        cp.wait()


def finish_kernel(z, ga, gb, emb, mg, res, gtok, *outs):
    res_o, gtok_o, gq, gk, gv, go, gu, gd, gm = outs
    hw = z.hw
    res_o[...] = res[...]
    gtok_o[...] = gtok[...]
    for i, out in enumerate((gq, gk, gv, go)):
        out[...] = gb[i * hw : (i + 1) * hw, :].astype(F32)
    gu[...] = ga[:, 0 : z.ff].astype(F32)
    gd[...] = ga[:, z.ff : 2 * z.ff].astype(F32)
    e = emb[...].reshape(z.nc * 8, z.half)
    m = mg[...].reshape(z.nc * 8, z.mcols)
    gm[...] = lax.dot_general(e, m, TN, precision=lax.Precision.HIGHEST, preferred_element_type=F32)


IN_NAMES = (
    "tok_in",
    "ts_in",
    "wq_in",
    "wk_in",
    "wv_in",
    "wo_in",
    "wu_in",
    "wd_in",
    "wm_in",
    "cot_in",
    "rate_in",
    "rope_in",
)
OUT_NAMES = ("res_out", "gtok_out", "ga_out", "gb_out", "emb_out", "mg_out")


def solution(mesh):
    def shards(tokens, steps, wq, wk, wv, wo, wu, wd, wm, cot):
        wq, wk, wv, wo = wq.T, wk.T, wv.T, wo.T
        z = Dims(mesh, tokens.shape, wq.shape, wu.shape, wm.shape)
        half_dim = z.width // 2
        rate = jnp.exp(jnp.arange(half_dim, dtype=F32) * (-math.log(10000.0) / half_dim))
        rope = jnp.exp(
            jnp.arange(HEAD_DIM // 2, dtype=F32) * (-2.0 * math.log(10000.0) / HEAD_DIM)
        )
        rope = jnp.tile(rope, LANES // (HEAD_DIM // 2))
        table = scratch_table(z)
        names = list(IN_NAMES) + list(OUT_NAMES) + list(table)
        hbm = pl.BlockSpec(memory_space=pl.ANY)
        vmem = pl.BlockSpec(memory_space=pltpu.VMEM)
        smem = pl.BlockSpec(memory_space=pltpu.SMEM)
        own = (z.seqs, z.rows, z.width)
        shape = jax.ShapeDtypeStruct
        outs = pl.pallas_call(
            functools.partial(layer_kernel, z, names),
            out_shape=(
                shape(own, BF16),
                shape(own, F32),
                shape((z.half, z.wide), BF16),
                shape((z.heads_rows, z.half), BF16),
                shape((z.nc, 8, z.half), F32),
                shape((z.nc, 8, z.mcols), F32),
            ),
            in_specs=[hbm, smem] + [hbm] * 8 + [vmem, vmem],
            out_specs=[hbm] * 6,
            scratch_shapes=list(table.values()),
            compiler_params=pltpu.CompilerParams(
                collective_id=0, has_side_effects=True, vmem_limit_bytes=VMEM_BYTES
            ),
            name="layer",
        )(tokens, steps, wq, wk, wv, wo, wu, wd, wm, cot, rate[None], rope[None])
        res, gtok, ga, gb, emb, mg = outs
        done = pl.pallas_call(
            functools.partial(finish_kernel, z),
            out_shape=(
                shape(own, BF16),
                shape(own, F32),
                shape((z.hw, z.half), F32),
                shape((z.hw, z.half), F32),
                shape((z.hw, z.half), F32),
                shape((z.hw, z.half), F32),
                shape((z.half, z.ff), F32),
                shape((z.half, z.ff), F32),
                shape((z.half, z.mcols), F32),
            ),
            in_specs=[vmem] * 6,
            out_specs=[vmem] * 9,
            compiler_params=pltpu.CompilerParams(vmem_limit_bytes=VMEM_BYTES),
            name="finish",
        )(ga, gb, emb, mg, res, gtok)
        return done[:2] + tuple(g.T for g in done[2:6]) + done[6:]

    rows = P("dp", ("ctx", "tp"), None)
    cols = P("dp", "tp")
    return jax.shard_map(
        shards,
        mesh=mesh,
        in_specs=(rows, P("dp", "ctx")) + (cols,) * 6 + (P("dp", None), rows),
        out_specs=(rows, rows) + (cols,) * 7,
        check_vma=False,
    )
```

```python
import functools
import math

import jax
import jax.numpy as jnp
from jax import lax
from jax.experimental import pallas as pl
from jax.experimental.pallas import tpu as pltpu
from jax.sharding import PartitionSpec as P

MESH = pl.DeviceIdType.MESH
HEAD_DIM = 64
WIN = 256
LANES = 128
EPS = 1e-06
NEG = -1e30
GELU_C = 0.7978845608028654
GELU_A = 0.044715
F32 = jnp.float32
BF16 = jnp.bfloat16
VMEM_BYTES = 62 * 1024 * 1024

NN = (((1,), (0,)), ((), ()))
NT = (((1,), (1,)), ((), ()))
TN = (((0,), (0,)), ((), ()))


def mm(a, b, dims=NN):
    return lax.dot_general(a, b, dims, preferred_element_type=F32)


def norm_parts(x):
    center = x - jnp.mean(x, axis=-1, keepdims=True)
    rstd = lax.rsqrt(jnp.mean(center * center, axis=-1, keepdims=True) + EPS)
    return center * rstd, rstd


def norm_back(grad, unit, rstd, scale):
    dn = grad * (1.0 + scale)
    return rstd * (
        dn
        - jnp.mean(dn, axis=-1, keepdims=True)
        - unit * jnp.mean(dn * unit, axis=-1, keepdims=True)
    )


def remote(src, dst, send, recv, **dev):
    return pltpu.make_async_remote_copy(
        src_ref=src, dst_ref=dst, send_sem=send, recv_sem=recv, device_id=dev, device_id_type=MESH
    )


def chunk_rows(count, devices):
    return 16 * -(-(count // 16) // devices)


class Dims:
    def __init__(self, mesh, tokens, query, up, mod):
        self.nc = mesh.shape["ctx"]
        self.nt = mesh.shape["tp"]
        self.seqs, self.rows, self.width = tokens
        self.block = self.rows * self.nt
        self.hw, self.half = query
        self.heads = self.hw // HEAD_DIM
        self.ff = up[1]
        self.mod = mod[1]
        self.kvw = 2 * self.hw
        self.vlo = self.kvw - WIN
        self.voff = self.hw - self.vlo
        self.wide = 2 * self.ff
        self.heads_rows = 4 * self.hw
        self.mcols = self.mod // self.nt


def scratch_table(z):
    vm = lambda shape, dtype=BF16: pltpu.VMEM(shape, dtype)
    sem = lambda *shape: pltpu.SemaphoreType.DMA(shape)
    full = (z.seqs, z.block, z.width)
    own = (z.seqs, z.rows, z.width)
    pair = (z.seqs, 2, z.rows, z.width)
    return dict(
        tok=vm(full),
        cot=vm(full),
        wqt=vm((WIN, z.width)),
        wkvt=vm((z.kvw, z.width)),
        wot=vm((WIN, z.width)),
        wu=vm((z.width, z.ff)),
        wd=vm((z.width, z.ff)),
        wm=vm((z.half, z.mod)),
        emb_s=vm((8, z.half), F32),
        emb_r=vm((8, z.half), F32),
        emb=vm((z.nc, 8, z.half), F32),
        mod_s=vm((8, z.mod), F32),
        mod_r=vm((8, z.mod), F32),
        mod=vm((8, z.mod), F32),
        cosine=vm((z.block, LANES), F32),
        sine=vm((z.block, LANES), F32),
        nrm=vm(full),
        q=vm((z.seqs, z.block, WIN)),
        kv=vm((z.nc, z.seqs, z.block, z.kvw)),
        vt=vm((WIN, z.block)),
        stat=vm((2, 8, z.block), F32),
        acc=vm((z.hw, z.block), F32),
        att=vm((z.seqs, z.hw, z.block), F32),
        attl=vm((z.seqs, z.block, WIN)),
        lse=vm((z.seqs, 8, z.block), F32),
        delta=vm((z.seqs, 8, z.block), F32),
        br=vm(full),
        br_m=vm(pair),
        br_r=vm(pair),
        branch=vm(own, F32),
        middle=vm(own, F32),
        n2=vm(full),
        act=vm((z.seqs, z.block, z.ff)),
        hgrad=vm((z.seqs, z.block, z.ff)),
        mgrad=vm(full),
        g2=vm(full),
        g2_m=vm(pair),
        g2_r=vm(pair),
        ml=vm(full),
        ml_m=vm(pair),
        ml_r=vm(pair),
        midg=vm(own, F32),
        bg=vm(full),
        do=vm((z.seqs, z.block, WIN)),
        dot=vm((WIN, z.block)),
        dqt=vm((z.hw, z.block), F32),
        dq=vm((z.seqs, z.block, WIN), F32),
        dkv=vm((z.seqs, z.block, z.kvw), F32),
        dkv_r=vm((z.nc, z.seqs, z.block, z.kvw)),
        qb=vm((z.seqs, z.block, WIN)),
        kvb=vm((z.seqs, z.block, z.kvw)),
        n1_m=vm(pair),
        n1_r=vm(pair),
        ga_s=vm((z.half, z.wide)),
        ga_o=vm((z.half, z.wide)),
        ga_r=vm((z.half, z.wide)),
        ga_c=vm((z.nc, chunk_rows(z.half, z.nc), z.wide)),
        ga_t=vm((z.half, z.wide)),
        gb_s=vm((z.heads_rows, z.half)),
        gb_o=vm((z.heads_rows, z.half)),
        gb_r=vm((z.heads_rows, z.half)),
        gb_c=vm((z.nc, chunk_rows(z.heads_rows, z.nc), z.half)),
        gb_t=vm((z.heads_rows, z.half)),
        msum=vm((8, z.mod), F32),
        mt_r=vm((z.nt, 8, z.mcols), F32),
        md_s=vm((8, z.mcols), F32),
        md_r=vm((8, z.mcols), F32),
        mg=vm((z.nc, 8, z.mcols), F32),
        res=vm(own),
        gtok=vm(own, F32),
        s_loc=sem(16),
        s_w=sem(2, 6),
        s_e=sem(2),
        s_ec=sem(2, z.nc),
        s_m=sem(2, 2),
        s_tok=sem(z.seqs, 4),
        r_tok=sem(z.seqs, z.nt),
        s_cot=sem(z.seqs, 4),
        r_cot=sem(z.seqs, z.nt),
        s_kv=sem(z.nc, z.seqs, z.nt),
        r_kv=sem(z.nc, z.seqs, z.nt),
        s_br=sem(z.seqs, 4),
        m_br=sem(z.seqs, 2),
        r_br=sem(z.seqs, 2),
        s_n2=sem(z.seqs, 4),
        r_n2=sem(z.seqs, z.nt),
        s_g2=sem(z.seqs, 4),
        m_g2=sem(z.seqs, 2),
        r_g2=sem(z.seqs, 2),
        s_ml=sem(z.seqs, 4),
        m_ml=sem(z.seqs, 2),
        r_ml=sem(z.seqs, 2),
        s_bg=sem(z.seqs, 4),
        r_bg=sem(z.seqs, z.nt),
        s_dk=sem(z.nc, z.seqs),
        r_dk=sem(z.nc, z.seqs),
        s_n1=sem(z.seqs, 4),
        m_n1=sem(z.seqs, 2),
        r_n1=sem(z.seqs, 2),
        s_ga=sem(2),
        s_gac=sem(2, z.nc),
        s_gag=sem(2, z.nc),
        s_gb=sem(2),
        s_gbc=sem(2, z.nc),
        s_gbg=sem(2, z.nc),
        s_mt=sem(2, z.nt),
        s_md=sem(2),
        s_mc=sem(2, z.nc),
    )


class Box:
    pass


def layer_kernel(z, names, *refs):
    r = Box()
    for name, ref in zip(names, refs):
        setattr(r, name, ref)
    d, c, t = lax.axis_index("dp"), lax.axis_index("ctx"), lax.axis_index("tp")
    other = 1 - d
    nt, nc, rows, block, width, hw = z.nt, z.nc, z.rows, z.block, z.width, z.hw
    seqs, half = z.seqs, z.half

    def each(count, body, first=0):
        def step(i, carry):
            body(i)
            return carry

        lax.fori_loop(first, count, step, 0)

    def span(idx):
        return pl.ds(pl.multiple_of(idx * rows, rows), rows)

    def slot(ref, idx):
        return ref.at[:, span(idx), :]

    def piece(ref, s, idx):
        return ref.at[s, span(idx), :]

    def flat(x):
        return x.reshape(x.shape[0] * x.shape[1], x.shape[2])

    def lanes_of(shape, axis=1):
        return lax.broadcasted_iota(jnp.int32, shape, axis)

    local = []

    def fetch(src, dst):
        cp = pltpu.make_async_copy(src, dst, r.s_loc.at[len(local)])
        cp.start()
        local.append(cp)
        return cp

    my_half = pl.ds(pl.multiple_of(d * half, LANES), half)
    weights = [
        (r.wq_in, r.wqt.at[0:hw, my_half]),
        (r.wk_in, r.wkvt.at[0:hw, my_half]),
        (r.wv_in, r.wkvt.at[hw : z.kvw, my_half]),
        (r.wo_in, r.wot.at[z.voff : z.voff + hw, my_half]),
        (r.wu_in, r.wu.at[my_half, :]),
        (r.wd_in, r.wd.at[my_half, :]),
    ]
    first_cols = 2 * width
    cp_tok = fetch(r.tok_in, slot(r.tok, t))
    cp_wm1 = fetch(r.wm_in.at[:, 0:first_cols], r.wm.at[:, 0:first_cols])
    cp_w = [fetch(src, dst) for src, dst in weights]
    cp_wm2 = fetch(r.wm_in.at[:, first_cols : z.mod], r.wm.at[:, first_cols : z.mod])
    cp_cot = fetch(r.cot_in, slot(r.cot, t))

    r.wqt[hw:WIN, :] = jnp.zeros((WIN - hw, width), BF16)
    r.wot[0 : z.voff, :] = jnp.zeros((z.voff, width), BF16)

    bar = pltpu.get_barrier_semaphore()
    pl.semaphore_signal(bar, inc=1, device_id={"dp": other}, device_id_type=MESH)
    for k in range(1, nt):
        pl.semaphore_signal(bar, inc=1, device_id={"tp": (t + k) % nt}, device_id_type=MESH)

    def greet(k):
        pl.semaphore_signal(bar, inc=1, device_id={"ctx": (c + k) % nc}, device_id_type=MESH)

    each(nc, greet, 1)

    row8 = lanes_of((8, half), 0)
    step_of = jnp.where(
        row8 % 2 == 0, r.ts_in[0, 0].astype(F32), r.ts_in[0, 1].astype(F32)
    )
    angle = step_of * jnp.exp(
        lanes_of((8, half)).astype(F32) * (-math.log(10000.0) / half)
    )
    sin_e, cos_e = jnp.sin(angle), jnp.cos(angle)

    def silu_low(v):
        return (v / (1.0 + jnp.exp(-v))).astype(BF16).astype(F32)

    sin_e, cos_e = silu_low(sin_e), silu_low(cos_e)
    first = d == 0
    own_half = jnp.where(row8 < 2, jnp.where(first, sin_e, cos_e), 0.0)
    r.emb_s[...] = jnp.where(
        (row8 >= 2) & (row8 < 4), jnp.where(first, cos_e, sin_e), 0.0
    )
    pl.semaphore_wait(bar, 1 + (nt - 1) + (nc - 1))

    side = t // 2
    mate = t + 1 - 2 * (t % 2)
    cross = 2 - side
    outer = t % 3 == 0
    inner = t % 3 != 0

    def peer(i):
        far = i // 2
        return (1 - far) * (t + i * (1 - 2 * (t % 2))) + far * ((1 - side) * i + side * (3 - i))

    class Gather:
        def __init__(self, buf, send, recv):
            self.buf, self.sems, self.recv = buf, send, recv

        def copy(self, src, s, idx, k, to):
            return remote(
                src, piece(self.buf, s, idx), self.sems.at[s, k], self.recv.at[s, idx], tp=to
            )

        def open(self, src, s):
            self.copy(src, s, t, 0, mate).start()
            self.copy(src, s, t, 1, cross).start()

        def wait(self, s, idx):
            self.copy(piece(self.buf, s, idx), s, idx, 0, mate).wait_recv()

        def relay(self, s):
            @pl.when(inner)
            def _():
                def one(i):
                    idx = peer(i)
                    self.wait(s, idx)
                    self.copy(piece(self.buf, s, idx), s, idx, i, mate).start()

                each(4, one, 2)

        def collect(self, s, work):
            def one(i):
                idx = peer(i)

                @pl.when(outer | (i == 1))
                def _():
                    self.wait(s, idx)

                if work is not None:
                    work(s, idx, i)

            each(4, one, 1)

        def close(self, s):
            mine = piece(self.buf, s, t)
            self.copy(mine, s, t, 0, mate).wait_send()
            self.copy(mine, s, t, 1, cross).wait_send()

            @pl.when(inner)
            def _():
                each(4, lambda i: self.copy(mine, s, t, i, mate).wait_send(), 2)

    class Scatter:
        def __init__(self, part, merge, got, send, msem, gsem):
            self.part, self.merge, self.got = part, merge, got
            self.sems, self.msem, self.gsem = send, msem, gsem

        def to_got(self, s, idx, i, k):
            return remote(
                piece(self.part, s, idx),
                self.got.at[s, k],
                self.sems.at[s, i],
                self.gsem.at[s, k],
                tp=idx,
            )

        def to_merge(self, s, idx, i):
            return remote(
                piece(self.part, s, idx),
                self.merge.at[s, i - 2],
                self.sems.at[s, i],
                self.msem.at[s, i - 2],
                tp=mate,
            )

        def push(self, s, idx, i):
            @pl.when(i == 1)
            def _():
                self.to_got(s, idx, i, 0).start()

            @pl.when((i > 1) & outer)
            def _():
                self.to_merge(s, idx, i).start()

        def push_all(self, s):
            for i in (3, 2):
                self.push(s, peer(i), i)
            self.push(s, mate, 1)

        def join(self, s):
            @pl.when(inner)
            def _():
                def one(k):
                    i = 3 - k
                    idx = peer(i)
                    self.to_merge(s, idx, i).wait_recv()
                    at = span(idx)
                    self.part[s, at, :] = (
                        self.part[s, at, :].astype(F32) + self.merge[s, i - 2].astype(F32)
                    ).astype(BF16)
                    self.to_got(s, idx, i, 1).start()

                each(2, one)

        def total(self, s):
            for k in range(2):
                self.to_got(s, mate, 1, k).wait_recv()
            return (
                self.part[s, span(t), :].astype(F32)
                + self.got[s, 0].astype(F32)
                + self.got[s, 1].astype(F32)
            )

        def close(self, s):
            each(4, lambda i: self.to_got(s, mate, i, 0).wait_send(), 1)

    toks = Gather(r.tok, r.s_tok, r.r_tok)
    cots = Gather(r.cot, r.s_cot, r.r_cot)
    n2s = Gather(r.n2, r.s_n2, r.r_n2)
    bgs = Gather(r.bg, r.s_bg, r.r_bg)
    brs = Scatter(r.br, r.br_m, r.br_r, r.s_br, r.m_br, r.r_br)
    g2s = Scatter(r.g2, r.g2_m, r.g2_r, r.s_g2, r.m_g2, r.r_g2)
    mls = Scatter(r.ml, r.ml_m, r.ml_r, r.s_ml, r.m_ml, r.r_ml)
    n1s = Scatter(r.g2, r.n1_m, r.n1_r, r.s_n1, r.m_n1, r.r_n1)

    for s in range(seqs):
        toks.open(r.tok_in.at[s], s)
    send_emb = remote(r.emb_s, r.emb_r, r.s_e.at[0], r.s_e.at[1], dp=other)
    send_emb.start()
    send_w = [
        remote(src, dst, r.s_w.at[0, i], r.s_w.at[1, i], dp=other)
        for i, (src, dst) in enumerate(weights)
    ]
    for cp in send_w[:3]:
        cp.start()

    send_emb.wait()
    emb4 = own_half + r.emb_r[...]
    r.emb[pl.ds(c, 1)] = emb4[None]
    emb_low = emb4.astype(BF16)

    def mod_part(lo, hi, which, ready):
        ready.wait()
        r.mod_s[:, lo:hi] = mm(emb_low, r.wm[:, lo:hi])
        cp = remote(
            r.mod_s.at[:, lo:hi], r.mod_r.at[:, lo:hi], r.s_m.at[0, which], r.s_m.at[1, which], dp=other
        )
        cp.start()
        return cp

    def mod_take(lo, hi, cp):
        cp.wait()
        for s in range(seqs):
            r.mod[s : s + 1, lo:hi] = r.mod_s[s : s + 1, lo:hi] + r.mod_r[s + 2 : s + 3, lo:hi]

    def vec(slot_idx, s):
        lo = slot_idx * width
        return r.mod[s : s + 1, lo : lo + width]

    mod1 = mod_part(0, first_cols, 0, cp_wm1)
    for cp in send_w[3:]:
        cp.start()

    def send_ctx_emb(k):
        to = (c + k) % nc
        remote(r.emb.at[c], r.emb.at[c], r.s_ec.at[0, to], r.s_ec.at[1, c], ctx=to).start()

    each(nc, send_ctx_emb, 1)

    place = (c * block + lanes_of((block, LANES), 0)).astype(F32)
    pair_of = (lanes_of((block, LANES)) % (HEAD_DIM // 2)).astype(F32)
    turn = place * jnp.exp(pair_of * (-2.0 * math.log(10000.0) / HEAD_DIM))
    low_lane = lanes_of((block, LANES)) % HEAD_DIM < HEAD_DIM // 2
    r.cosine[...] = jnp.cos(turn)
    r.sine[...] = jnp.where(low_lane, -jnp.sin(turn), jnp.sin(turn))

    def swap(x):
        low = lanes_of(x.shape) % HEAD_DIM < HEAD_DIM // 2
        return jnp.where(
            low,
            pltpu.roll(x, LANES - HEAD_DIM // 2, 1),
            pltpu.roll(x, HEAD_DIM // 2, 1),
        )

    for i in range(3):
        cp_w[i].wait()
        send_w[i].wait_recv()
    mod_take(0, first_cols, mod1)

    def make_qkv(s, idx, i):
        at = span(idx)
        unit, _ = norm_parts(r.tok[s, at, :].astype(F32))
        low = (unit * (1.0 + vec(1, s)) + vec(0, s)).astype(BF16)
        r.nrm[s, at, :] = low
        cos1, sin1 = r.cosine[at, :], r.sine[at, :]
        q_pre = mm(low, r.wqt[...], NT)
        kv_pre = mm(low, r.wkvt[...], NT)
        for j in range(WIN // LANES):
            x = q_pre[:, j * LANES : (j + 1) * LANES]
            x = (x * cos1 + swap(x) * sin1) * (HEAD_DIM ** -0.5)
            r.q[s, at, j * LANES : (j + 1) * LANES] = x.astype(BF16)
        for j in range(z.kvw // LANES):
            x = kv_pre[:, j * LANES : (j + 1) * LANES]
            keys = min(max(hw - j * LANES, 0), LANES)
            if keys > 0:
                turned = x * cos1 + swap(x) * sin1
                x = turned if keys == LANES else jnp.where(lanes_of(x.shape) < keys, turned, x)
            r.kv[c, s, at, j * LANES : (j + 1) * LANES] = x.astype(BF16)

        def send_kv(to):
            mine = r.kv.at[c, s, at, :]
            remote(mine, mine, r.s_kv.at[to, s, idx], r.r_kv.at[c, s, idx], ctx=to).start()

        each(nc, send_kv, c + 1)

    cp_tok.wait()
    for s in range(seqs):
        make_qkv(s, t, 0)
    mod2 = mod_part(first_cols, z.mod, 1, cp_wm2)
    for s in range(seqs):
        toks.relay(s)
        toks.collect(s, make_qkv)
    for s in range(seqs):
        toks.close(s)
    cp_cot.wait()
    for s in range(seqs):
        cots.open(r.cot_in.at[s], s)
    mod_take(first_cols, z.mod, mod2)
    for i in range(3, 6):
        cp_w[i].wait()
        send_w[i].wait_recv()

    eye = (lanes_of((WIN, WIN), 0) == lanes_of((WIN, WIN))).astype(BF16)

    def head_of(x, h, off=0):
        lane = lanes_of(x.shape)
        lo = off + h * HEAD_DIM
        return jnp.where((lane >= lo) & (lane < lo + HEAD_DIM), x, jnp.zeros_like(x))

    def attend_seq(s):
        r.stat[0] = jnp.full((8, block), NEG, F32)
        r.stat[1] = jnp.zeros((8, block), F32)
        r.acc[...] = jnp.zeros((hw, block), F32)
        q = r.q[s]

        def one_block(back):
            j = c - back

            @pl.when(back > 0)
            def _():
                def take(idx):
                    there = r.kv.at[j, s, span(idx), :]
                    remote(
                        there, there, r.s_kv.at[j, s, idx], r.r_kv.at[j, s, idx], ctx=j
                    ).wait_recv()

                each(nt, take)

            keys = r.kv[j, s, :, 0:WIN]
            r.vt[...] = mm(eye, r.kv[j, s, :, z.vlo : z.vlo + WIN], NT).astype(BF16)
            for h in range(z.heads):
                scores = mm(keys, head_of(q, h), NT)
                old = r.stat[0, h : h + 1, :]
                top = jnp.maximum(old, jnp.max(scores, axis=0, keepdims=True))
                prob = jnp.exp(scores - top)
                fade = jnp.exp(old - top)
                r.stat[0, h : h + 1, :] = top
                r.stat[1, h : h + 1, :] = r.stat[1, h : h + 1, :] * fade + jnp.sum(
                    prob, axis=0, keepdims=True
                )
                lo = h * HEAD_DIM
                vt = r.vt[z.voff + lo : z.voff + lo + HEAD_DIM, :]
                r.acc[lo : lo + HEAD_DIM, :] = r.acc[lo : lo + HEAD_DIM, :] * fade + mm(
                    vt, prob.astype(BF16)
                )

        each(c + 1, one_block)
        for h in range(z.heads):
            lo = h * HEAD_DIM
            denom = r.stat[1, h : h + 1, :]
            r.lse[s, h : h + 1, :] = r.stat[0, h : h + 1, :] + jnp.log(denom)
            r.att[s, lo : lo + HEAD_DIM, :] = r.acc[lo : lo + HEAD_DIM, :] / denom
        low = jnp.transpose(r.att[s]).astype(BF16)
        r.attl[s, :, 0:hw] = low
        r.attl[s, :, hw:WIN] = jnp.zeros((block, WIN - hw), BF16)
        r.br[s] = mm(low, r.wot[z.voff : z.voff + hw, :]).astype(BF16)
        brs.push_all(s)

    each(seqs, attend_seq)
    for s in range(seqs):
        brs.join(s)
    for s in range(seqs):
        cots.relay(s)

    for s in range(seqs):
        branch = brs.total(s)
        r.branch[s] = branch
        middle = r.tok[s, span(t), :].astype(F32) + vec(2, s) * branch
        r.middle[s] = middle
        unit, _ = norm_parts(middle)
        r.n2[s, span(t), :] = (unit * (1.0 + vec(4, s)) + vec(3, s)).astype(BF16)
        n2s.open(piece(r.n2, s, t), s)

    def feed(s, idx, i):
        at = span(idx)
        hid = mm(r.n2[s, at, :], r.wu[...])
        square = hid * hid
        tanh = jnp.tanh(GELU_C * (hid + GELU_A * (hid * square)))
        r.act[s, at, :] = (0.5 * hid * (1.0 + tanh)).astype(BF16)
        slope = 0.5 * (1.0 + tanh) + 0.5 * hid * (1.0 - tanh * tanh) * (
            GELU_C * (1.0 + 3.0 * GELU_A * square)
        )
        low = (vec(5, s) * r.cot[s, at, :].astype(F32)).astype(BF16)
        r.mgrad[s, at, :] = low
        hgrad = (slope * mm(low, r.wd[...])).astype(BF16)
        r.hgrad[s, at, :] = hgrad
        r.g2[s, at, :] = mm(hgrad, r.wu[...], NT).astype(BF16)
        g2s.push(s, idx, i)

    for s in range(seqs):
        feed(s, t, 0)
    for s in range(seqs):
        cots.collect(s, None)
        n2s.relay(s)
        n2s.collect(s, feed)
    g2s.join(0)

    def pair_grads(lhs, rhs, mine, sent, lo, hi):
        right = flat(rhs[...])
        for which, dst in ((other, sent), (d, mine)):
            cols = pl.ds(pl.multiple_of(which * half, half), half)
            left = flat(lhs[:, :, cols])
            dst[:, lo:hi] = mm(left, right, TN).astype(BF16)

    pair_grads(r.mgrad, r.act, r.ga_o, r.ga_s, z.ff, 2 * z.ff)
    pair_grads(r.n2, r.hgrad, r.ga_o, r.ga_s, 0, z.ff)
    send_ga = remote(r.ga_s, r.ga_r, r.s_ga.at[0], r.s_ga.at[1], dp=other)
    send_ga.start()
    g2s.join(1)
    for s in range(seqs):
        r.ml[s] = mm(r.act[s], r.wd[...], NT).astype(BF16)

    r.msum[...] = jnp.zeros((8, z.mod), F32)

    def keep_sum(slot_idx, s, value):
        lo = slot_idx * width
        r.msum[s : s + 1, lo : lo + width] = jnp.sum(value, axis=0, keepdims=True)

    for s in range(seqs):
        grad2 = g2s.total(s)
        unit, rstd = norm_parts(r.middle[s])
        mid_grad = r.cot[s, span(t), :].astype(F32) + norm_back(grad2, unit, rstd, vec(4, s))
        r.midg[s] = mid_grad
        r.bg[s, span(t), :] = (vec(2, s) * mid_grad).astype(BF16)
        bgs.open(piece(r.bg, s, t), s)
        keep_sum(3, s, grad2)
        keep_sum(4, s, grad2 * unit)
        keep_sum(2, s, mid_grad * r.branch[s])

    def out_grads(s, idx, i):
        at = span(idx)
        r.do[s, at, :] = mm(r.bg[s, at, :], r.wot[...], NT).astype(BF16)

    for s in range(seqs):
        out_grads(s, t, 0)
    bgs.relay(0)
    bgs.collect(0, out_grads)

    class Reduction:
        def __init__(self, got, mine, theirs, buf, total, sems, sems_all):
            self.got, self.mine, self.theirs, self.buf, self.total = got, mine, theirs, buf, total
            self.sems, self.sems_all = sems, sems_all
            self.chunk = buf.shape[1]
            self.owners = mine.shape[0] // self.chunk

        def rows(self, o):
            return pl.ds(pl.multiple_of(o * self.chunk, 16), self.chunk)

        def part(self, o):
            return remote(
                self.mine.at[self.rows(o), :],
                self.buf.at[c],
                self.sems.at[0, o],
                self.sems.at[1, c],
                ctx=o,
            )

        def share(self, owner, to):
            here = self.total.at[self.rows(owner), :]
            return remote(here, here, self.sems_all.at[0, to], self.sems_all.at[1, owner], ctx=to)

        def to_owners(self, body):
            def one(k):
                o = (c + k) % nc

                @pl.when(o < self.owners)
                def _():
                    body(o)

            each(nc, one, 1)

        def as_owner(self, body):
            @pl.when(c < self.owners)
            def _():
                body()

        def send(self):
            self.got.wait()
            self.mine[...] = (self.mine[...].astype(F32) + self.theirs[...].astype(F32)).astype(
                BF16
            )
            self.to_owners(lambda o: self.part(o).start())

        def sum(self):
            def body():
                def add(k, acc):
                    fr = (c + k) % nc
                    there = self.buf.at[fr]
                    remote(
                        there, there, self.sems.at[0, fr], self.sems.at[1, fr], ctx=fr
                    ).wait_recv()
                    return acc + self.buf[fr].astype(F32)

                acc = self.mine[self.rows(c), :].astype(F32)
                if nc <= 4:
                    for k in range(1, nc):
                        acc = add(k, acc)
                else:
                    acc = lax.fori_loop(1, nc, add, acc)
                self.total[self.rows(c), :] = acc.astype(BF16)
                each(nc, lambda k: self.share(c, (c + k) % nc).start(), 1)

            self.as_owner(body)

        def take(self):
            def one(o):
                self.share(o, o).wait_recv()
                self.part(o).wait_send()

            self.to_owners(one)
            self.as_owner(
                lambda: each(nc, lambda k: self.share(c, (c + k) % nc).wait_send(), 1)
            )

    red_a = Reduction(send_ga, r.ga_o, r.ga_r, r.ga_c, r.ga_t, r.s_gac, r.s_gag)
    red_a.send()
    bgs.relay(1)

    def back_seq(s):
        do = r.do[s]
        r.dot[...] = mm(eye, do, NT).astype(BF16)
        for h in range(z.heads):
            lo = h * HEAD_DIM
            r.delta[s, h : h + 1, :] = jnp.sum(
                r.dot[z.voff + lo : z.voff + lo + HEAD_DIM, :].astype(F32)
                * r.att[s, lo : lo + HEAD_DIM, :],
                axis=0,
                keepdims=True,
            )
        r.dqt[...] = jnp.zeros((hw, block), F32)
        q = r.q[s]

        def one_block(j):
            keys = r.kv[j, s, :, 0:WIN]
            vals = r.kv[j, s, :, z.vlo : z.vlo + WIN]
            r.vt[...] = mm(eye, keys, NT).astype(BF16)
            dk = jnp.zeros((block, WIN), F32)
            dv = jnp.zeros((block, WIN), F32)
            for h in range(z.heads):
                lo = h * HEAD_DIM
                qh = head_of(q, h)
                doh = head_of(do, h, z.voff)
                prob = jnp.exp(mm(keys, qh, NT) - r.lse[s, h : h + 1, :])
                dprob = mm(vals, doh, NT)
                dsc = (prob * (dprob - r.delta[s, h : h + 1, :])).astype(BF16)
                dv = dv + mm(prob.astype(BF16), doh)
                dk = dk + mm(dsc, qh)
                r.dqt[lo : lo + HEAD_DIM, :] += mm(r.vt[lo : lo + HEAD_DIM, :], dsc)
            over = WIN - z.vlo
            pieces = (
                (0, z.vlo, dk[:, 0 : z.vlo]),
                (z.vlo, WIN, dk[:, z.vlo : WIN] + dv[:, 0:over]),
                (WIN, z.kvw, dv[:, over:WIN]),
            )

            @pl.when(j < c)
            def _():
                for lo, hi, piece in pieces:
                    r.kv[j, s, :, lo:hi] = piece.astype(BF16)
                remote(
                    r.kv.at[j, s], r.dkv_r.at[c, s], r.s_dk.at[j, s], r.r_dk.at[c, s], ctx=j
                ).start()

            @pl.when(j == c)
            def _():
                for lo, hi, piece in pieces:
                    r.dkv[s, :, lo:hi] = piece

        each(c + 1, one_block)
        r.dq[s, :, 0:hw] = jnp.transpose(r.dqt[...]) * (HEAD_DIM ** -0.5)
        r.dq[s, :, hw:WIN] = jnp.zeros((block, WIN - hw), F32)

    def kv_sent(j):
        for s in range(seqs):
            each(
                nt,
                lambda idx: remote(
                    r.kv.at[c, s, span(idx), :],
                    r.kv.at[c, s, span(idx), :],
                    r.s_kv.at[j, s, idx],
                    r.r_kv.at[c, s, idx],
                    ctx=j,
                ).wait_send(),
            )

    each(nc, kv_sent, c + 1)

    def back_step(s):
        @pl.when(s == 1)
        def _():
            bgs.collect(1, out_grads)
            for i in range(seqs):
                mls.push_all(i)

        back_seq(s)

    each(seqs, back_step)

    for s in range(seqs):
        g2s.close(s)
    cos1, sin1 = r.cosine[...], r.sine[...]
    for s in range(seqs):

        def add_dkv(j):
            there = r.dkv_r.at[j, s]
            remote(there, there, r.s_dk.at[j, s], r.r_dk.at[j, s], ctx=j).wait_recv()
            r.dkv[s] += r.dkv_r[j, s].astype(F32)

        each(nc, add_dkv, c + 1)
        for j in range(WIN // LANES):
            x = r.dq[s, :, j * LANES : (j + 1) * LANES]
            r.qb[s, :, j * LANES : (j + 1) * LANES] = (x * cos1 - swap(x) * sin1).astype(BF16)
        for j in range(z.kvw // LANES):
            x = r.dkv[s, :, j * LANES : (j + 1) * LANES]
            keys = min(max(hw - j * LANES, 0), LANES)
            if keys > 0:
                turned = x * cos1 - swap(x) * sin1
                x = turned if keys == LANES else jnp.where(lanes_of(x.shape) < keys, turned, x)
            r.kvb[s, :, j * LANES : (j + 1) * LANES] = x.astype(BF16)
        r.g2[s] = (mm(r.qb[s], r.wqt[...]) + mm(r.kvb[s], r.wkvt[...])).astype(BF16)
        n1s.push_all(s)

    for which, dst in ((other, r.gb_s), (d, r.gb_o)):
        cols = pl.ds(pl.multiple_of(which * half, LANES), half)
        right = flat(r.nrm[:, :, cols])
        dst[0:hw, :] = mm(flat(r.qb[:, :, 0:hw]), right, TN).astype(BF16)
        dst[hw : 3 * hw, :] = mm(flat(r.kvb[...]), right, TN).astype(BF16)
        right = flat(r.bg[:, :, cols])
        dst[3 * hw : 4 * hw, :] = mm(flat(r.attl[:, :, 0:hw]), right, TN).astype(BF16)
    send_gb = remote(r.gb_s, r.gb_r, r.s_gb.at[0], r.s_gb.at[1], dp=other)
    send_gb.start()
    red_a.sum()
    for s in range(seqs):
        n1s.join(s)

    for s in range(seqs):
        mls.join(s)
    outs = []

    def store(src, dst):
        cp = pltpu.make_async_copy(src, dst, r.s_loc.at[len(local) + len(outs)])
        cp.start()
        outs.append(cp)

    for s in range(seqs):
        grad1 = n1s.total(s)
        unit, rstd = norm_parts(r.tok[s, span(t), :].astype(F32))
        keep_sum(0, s, grad1)
        keep_sum(1, s, grad1 * unit)
        r.gtok[s] = r.midg[s] + norm_back(grad1, unit, rstd, vec(1, s))
        mlp = mls.total(s)
        r.res[s] = (r.middle[s] + vec(5, s) * mlp).astype(BF16)
        keep_sum(5, s, r.cot[s, span(t), :].astype(F32) * mlp)
    red_b = Reduction(send_gb, r.gb_o, r.gb_r, r.gb_c, r.gb_t, r.s_gbc, r.s_gbg)
    red_b.send()

    def mcol(idx):
        return pl.ds(pl.multiple_of(idx * z.mcols, LANES), z.mcols)

    for k in range(1, nt):
        to = (t + k) % nt
        remote(
            r.msum.at[:, mcol(to)], r.mt_r.at[t], r.s_mt.at[0, to], r.s_mt.at[1, t], tp=to
        ).start()
    store(r.res, r.res_out)
    store(r.gtok, r.gtok_out)
    red_b.sum()
    total = r.msum[:, mcol(t)]
    for k in range(1, nt):
        fr = (t + k) % nt
        there = r.mt_r.at[fr]
        remote(there, there, r.s_mt.at[0, fr], r.s_mt.at[1, fr], tp=fr).wait_recv()
        total = total + r.mt_r[fr]
    r.md_s[...] = total
    send_md = remote(r.md_s, r.md_r, r.s_md.at[0], r.s_md.at[1], dp=other)
    send_md.start()
    send_md.wait()
    r.mg[pl.ds(c, 1), 0:2, :] = total[None, 0:2, :]
    r.mg[pl.ds(c, 1), 2:4, :] = r.md_r[0:2, :][None]
    r.mg[pl.ds(c, 1), 4:8, :] = jnp.zeros((1, 4, z.mcols), F32)

    def send_mg(k):
        to = (c + k) % nc
        remote(r.mg.at[c], r.mg.at[c], r.s_mc.at[0, to], r.s_mc.at[1, c], ctx=to).start()

    each(nc, send_mg, 1)
    red_a.take()
    store(r.ga_t, r.ga_out)
    red_b.take()
    store(r.gb_t, r.gb_out)

    def take_small(k):
        fr = (c + k) % nc
        for buf, sems in ((r.mg, r.s_mc), (r.emb, r.s_ec)):
            remote(buf.at[fr], buf.at[fr], sems.at[0, fr], sems.at[1, fr], ctx=fr).wait_recv()
            remote(buf.at[c], buf.at[c], sems.at[0, fr], sems.at[1, c], ctx=fr).wait_send()

    each(nc, take_small, 1)
    store(r.mg, r.mg_out)
    store(r.emb, r.emb_out)

    for cp in send_w:
        cp.wait_send()
    for s in range(seqs):
        for group in (cots, n2s, bgs, brs, mls, n1s):
            group.close(s)
    for k in range(1, nt):
        to = (t + k) % nt
        remote(
            r.msum.at[:, mcol(to)], r.mt_r.at[t], r.s_mt.at[0, to], r.s_mt.at[1, t], tp=to
        ).wait_send()

    def dkv_sent(j):
        for s in range(seqs):
            remote(
                r.kv.at[j, s], r.dkv_r.at[c, s], r.s_dk.at[j, s], r.r_dk.at[c, s], ctx=j
            ).wait_send()

    each(c, dkv_sent)
    for cp in outs:
        cp.wait()


def finish_kernel(z, ga, gb, emb, mg, res, gtok, *refs):
    outs, stage, sems = refs[:9], refs[9:18], refs[18]
    hw = z.hw
    copies = []

    def put(i, value):
        stage[i][...] = value
        cp = pltpu.make_async_copy(stage[i], outs[i], sems.at[i])
        cp.start()
        copies.append(cp)

    put(6, ga[:, 0 : z.ff].astype(F32))
    put(7, ga[:, z.ff : 2 * z.ff].astype(F32))
    for i in range(4):
        put(2 + i, gb[i * hw : (i + 1) * hw, :].astype(F32))
    put(0, res[...])
    put(1, gtok[...])
    e = emb[...].reshape(z.nc * 8, z.half)
    m = mg[...].reshape(z.nc * 8, z.mcols)
    put(
        8,
        lax.dot_general(
            e, m, TN, precision=lax.Precision.HIGHEST, preferred_element_type=F32
        ),
    )
    for cp in copies:
        cp.wait()


IN_NAMES = (
    "tok_in",
    "ts_in",
    "wq_in",
    "wk_in",
    "wv_in",
    "wo_in",
    "wu_in",
    "wd_in",
    "wm_in",
    "cot_in",
)
OUT_NAMES = ("res_out", "gtok_out", "ga_out", "gb_out", "emb_out", "mg_out")


def solution(mesh):
    def shards(tokens, steps, wq, wk, wv, wo, wu, wd, wm, cot):
        wq, wk, wv, wo = wq.T, wk.T, wv.T, wo.T
        z = Dims(mesh, tokens.shape, wq.shape, wu.shape, wm.shape)
        table = scratch_table(z)
        names = list(IN_NAMES) + list(OUT_NAMES) + list(table)
        hbm = pl.BlockSpec(memory_space=pl.ANY)
        vmem = pl.BlockSpec(memory_space=pltpu.VMEM)
        smem = pl.BlockSpec(memory_space=pltpu.SMEM)
        own = (z.seqs, z.rows, z.width)
        shape = jax.ShapeDtypeStruct
        outs = pl.pallas_call(
            functools.partial(layer_kernel, z, names),
            out_shape=(
                shape(own, BF16),
                shape(own, F32),
                shape((z.half, z.wide), BF16),
                shape((z.heads_rows, z.half), BF16),
                shape((z.nc, 8, z.half), F32),
                shape((z.nc, 8, z.mcols), F32),
            ),
            in_specs=[hbm, smem] + [hbm] * 8,
            out_specs=[hbm] * 6,
            scratch_shapes=list(table.values()),
            compiler_params=pltpu.CompilerParams(
                collective_id=0, has_side_effects=True, vmem_limit_bytes=VMEM_BYTES
            ),
            name="layer",
        )(tokens, steps.T, wq, wk, wv, wo, wu, wd, wm, cot)
        res, gtok, ga, gb, emb, mg = outs
        shapes = (
            (own, BF16),
            (own, F32),
            ((z.hw, z.half), F32),
            ((z.hw, z.half), F32),
            ((z.hw, z.half), F32),
            ((z.hw, z.half), F32),
            ((z.half, z.ff), F32),
            ((z.half, z.ff), F32),
            ((z.half, z.mcols), F32),
        )
        done = pl.pallas_call(
            functools.partial(finish_kernel, z),
            out_shape=tuple(shape(*o) for o in shapes),
            in_specs=[vmem] * 6,
            out_specs=[hbm] * 9,
            scratch_shapes=[pltpu.VMEM(*o) for o in shapes] + [pltpu.SemaphoreType.DMA((9,))],
            compiler_params=pltpu.CompilerParams(vmem_limit_bytes=VMEM_BYTES),
            name="finish",
        )(ga, gb, emb, mg, res, gtok)
        return done[:2] + tuple(g.T for g in done[2:6]) + done[6:]

    rows = P("dp", ("ctx", "tp"), None)
    cols = P("dp", "tp")
    return jax.shard_map(
        shards,
        mesh=mesh,
        in_specs=(rows, P("dp", "ctx")) + (cols,) * 6 + (P("dp", None), rows),
        out_specs=(rows, rows) + (cols,) * 7,
        check_vma=False,
    )
```

```python
import functools
import math

import jax
import jax.numpy as jnp
from jax import lax
from jax.experimental import pallas as pl
from jax.experimental.pallas import tpu as pltpu
from jax.sharding import PartitionSpec as P

MESH = pl.DeviceIdType.MESH
HEAD_DIM = 64
WIN = 256
LANES = 128
EPS = 1e-06
NEG = -1e30
GELU_C = 0.7978845608028654
GELU_A = 0.044715
F32 = jnp.float32
BF16 = jnp.bfloat16
VMEM_BYTES = 62 * 1024 * 1024

NN = (((1,), (0,)), ((), ()))
NT = (((1,), (1,)), ((), ()))
TN = (((0,), (0,)), ((), ()))


def mm(a, b, dims=NN):
    return lax.dot_general(a, b, dims, preferred_element_type=F32)


def norm_parts(x):
    center = x - jnp.mean(x, axis=-1, keepdims=True)
    rstd = lax.rsqrt(jnp.mean(center * center, axis=-1, keepdims=True) + EPS)
    return center * rstd, rstd


def norm_back(grad, unit, rstd, scale):
    dn = grad * (1.0 + scale)
    return rstd * (
        dn
        - jnp.mean(dn, axis=-1, keepdims=True)
        - unit * jnp.mean(dn * unit, axis=-1, keepdims=True)
    )


def remote(src, dst, send, recv, **dev):
    return pltpu.make_async_remote_copy(
        src_ref=src, dst_ref=dst, send_sem=send, recv_sem=recv, device_id=dev, device_id_type=MESH
    )


def chunk_rows(count, devices):
    return 16 * -(-(count // 16) // devices)


class Dims:
    def __init__(self, mesh, tokens, query, up, mod):
        self.nc = mesh.shape["ctx"]
        self.nt = mesh.shape["tp"]
        self.seqs, self.rows, self.width = tokens
        self.block = self.rows * self.nt
        self.hw, self.half = query
        self.heads = self.hw // HEAD_DIM
        self.ff = up[1]
        self.mod = mod[1]
        self.kvw = 2 * self.hw
        self.vlo = self.kvw - WIN
        self.voff = self.hw - self.vlo
        self.wide = 2 * self.ff
        self.heads_rows = 4 * self.hw
        self.mcols = self.mod // self.nt


def scratch_table(z):
    vm = lambda shape, dtype=BF16: pltpu.VMEM(shape, dtype)
    sem = lambda *shape: pltpu.SemaphoreType.DMA(shape)
    full = (z.seqs, z.block, z.width)
    own = (z.seqs, z.rows, z.width)
    pair = (z.seqs, 2, z.rows, z.width)
    return dict(
        tok=vm(full),
        cot=vm(full),
        wqt=vm((WIN, z.width)),
        wkvt=vm((z.kvw, z.width)),
        wot=vm((WIN, z.width)),
        wu=vm((z.width, z.ff)),
        wd=vm((z.width, z.ff)),
        wm=vm((z.half, z.mod)),
        emb_s=vm((8, z.half), F32),
        emb_r=vm((8, z.half), F32),
        emb=vm((z.nc, 8, z.half), F32),
        mod_s=vm((8, z.mod), F32),
        mod_r=vm((8, z.mod), F32),
        mod=vm((8, z.mod), F32),
        cosine=vm((z.block, LANES), F32),
        sine=vm((z.block, LANES), F32),
        nrm=vm(full),
        q=vm((z.seqs, z.block, WIN)),
        kv=vm((z.nc, z.seqs, z.block, z.kvw)),
        vt=vm((WIN, z.block)),
        stat=vm((2, 8, z.block), F32),
        acc=vm((z.hw, z.block), F32),
        att=vm((z.seqs, z.hw, z.block), F32),
        attl=vm((z.seqs, z.block, WIN)),
        lse=vm((z.seqs, 8, z.block), F32),
        delta=vm((z.seqs, 8, z.block), F32),
        br=vm(full),
        br_m=vm(pair),
        br_r=vm(pair),
        branch=vm(own, F32),
        middle=vm(own, F32),
        n2=vm(full),
        act=vm((z.seqs, z.block, z.ff)),
        hgrad=vm((z.seqs, z.block, z.ff)),
        mgrad=vm(full),
        g2=vm(full),
        g2_m=vm(pair),
        g2_r=vm(pair),
        ml=vm(full),
        ml_m=vm(pair),
        ml_r=vm(pair),
        midg=vm(own, F32),
        bg=vm(full),
        do=vm((z.seqs, z.block, WIN)),
        dot=vm((WIN, z.block)),
        dqt=vm((z.hw, z.block), F32),
        dq=vm((z.seqs, z.block, WIN), F32),
        dkv=vm((z.seqs, z.block, z.kvw), F32),
        dkv_r=vm((z.nc, z.seqs, z.block, z.kvw)),
        qb=vm((z.seqs, z.block, WIN)),
        kvb=vm((z.seqs, z.block, z.kvw)),
        n1_m=vm(pair),
        n1_r=vm(pair),
        ga_s=vm((z.half, z.wide)),
        ga_o=vm((z.half, z.wide)),
        ga_r=vm((z.half, z.wide)),
        ga_c=vm((z.nc, chunk_rows(z.half, z.nc), z.wide)),
        ga_t=vm((z.half, z.wide)),
        gb_s=vm((z.heads_rows, z.half)),
        gb_o=vm((z.heads_rows, z.half)),
        gb_r=vm((z.heads_rows, z.half)),
        gb_c=vm((z.nc, chunk_rows(z.heads_rows, z.nc), z.half)),
        gb_t=vm((z.heads_rows, z.half)),
        msum=vm((8, z.mod), F32),
        mt_r=vm((z.nt, 8, z.mcols), F32),
        md_s=vm((8, z.mcols), F32),
        md_r=vm((8, z.mcols), F32),
        mg=vm((z.nc, 8, z.mcols), F32),
        res=vm(own),
        gtok=vm(own, F32),
        s_loc=sem(16),
        s_w=sem(2, 6),
        s_e=sem(2),
        s_ec=sem(2, z.nc),
        s_m=sem(2, 2),
        s_tok=sem(z.seqs, 4),
        r_tok=sem(z.seqs, z.nt),
        s_cot=sem(z.seqs, 4),
        r_cot=sem(z.seqs, z.nt),
        s_kv=sem(z.nc, z.seqs, z.nt),
        r_kv=sem(z.nc, z.seqs, z.nt),
        s_br=sem(z.seqs, 4),
        m_br=sem(z.seqs, 2),
        r_br=sem(z.seqs, 2),
        s_n2=sem(z.seqs, 4),
        r_n2=sem(z.seqs, z.nt),
        s_g2=sem(z.seqs, 4),
        m_g2=sem(z.seqs, 2),
        r_g2=sem(z.seqs, 2),
        s_ml=sem(z.seqs, 4),
        m_ml=sem(z.seqs, 2),
        r_ml=sem(z.seqs, 2),
        s_bg=sem(z.seqs, 4),
        r_bg=sem(z.seqs, z.nt),
        s_dk=sem(z.nc, z.seqs),
        r_dk=sem(z.nc, z.seqs),
        s_n1=sem(z.seqs, 4),
        m_n1=sem(z.seqs, 2),
        r_n1=sem(z.seqs, 2),
        s_ga=sem(2),
        s_gac=sem(2, z.nc),
        s_gag=sem(2, z.nc),
        s_gb=sem(2),
        s_gbc=sem(2, z.nc),
        s_gbg=sem(2, z.nc),
        s_mt=sem(2, z.nt),
        s_md=sem(2),
        s_mc=sem(2, z.nc),
    )


class Box:
    pass


def layer_kernel(z, names, *refs):
    r = Box()
    for name, ref in zip(names, refs):
        setattr(r, name, ref)
    d, c, t = lax.axis_index("dp"), lax.axis_index("ctx"), lax.axis_index("tp")
    other = 1 - d
    nt, nc, rows, block, width, hw = z.nt, z.nc, z.rows, z.block, z.width, z.hw
    seqs, half = z.seqs, z.half

    def each(count, body, first=0):
        def step(i, carry):
            body(i)
            return carry

        lax.fori_loop(first, count, step, 0)

    def span(idx):
        return pl.ds(pl.multiple_of(idx * rows, rows), rows)

    def slot(ref, idx):
        return ref.at[:, span(idx), :]

    def piece(ref, s, idx):
        return ref.at[s, span(idx), :]

    def flat(x):
        return x.reshape(x.shape[0] * x.shape[1], x.shape[2])

    def lanes_of(shape, axis=1):
        return lax.broadcasted_iota(jnp.int32, shape, axis)

    local = []

    def fetch(src, dst):
        cp = pltpu.make_async_copy(src, dst, r.s_loc.at[len(local)])
        cp.start()
        local.append(cp)
        return cp

    my_half = pl.ds(pl.multiple_of(d * half, LANES), half)
    weights = [
        (r.wq_in, r.wqt.at[0:hw, my_half]),
        (r.wk_in, r.wkvt.at[0:hw, my_half]),
        (r.wv_in, r.wkvt.at[hw : z.kvw, my_half]),
        (r.wo_in, r.wot.at[z.voff : z.voff + hw, my_half]),
        (r.wu_in, r.wu.at[my_half, :]),
        (r.wd_in, r.wd.at[my_half, :]),
    ]
    first_cols = 2 * width
    cp_tok = fetch(r.tok_in, slot(r.tok, t))
    cp_wm1 = fetch(r.wm_in.at[:, 0:first_cols], r.wm.at[:, 0:first_cols])
    cp_w = [fetch(src, dst) for src, dst in weights]
    cp_wm2 = fetch(r.wm_in.at[:, first_cols : z.mod], r.wm.at[:, first_cols : z.mod])
    cp_cot = fetch(r.cot_in, slot(r.cot, t))

    r.wqt[hw:WIN, :] = jnp.zeros((WIN - hw, width), BF16)
    r.wot[0 : z.voff, :] = jnp.zeros((z.voff, width), BF16)

    bar = pltpu.get_barrier_semaphore()
    pl.semaphore_signal(bar, inc=1, device_id={"dp": other}, device_id_type=MESH)
    for k in range(1, nt):
        pl.semaphore_signal(bar, inc=1, device_id={"tp": (t + k) % nt}, device_id_type=MESH)

    def greet(k):
        pl.semaphore_signal(bar, inc=1, device_id={"ctx": (c + k) % nc}, device_id_type=MESH)

    each(nc, greet, 1)

    row8 = lanes_of((8, half), 0)
    step_of = jnp.where(
        row8 % 2 == 0, r.ts_in[0, 0].astype(F32), r.ts_in[0, 1].astype(F32)
    )
    angle = step_of * jnp.exp(
        lanes_of((8, half)).astype(F32) * (-math.log(10000.0) / half)
    )
    sin_e, cos_e = jnp.sin(angle), jnp.cos(angle)

    def silu_low(v):
        return (v / (1.0 + jnp.exp(-v))).astype(BF16).astype(F32)

    sin_e, cos_e = silu_low(sin_e), silu_low(cos_e)
    first = d == 0
    own_half = jnp.where(row8 < 2, jnp.where(first, sin_e, cos_e), 0.0)
    r.emb_s[...] = jnp.where(
        (row8 >= 2) & (row8 < 4), jnp.where(first, cos_e, sin_e), 0.0
    )
    pl.semaphore_wait(bar, 1 + (nt - 1) + (nc - 1))

    side = t // 2
    mate = t + 1 - 2 * (t % 2)
    cross = 2 - side
    outer = t % 3 == 0
    inner = t % 3 != 0

    def peer(i):
        far = i // 2
        return (1 - far) * (t + i * (1 - 2 * (t % 2))) + far * ((1 - side) * i + side * (3 - i))

    class Gather:
        def __init__(self, buf, send, recv):
            self.buf, self.sems, self.recv = buf, send, recv

        def copy(self, src, s, idx, k, to):
            return remote(
                src, piece(self.buf, s, idx), self.sems.at[s, k], self.recv.at[s, idx], tp=to
            )

        def open(self, src, s):
            self.copy(src, s, t, 0, mate).start()
            self.copy(src, s, t, 1, cross).start()

        def wait(self, s, idx):
            self.copy(piece(self.buf, s, idx), s, idx, 0, mate).wait_recv()

        def relay(self, s):
            @pl.when(inner)
            def _():
                def one(i):
                    idx = peer(i)
                    self.wait(s, idx)
                    self.copy(piece(self.buf, s, idx), s, idx, i, mate).start()

                each(4, one, 2)

        def collect(self, s, work):
            def one(i):
                idx = peer(i)

                @pl.when(outer | (i == 1))
                def _():
                    self.wait(s, idx)

                if work is not None:
                    work(s, idx, i)

            each(4, one, 1)

        def close(self, s):
            mine = piece(self.buf, s, t)
            self.copy(mine, s, t, 0, mate).wait_send()
            self.copy(mine, s, t, 1, cross).wait_send()

            @pl.when(inner)
            def _():
                each(4, lambda i: self.copy(mine, s, t, i, mate).wait_send(), 2)

    class Scatter:
        def __init__(self, part, merge, got, send, msem, gsem):
            self.part, self.merge, self.got = part, merge, got
            self.sems, self.msem, self.gsem = send, msem, gsem

        def to_got(self, s, idx, i, k):
            return remote(
                piece(self.part, s, idx),
                self.got.at[s, k],
                self.sems.at[s, i],
                self.gsem.at[s, k],
                tp=idx,
            )

        def to_merge(self, s, idx, i):
            return remote(
                piece(self.part, s, idx),
                self.merge.at[s, i - 2],
                self.sems.at[s, i],
                self.msem.at[s, i - 2],
                tp=mate,
            )

        def push(self, s, idx, i):
            @pl.when(i == 1)
            def _():
                self.to_got(s, idx, i, 0).start()

            @pl.when((i > 1) & outer)
            def _():
                self.to_merge(s, idx, i).start()

        def push_all(self, s):
            for i in (3, 2):
                self.push(s, peer(i), i)
            self.push(s, mate, 1)

        def join(self, s):
            @pl.when(inner)
            def _():
                def one(k):
                    i = 3 - k
                    idx = peer(i)
                    self.to_merge(s, idx, i).wait_recv()
                    at = span(idx)
                    self.part[s, at, :] = (
                        self.part[s, at, :].astype(F32) + self.merge[s, i - 2].astype(F32)
                    ).astype(BF16)
                    self.to_got(s, idx, i, 1).start()

                each(2, one)

        def total(self, s):
            for k in range(2):
                self.to_got(s, mate, 1, k).wait_recv()
            return (
                self.part[s, span(t), :].astype(F32)
                + self.got[s, 0].astype(F32)
                + self.got[s, 1].astype(F32)
            )

        def close(self, s):
            each(4, lambda i: self.to_got(s, mate, i, 0).wait_send(), 1)

    toks = Gather(r.tok, r.s_tok, r.r_tok)
    cots = Gather(r.cot, r.s_cot, r.r_cot)
    n2s = Gather(r.n2, r.s_n2, r.r_n2)
    bgs = Gather(r.bg, r.s_bg, r.r_bg)
    brs = Scatter(r.br, r.br_m, r.br_r, r.s_br, r.m_br, r.r_br)
    g2s = Scatter(r.g2, r.g2_m, r.g2_r, r.s_g2, r.m_g2, r.r_g2)
    mls = Scatter(r.ml, r.ml_m, r.ml_r, r.s_ml, r.m_ml, r.r_ml)
    n1s = Scatter(r.g2, r.n1_m, r.n1_r, r.s_n1, r.m_n1, r.r_n1)

    for s in range(seqs):
        toks.open(r.tok_in.at[s], s)

    @pl.when(outer)
    def _():
        for s in range(seqs):
            cots.open(r.cot_in.at[s], s)

    send_emb = remote(r.emb_s, r.emb_r, r.s_e.at[0], r.s_e.at[1], dp=other)
    send_emb.start()
    send_w = [
        remote(src, dst, r.s_w.at[0, i], r.s_w.at[1, i], dp=other)
        for i, (src, dst) in enumerate(weights)
    ]
    for cp in send_w[:3]:
        cp.start()

    send_emb.wait()
    emb4 = own_half + r.emb_r[...]
    r.emb[pl.ds(c, 1)] = emb4[None]
    emb_low = emb4.astype(BF16)

    def mod_part(lo, hi, which, ready):
        ready.wait()
        r.mod_s[:, lo:hi] = mm(emb_low, r.wm[:, lo:hi])
        cp = remote(
            r.mod_s.at[:, lo:hi], r.mod_r.at[:, lo:hi], r.s_m.at[0, which], r.s_m.at[1, which], dp=other
        )
        cp.start()
        return cp

    def mod_take(lo, hi, cp):
        cp.wait()
        for s in range(seqs):
            r.mod[s : s + 1, lo:hi] = r.mod_s[s : s + 1, lo:hi] + r.mod_r[s + 2 : s + 3, lo:hi]

    def vec(slot_idx, s):
        lo = slot_idx * width
        return r.mod[s : s + 1, lo : lo + width]

    mod1 = mod_part(0, first_cols, 0, cp_wm1)
    for cp in send_w[3:]:
        cp.start()

    def send_ctx_emb(k):
        to = (c + k) % nc
        remote(r.emb.at[c], r.emb.at[c], r.s_ec.at[0, to], r.s_ec.at[1, c], ctx=to).start()

    each(nc, send_ctx_emb, 1)

    place = (c * block + lanes_of((block, LANES), 0)).astype(F32)
    pair_of = (lanes_of((block, LANES)) % (HEAD_DIM // 2)).astype(F32)
    turn = place * jnp.exp(pair_of * (-2.0 * math.log(10000.0) / HEAD_DIM))
    low_lane = lanes_of((block, LANES)) % HEAD_DIM < HEAD_DIM // 2
    r.cosine[...] = jnp.cos(turn)
    r.sine[...] = jnp.where(low_lane, -jnp.sin(turn), jnp.sin(turn))

    def swap(x):
        low = lanes_of(x.shape) % HEAD_DIM < HEAD_DIM // 2
        return jnp.where(
            low,
            pltpu.roll(x, LANES - HEAD_DIM // 2, 1),
            pltpu.roll(x, HEAD_DIM // 2, 1),
        )

    for i in range(3):
        cp_w[i].wait()
        send_w[i].wait_recv()
    mod_take(0, first_cols, mod1)

    def make_qkv(s, idx, i):
        at = span(idx)
        unit, _ = norm_parts(r.tok[s, at, :].astype(F32))
        low = (unit * (1.0 + vec(1, s)) + vec(0, s)).astype(BF16)
        r.nrm[s, at, :] = low
        cos1, sin1 = r.cosine[at, :], r.sine[at, :]
        q_pre = mm(low, r.wqt[...], NT)
        kv_pre = mm(low, r.wkvt[...], NT)
        for j in range(WIN // LANES):
            x = q_pre[:, j * LANES : (j + 1) * LANES]
            x = (x * cos1 + swap(x) * sin1) * (HEAD_DIM ** -0.5)
            r.q[s, at, j * LANES : (j + 1) * LANES] = x.astype(BF16)
        for j in range(z.kvw // LANES):
            x = kv_pre[:, j * LANES : (j + 1) * LANES]
            keys = min(max(hw - j * LANES, 0), LANES)
            if keys > 0:
                turned = x * cos1 + swap(x) * sin1
                x = turned if keys == LANES else jnp.where(lanes_of(x.shape) < keys, turned, x)
            r.kv[c, s, at, j * LANES : (j + 1) * LANES] = x.astype(BF16)

        def send_kv(to):
            mine = r.kv.at[c, s, at, :]
            remote(mine, mine, r.s_kv.at[to, s, idx], r.r_kv.at[c, s, idx], ctx=to).start()

        each(nc, send_kv, c + 1)

    cp_tok.wait()
    for s in range(seqs):
        make_qkv(s, t, 0)
    mod2 = mod_part(first_cols, z.mod, 1, cp_wm2)
    for s in range(seqs):
        toks.relay(s)
        toks.collect(s, make_qkv)

    @pl.when(inner)
    def _():
        for s in range(seqs):
            cots.open(r.cot_in.at[s], s)

    cp_cot.wait()
    mod_take(first_cols, z.mod, mod2)
    for i in range(3, 6):
        cp_w[i].wait()
        send_w[i].wait_recv()

    eye = (lanes_of((WIN, WIN), 0) == lanes_of((WIN, WIN))).astype(BF16)

    def head_of(x, h, off=0):
        lane = lanes_of(x.shape)
        lo = off + h * HEAD_DIM
        return jnp.where((lane >= lo) & (lane < lo + HEAD_DIM), x, jnp.zeros_like(x))

    def attend_seq(s):
        r.stat[0] = jnp.full((8, block), NEG, F32)
        r.stat[1] = jnp.zeros((8, block), F32)
        r.acc[...] = jnp.zeros((hw, block), F32)
        q = r.q[s]

        def one_block(back):
            j = c - back

            @pl.when(back > 0)
            def _():
                def take(idx):
                    there = r.kv.at[j, s, span(idx), :]
                    remote(
                        there, there, r.s_kv.at[j, s, idx], r.r_kv.at[j, s, idx], ctx=j
                    ).wait_recv()

                each(nt, take)

            keys = r.kv[j, s, :, 0:WIN]
            r.vt[...] = mm(eye, r.kv[j, s, :, z.vlo : z.vlo + WIN], NT).astype(BF16)
            for h in range(z.heads):
                scores = mm(keys, head_of(q, h), NT)
                old = r.stat[0, h : h + 1, :]
                top = jnp.maximum(old, jnp.max(scores, axis=0, keepdims=True))
                prob = jnp.exp(scores - top)
                fade = jnp.exp(old - top)
                r.stat[0, h : h + 1, :] = top
                r.stat[1, h : h + 1, :] = r.stat[1, h : h + 1, :] * fade + jnp.sum(
                    prob, axis=0, keepdims=True
                )
                lo = h * HEAD_DIM
                vt = r.vt[z.voff + lo : z.voff + lo + HEAD_DIM, :]
                r.acc[lo : lo + HEAD_DIM, :] = r.acc[lo : lo + HEAD_DIM, :] * fade + mm(
                    vt, prob.astype(BF16)
                )

        each(c + 1, one_block)
        for h in range(z.heads):
            lo = h * HEAD_DIM
            denom = r.stat[1, h : h + 1, :]
            r.lse[s, h : h + 1, :] = r.stat[0, h : h + 1, :] + jnp.log(denom)
            r.att[s, lo : lo + HEAD_DIM, :] = r.acc[lo : lo + HEAD_DIM, :] / denom
        low = jnp.transpose(r.att[s]).astype(BF16)
        r.attl[s, :, 0:hw] = low
        r.attl[s, :, hw:WIN] = jnp.zeros((block, WIN - hw), BF16)
        r.br[s] = mm(low, r.wot[z.voff : z.voff + hw, :]).astype(BF16)
        brs.push_all(s)

    each(seqs, attend_seq)
    for s in range(seqs):
        cots.relay(s)
    for s in range(seqs):
        brs.join(s)

    for s in range(seqs):
        branch = brs.total(s)
        r.branch[s] = branch
        middle = r.tok[s, span(t), :].astype(F32) + vec(2, s) * branch
        r.middle[s] = middle
        unit, _ = norm_parts(middle)
        r.n2[s, span(t), :] = (unit * (1.0 + vec(4, s)) + vec(3, s)).astype(BF16)
        n2s.open(piece(r.n2, s, t), s)

    def feed(s, idx, i):
        at = span(idx)
        hid = mm(r.n2[s, at, :], r.wu[...])
        square = hid * hid
        tanh = jnp.tanh(GELU_C * (hid + GELU_A * (hid * square)))
        r.act[s, at, :] = (0.5 * hid * (1.0 + tanh)).astype(BF16)
        slope = 0.5 * (1.0 + tanh) + 0.5 * hid * (1.0 - tanh * tanh) * (
            GELU_C * (1.0 + 3.0 * GELU_A * square)
        )
        low = (vec(5, s) * r.cot[s, at, :].astype(F32)).astype(BF16)
        r.mgrad[s, at, :] = low
        hgrad = (slope * mm(low, r.wd[...])).astype(BF16)
        r.hgrad[s, at, :] = hgrad
        r.g2[s, at, :] = mm(hgrad, r.wu[...], NT).astype(BF16)
        g2s.push(s, idx, i)

    for s in range(seqs):
        feed(s, t, 0)
    for s in range(seqs):
        cots.collect(s, None)
        n2s.relay(s)
        n2s.collect(s, feed)
    g2s.join(0)

    class Reduction:
        def __init__(self, got, mine, theirs, buf, total, sems, sems_all):
            self.got, self.mine, self.theirs, self.buf, self.total = got, mine, theirs, buf, total
            self.sems, self.sems_all = sems, sems_all
            self.chunk = buf.shape[1]
            self.owners = mine.shape[0] // self.chunk

        def rows(self, o):
            return pl.ds(pl.multiple_of(o * self.chunk, 16), self.chunk)

        def part(self, o):
            return remote(
                self.mine.at[self.rows(o), :],
                self.buf.at[c],
                self.sems.at[0, o],
                self.sems.at[1, c],
                ctx=o,
            )

        def share(self, owner, to):
            here = self.total.at[self.rows(owner), :]
            return remote(here, here, self.sems_all.at[0, to], self.sems_all.at[1, owner], ctx=to)

        def to_owners(self, body):
            def one(k):
                o = (c + k) % nc

                @pl.when(o < self.owners)
                def _():
                    body(o)

            each(nc, one, 1)

        def as_owner(self, body):
            @pl.when(c < self.owners)
            def _():
                body()

        def send(self):
            self.got.wait()
            self.mine[...] = (self.mine[...].astype(F32) + self.theirs[...].astype(F32)).astype(
                BF16
            )
            self.to_owners(lambda o: self.part(o).start())

        def sum(self):
            def body():
                def add(k, acc):
                    fr = (c + k) % nc
                    there = self.buf.at[fr]
                    remote(
                        there, there, self.sems.at[0, fr], self.sems.at[1, fr], ctx=fr
                    ).wait_recv()
                    return acc + self.buf[fr].astype(F32)

                acc = self.mine[self.rows(c), :].astype(F32)
                if nc <= 4:
                    for k in range(1, nc):
                        acc = add(k, acc)
                else:
                    acc = lax.fori_loop(1, nc, add, acc)
                self.total[self.rows(c), :] = acc.astype(BF16)
                each(nc, lambda k: self.share(c, (c + k) % nc).start(), 1)

            self.as_owner(body)

        def take(self):
            def one(o):
                self.share(o, o).wait_recv()
                self.part(o).wait_send()

            self.to_owners(one)
            self.as_owner(
                lambda: each(nc, lambda k: self.share(c, (c + k) % nc).wait_send(), 1)
            )

    def pair_grads(lhs, rhs, mine, sent, lo, hi):
        right = flat(rhs[...])
        for which, dst in ((other, sent), (d, mine)):
            cols = pl.ds(pl.multiple_of(which * half, half), half)
            left = flat(lhs[:, :, cols])
            dst[:, lo:hi] = mm(left, right, TN).astype(BF16)

    pair_grads(r.mgrad, r.act, r.ga_o, r.ga_s, z.ff, 2 * z.ff)
    pair_grads(r.n2, r.hgrad, r.ga_o, r.ga_s, 0, z.ff)
    send_ga = remote(r.ga_s, r.ga_r, r.s_ga.at[0], r.s_ga.at[1], dp=other)
    send_ga.start()
    g2s.join(1)
    for s in range(seqs):
        r.ml[s] = mm(r.act[s], r.wd[...], NT).astype(BF16)

    red_a = Reduction(send_ga, r.ga_o, r.ga_r, r.ga_c, r.ga_t, r.s_gac, r.s_gag)
    red_a.send()

    r.msum[...] = jnp.zeros((8, z.mod), F32)

    def keep_sum(slot_idx, s, value):
        lo = slot_idx * width
        r.msum[s : s + 1, lo : lo + width] = jnp.sum(value, axis=0, keepdims=True)

    for s in range(seqs):
        grad2 = g2s.total(s)
        unit, rstd = norm_parts(r.middle[s])
        mid_grad = r.cot[s, span(t), :].astype(F32) + norm_back(grad2, unit, rstd, vec(4, s))
        r.midg[s] = mid_grad
        r.bg[s, span(t), :] = (vec(2, s) * mid_grad).astype(BF16)
        bgs.open(piece(r.bg, s, t), s)
        keep_sum(3, s, grad2)
        keep_sum(4, s, grad2 * unit)
        keep_sum(2, s, mid_grad * r.branch[s])

    def out_grads(s, idx, i):
        at = span(idx)
        r.do[s, at, :] = mm(r.bg[s, at, :], r.wot[...], NT).astype(BF16)

    for s in range(seqs):
        out_grads(s, t, 0)
    bgs.relay(0)
    bgs.collect(0, out_grads)

    bgs.relay(1)

    def back_seq(s):
        do = r.do[s]
        r.dot[...] = mm(eye, do, NT).astype(BF16)
        for h in range(z.heads):
            lo = h * HEAD_DIM
            r.delta[s, h : h + 1, :] = jnp.sum(
                r.dot[z.voff + lo : z.voff + lo + HEAD_DIM, :].astype(F32)
                * r.att[s, lo : lo + HEAD_DIM, :],
                axis=0,
                keepdims=True,
            )
        r.dqt[...] = jnp.zeros((hw, block), F32)
        q = r.q[s]

        def one_block(j):
            keys = r.kv[j, s, :, 0:WIN]
            vals = r.kv[j, s, :, z.vlo : z.vlo + WIN]
            r.vt[...] = mm(eye, keys, NT).astype(BF16)
            dk = jnp.zeros((block, WIN), F32)
            dv = jnp.zeros((block, WIN), F32)
            for h in range(z.heads):
                lo = h * HEAD_DIM
                qh = head_of(q, h)
                doh = head_of(do, h, z.voff)
                prob = jnp.exp(mm(keys, qh, NT) - r.lse[s, h : h + 1, :])
                dprob = mm(vals, doh, NT)
                dsc = (prob * (dprob - r.delta[s, h : h + 1, :])).astype(BF16)
                dv = dv + mm(prob.astype(BF16), doh)
                dk = dk + mm(dsc, qh)
                r.dqt[lo : lo + HEAD_DIM, :] += mm(r.vt[lo : lo + HEAD_DIM, :], dsc)
            over = WIN - z.vlo
            pieces = (
                (0, z.vlo, dk[:, 0 : z.vlo]),
                (z.vlo, WIN, dk[:, z.vlo : WIN] + dv[:, 0:over]),
                (WIN, z.kvw, dv[:, over:WIN]),
            )

            @pl.when(j < c)
            def _():
                for lo, hi, piece in pieces:
                    r.kv[j, s, :, lo:hi] = piece.astype(BF16)
                remote(
                    r.kv.at[j, s], r.dkv_r.at[c, s], r.s_dk.at[j, s], r.r_dk.at[c, s], ctx=j
                ).start()

            @pl.when(j == c)
            def _():
                for lo, hi, piece in pieces:
                    r.dkv[s, :, lo:hi] = piece

        each(c + 1, one_block)
        r.dq[s, :, 0:hw] = jnp.transpose(r.dqt[...]) * (HEAD_DIM ** -0.5)
        r.dq[s, :, hw:WIN] = jnp.zeros((block, WIN - hw), F32)

    def kv_sent(j):
        for s in range(seqs):
            each(
                nt,
                lambda idx: remote(
                    r.kv.at[c, s, span(idx), :],
                    r.kv.at[c, s, span(idx), :],
                    r.s_kv.at[j, s, idx],
                    r.r_kv.at[c, s, idx],
                    ctx=j,
                ).wait_send(),
            )

    each(nc, kv_sent, c + 1)

    def back_step(s):
        @pl.when(s == 1)
        def _():
            bgs.collect(1, out_grads)
            for i in range(seqs):
                mls.push_all(i)

        back_seq(s)

    each(seqs, back_step)
    red_a.sum()

    for s in range(seqs):
        g2s.close(s)
    cos1, sin1 = r.cosine[...], r.sine[...]
    for s in range(seqs):

        def add_dkv(j):
            there = r.dkv_r.at[j, s]
            remote(there, there, r.s_dk.at[j, s], r.r_dk.at[j, s], ctx=j).wait_recv()
            r.dkv[s] += r.dkv_r[j, s].astype(F32)

        each(nc, add_dkv, c + 1)
        for j in range(WIN // LANES):
            x = r.dq[s, :, j * LANES : (j + 1) * LANES]
            r.qb[s, :, j * LANES : (j + 1) * LANES] = (x * cos1 - swap(x) * sin1).astype(BF16)
        for j in range(z.kvw // LANES):
            x = r.dkv[s, :, j * LANES : (j + 1) * LANES]
            keys = min(max(hw - j * LANES, 0), LANES)
            if keys > 0:
                turned = x * cos1 - swap(x) * sin1
                x = turned if keys == LANES else jnp.where(lanes_of(x.shape) < keys, turned, x)
            r.kvb[s, :, j * LANES : (j + 1) * LANES] = x.astype(BF16)
        r.g2[s] = (mm(r.qb[s], r.wqt[...]) + mm(r.kvb[s], r.wkvt[...])).astype(BF16)
        n1s.push_all(s)

    for which, dst in ((other, r.gb_s), (d, r.gb_o)):
        cols = pl.ds(pl.multiple_of(which * half, LANES), half)
        right = flat(r.nrm[:, :, cols])
        dst[0:hw, :] = mm(flat(r.qb[:, :, 0:hw]), right, TN).astype(BF16)
        dst[hw : 3 * hw, :] = mm(flat(r.kvb[...]), right, TN).astype(BF16)
        right = flat(r.bg[:, :, cols])
        dst[3 * hw : 4 * hw, :] = mm(flat(r.attl[:, :, 0:hw]), right, TN).astype(BF16)
    send_gb = remote(r.gb_s, r.gb_r, r.s_gb.at[0], r.s_gb.at[1], dp=other)
    send_gb.start()
    red_b = Reduction(send_gb, r.gb_o, r.gb_r, r.gb_c, r.gb_t, r.s_gbc, r.s_gbg)
    n1s.join(0)
    red_b.send()
    n1s.join(1)

    for s in range(seqs):
        mls.join(s)
    outs = []

    def store(src, dst):
        cp = pltpu.make_async_copy(src, dst, r.s_loc.at[len(local) + len(outs)])
        cp.start()
        outs.append(cp)

    for s in range(seqs):
        grad1 = n1s.total(s)
        unit, rstd = norm_parts(r.tok[s, span(t), :].astype(F32))
        keep_sum(0, s, grad1)
        keep_sum(1, s, grad1 * unit)
        r.gtok[s] = r.midg[s] + norm_back(grad1, unit, rstd, vec(1, s))
        if s == 0:
            red_b.sum()
        mlp = mls.total(s)
        r.res[s] = (r.middle[s] + vec(5, s) * mlp).astype(BF16)
        keep_sum(5, s, r.cot[s, span(t), :].astype(F32) * mlp)
    def mcol(idx):
        return pl.ds(pl.multiple_of(idx * z.mcols, LANES), z.mcols)

    for k in range(1, nt):
        to = (t + k) % nt
        remote(
            r.msum.at[:, mcol(to)], r.mt_r.at[t], r.s_mt.at[0, to], r.s_mt.at[1, t], tp=to
        ).start()
    store(r.res, r.res_out)
    store(r.gtok, r.gtok_out)
    total = r.msum[:, mcol(t)]
    for k in range(1, nt):
        fr = (t + k) % nt
        there = r.mt_r.at[fr]
        remote(there, there, r.s_mt.at[0, fr], r.s_mt.at[1, fr], tp=fr).wait_recv()
        total = total + r.mt_r[fr]
    r.md_s[...] = total
    send_md = remote(r.md_s, r.md_r, r.s_md.at[0], r.s_md.at[1], dp=other)
    send_md.start()
    send_md.wait()
    r.mg[pl.ds(c, 1), 0:2, :] = total[None, 0:2, :]
    r.mg[pl.ds(c, 1), 2:4, :] = r.md_r[0:2, :][None]
    r.mg[pl.ds(c, 1), 4:8, :] = jnp.zeros((1, 4, z.mcols), F32)

    def send_mg(k):
        to = (c + k) % nc
        remote(r.mg.at[c], r.mg.at[c], r.s_mc.at[0, to], r.s_mc.at[1, c], ctx=to).start()

    each(nc, send_mg, 1)
    red_a.take()
    store(r.ga_t, r.ga_out)
    red_b.take()
    store(r.gb_t, r.gb_out)

    def take_small(k):
        fr = (c + k) % nc
        for buf, sems in ((r.mg, r.s_mc), (r.emb, r.s_ec)):
            remote(buf.at[fr], buf.at[fr], sems.at[0, fr], sems.at[1, fr], ctx=fr).wait_recv()
            remote(buf.at[c], buf.at[c], sems.at[0, fr], sems.at[1, c], ctx=fr).wait_send()

    each(nc, take_small, 1)
    store(r.mg, r.mg_out)
    store(r.emb, r.emb_out)

    for cp in send_w:
        cp.wait_send()
    for s in range(seqs):
        for group in (toks, cots, n2s, bgs, brs, mls, n1s):
            group.close(s)
    for k in range(1, nt):
        to = (t + k) % nt
        remote(
            r.msum.at[:, mcol(to)], r.mt_r.at[t], r.s_mt.at[0, to], r.s_mt.at[1, t], tp=to
        ).wait_send()

    def dkv_sent(j):
        for s in range(seqs):
            remote(
                r.kv.at[j, s], r.dkv_r.at[c, s], r.s_dk.at[j, s], r.r_dk.at[c, s], ctx=j
            ).wait_send()

    each(c, dkv_sent)
    for cp in outs:
        cp.wait()


def finish_kernel(z, ga, gb, emb, mg, res, gtok, *refs):
    outs, stage, sems = refs[:9], refs[9:18], refs[18]
    hw = z.hw
    copies = []

    def put(i, value):
        stage[i][...] = value
        cp = pltpu.make_async_copy(stage[i], outs[i], sems.at[i])
        cp.start()
        copies.append(cp)

    put(6, ga[:, 0 : z.ff].astype(F32))
    put(7, ga[:, z.ff : 2 * z.ff].astype(F32))
    for i in range(4):
        put(2 + i, gb[i * hw : (i + 1) * hw, :].astype(F32))
    put(0, res[...])
    put(1, gtok[...])
    e = emb[...].reshape(z.nc * 8, z.half)
    m = mg[...].reshape(z.nc * 8, z.mcols)
    put(
        8,
        lax.dot_general(
            e, m, TN, precision=lax.Precision.HIGHEST, preferred_element_type=F32
        ),
    )
    for cp in copies:
        cp.wait()


IN_NAMES = (
    "tok_in",
    "ts_in",
    "wq_in",
    "wk_in",
    "wv_in",
    "wo_in",
    "wu_in",
    "wd_in",
    "wm_in",
    "cot_in",
)
OUT_NAMES = ("res_out", "gtok_out", "ga_out", "gb_out", "emb_out", "mg_out")


def solution(mesh):
    def shards(tokens, steps, wq, wk, wv, wo, wu, wd, wm, cot):
        wq, wk, wv, wo = wq.T, wk.T, wv.T, wo.T
        z = Dims(mesh, tokens.shape, wq.shape, wu.shape, wm.shape)
        table = scratch_table(z)
        names = list(IN_NAMES) + list(OUT_NAMES) + list(table)
        hbm = pl.BlockSpec(memory_space=pl.ANY)
        vmem = pl.BlockSpec(memory_space=pltpu.VMEM)
        smem = pl.BlockSpec(memory_space=pltpu.SMEM)
        own = (z.seqs, z.rows, z.width)
        shape = jax.ShapeDtypeStruct
        outs = pl.pallas_call(
            functools.partial(layer_kernel, z, names),
            out_shape=(
                shape(own, BF16),
                shape(own, F32),
                shape((z.half, z.wide), BF16),
                shape((z.heads_rows, z.half), BF16),
                shape((z.nc, 8, z.half), F32),
                shape((z.nc, 8, z.mcols), F32),
            ),
            in_specs=[hbm, smem] + [hbm] * 8,
            out_specs=[hbm] * 6,
            scratch_shapes=list(table.values()),
            compiler_params=pltpu.CompilerParams(
                collective_id=0, has_side_effects=True, vmem_limit_bytes=VMEM_BYTES
            ),
            name="layer",
        )(tokens, steps.T, wq, wk, wv, wo, wu, wd, wm, cot)
        res, gtok, ga, gb, emb, mg = outs
        shapes = (
            (own, BF16),
            (own, F32),
            ((z.hw, z.half), F32),
            ((z.hw, z.half), F32),
            ((z.hw, z.half), F32),
            ((z.hw, z.half), F32),
            ((z.half, z.ff), F32),
            ((z.half, z.ff), F32),
            ((z.half, z.mcols), F32),
        )
        done = pl.pallas_call(
            functools.partial(finish_kernel, z),
            out_shape=tuple(shape(*o) for o in shapes),
            in_specs=[vmem] * 6,
            out_specs=[hbm] * 9,
            scratch_shapes=[pltpu.VMEM(*o) for o in shapes] + [pltpu.SemaphoreType.DMA((9,))],
            compiler_params=pltpu.CompilerParams(vmem_limit_bytes=VMEM_BYTES),
            name="finish",
        )(ga, gb, emb, mg, res, gtok)
        return done[:2] + tuple(g.T for g in done[2:6]) + done[6:]

    rows = P("dp", ("ctx", "tp"), None)
    cols = P("dp", "tp")
    return jax.shard_map(
        shards,
        mesh=mesh,
        in_specs=(rows, P("dp", "ctx")) + (cols,) * 6 + (P("dp", None), rows),
        out_specs=(rows, rows) + (cols,) * 7,
        check_vma=False,
    )
```

```python
import functools
import math

import jax
import jax.numpy as jnp
from jax import lax
from jax.experimental import pallas as pl
from jax.experimental.pallas import tpu as pltpu
from jax.sharding import PartitionSpec as P

MESH = pl.DeviceIdType.MESH
HEAD_DIM = 64
WIN = 256
LANES = 128
EPS = 1e-06
NEG = -1e30
GELU_C = 0.7978845608028654
GELU_A = 0.044715
F32 = jnp.float32
BF16 = jnp.bfloat16
VMEM_BYTES = 62 * 1024 * 1024

NN = (((1,), (0,)), ((), ()))
NT = (((1,), (1,)), ((), ()))
TN = (((0,), (0,)), ((), ()))


def mm(a, b, dims=NN):
    return lax.dot_general(a, b, dims, preferred_element_type=F32)


def norm_parts(x):
    center = x - jnp.mean(x, axis=-1, keepdims=True)
    rstd = lax.rsqrt(jnp.mean(center * center, axis=-1, keepdims=True) + EPS)
    return center * rstd, rstd


def norm_back(grad, unit, rstd, scale):
    dn = grad * (1.0 + scale)
    return rstd * (
        dn
        - jnp.mean(dn, axis=-1, keepdims=True)
        - unit * jnp.mean(dn * unit, axis=-1, keepdims=True)
    )


def remote(src, dst, send, recv, **dev):
    return pltpu.make_async_remote_copy(
        src_ref=src, dst_ref=dst, send_sem=send, recv_sem=recv, device_id=dev, device_id_type=MESH
    )


def chunk_rows(count, devices):
    return 16 * -(-(count // 16) // devices)


class Dims:
    def __init__(self, mesh, tokens, query, up, mod):
        self.nc = mesh.shape["ctx"]
        self.nt = mesh.shape["tp"]
        self.seqs, self.rows, self.width = tokens
        self.block = self.rows * self.nt
        self.hw, self.half = query
        self.heads = self.hw // HEAD_DIM
        self.ff = up[1]
        self.mod = mod[1]
        self.kvw = 2 * self.hw
        self.vlo = self.kvw - WIN
        self.voff = self.hw - self.vlo
        self.wide = 2 * self.ff
        self.heads_rows = 4 * self.hw
        self.mcols = self.mod // self.nt


def scratch_table(z):
    vm = lambda shape, dtype=BF16: pltpu.VMEM(shape, dtype)
    sem = lambda *shape: pltpu.SemaphoreType.DMA(shape)
    full = (z.seqs, z.block, z.width)
    own = (z.seqs, z.rows, z.width)
    pair = (z.seqs, 2, z.rows, z.width)
    return dict(
        tok=vm(full),
        cot=vm(full),
        wqt=vm((WIN, z.width)),
        wkvt=vm((z.kvw, z.width)),
        wot=vm((WIN, z.width)),
        wu=vm((z.width, z.ff)),
        wd=vm((z.width, z.ff)),
        wm=vm((z.half, z.mod)),
        emb_s=vm((8, z.half), F32),
        emb_r=vm((8, z.half), F32),
        emb=vm((z.nc, 8, z.half), F32),
        mod_s=vm((8, z.mod), F32),
        mod_r=vm((8, z.mod), F32),
        mod=vm((8, z.mod), F32),
        cosine=vm((z.block, LANES), F32),
        sine=vm((z.block, LANES), F32),
        nrm=vm(full),
        qd=vm((z.seqs, z.block, z.kvw)),
        kv=vm((z.nc, z.seqs, z.block, z.kvw)),
        vt=vm((WIN, z.block)),
        stat=vm((2, 8, z.block), F32),
        acc=vm((z.hw, z.block), F32),
        att=vm((z.seqs, z.hw, z.block), F32),
        attl=vm((z.seqs, z.block, WIN)),
        lse=vm((z.nc, z.seqs, 8, z.block), F32),
        delta=vm((z.nc, z.seqs, 8, z.block), F32),
        br=vm(full),
        br_m=vm(pair),
        br_r=vm(pair),
        branch=vm(own, F32),
        middle=vm(own, F32),
        n2=vm(full),
        act=vm((z.seqs, z.block, z.ff)),
        hgrad=vm((z.seqs, z.block, z.ff)),
        mgrad=vm(full),
        g2=vm(full),
        g2_m=vm(pair),
        g2_r=vm(pair),
        ml=vm(full),
        ml_m=vm(pair),
        ml_r=vm(pair),
        midg=vm(own, F32),
        bg=vm(full),
        seen=vm((z.block, z.kvw)),
        dot=vm((WIN, z.block)),
        dqt=vm((z.seqs, z.hw, z.block), F32),
        dq_s=vm((z.nc, z.seqs, z.hw, z.block)),
        dq_r=vm((z.nc, z.seqs, z.hw, z.block)),
        dq=vm((z.seqs, z.block, WIN), F32),
        dkv=vm((z.seqs, z.block, z.kvw), F32),
        qb=vm((z.seqs, z.block, WIN)),
        kvb=vm((z.seqs, z.block, z.kvw)),
        n1_m=vm(pair),
        n1_r=vm(pair),
        ga_s=vm((z.half, z.wide)),
        ga_o=vm((z.half, z.wide)),
        ga_r=vm((z.half, z.wide)),
        ga_c=vm((z.nc, chunk_rows(z.half, z.nc), z.wide)),
        ga_t=vm((z.half, z.wide)),
        gb_s=vm((z.heads_rows, z.half)),
        gb_o=vm((z.heads_rows, z.half)),
        gb_r=vm((z.heads_rows, z.half)),
        gb_c=vm((z.nc, chunk_rows(z.heads_rows, z.nc), z.half)),
        gb_t=vm((z.heads_rows, z.half)),
        msum=vm((8, z.mod), F32),
        mt_r=vm((z.nt, 8, z.mcols), F32),
        md_s=vm((8, z.mcols), F32),
        md_r=vm((8, z.mcols), F32),
        mg=vm((z.nc, 8, z.mcols), F32),
        res=vm(own),
        gtok=vm(own, F32),
        s_loc=sem(16),
        s_w=sem(2, 6),
        s_e=sem(2),
        s_ec=sem(2, z.nc),
        s_m=sem(2, 2),
        s_tok=sem(z.seqs, 4),
        r_tok=sem(z.seqs, z.nt),
        s_cot=sem(z.seqs, 4),
        r_cot=sem(z.seqs, z.nt),
        s_kv=sem(z.nc, z.seqs, z.nt),
        r_kv=sem(z.nc, z.seqs, z.nt),
        s_br=sem(z.seqs, 4),
        m_br=sem(z.seqs, 2),
        r_br=sem(z.seqs, 2),
        s_n2=sem(z.seqs, 4),
        r_n2=sem(z.seqs, z.nt),
        s_g2=sem(z.seqs, 4),
        m_g2=sem(z.seqs, 2),
        r_g2=sem(z.seqs, 2),
        s_ml=sem(z.seqs, 4),
        m_ml=sem(z.seqs, 2),
        r_ml=sem(z.seqs, 2),
        s_bg=sem(z.seqs, 4),
        r_bg=sem(z.seqs, z.nt),
        s_q=sem(z.nc, z.seqs),
        r_q=sem(z.nc, z.seqs),
        s_do=sem(z.nc, z.seqs, z.nt),
        r_do=sem(z.nc, z.seqs, z.nt),
        s_st=sem(2, z.nc, z.seqs),
        r_st=sem(2, z.nc, z.seqs),
        s_dq=sem(z.nc, z.seqs),
        r_dq=sem(z.nc, z.seqs),
        s_n1=sem(z.seqs, 4),
        m_n1=sem(z.seqs, 2),
        r_n1=sem(z.seqs, 2),
        s_ga=sem(2),
        s_gac=sem(2, max(z.nc, 12)),
        s_gag=sem(2, max(z.nc, 12)),
        s_gb=sem(2),
        s_gbc=sem(2, max(z.nc, 12)),
        s_gbg=sem(2, max(z.nc, 12)),
        s_mt=sem(2, z.nt),
        s_md=sem(2),
        s_mc=sem(2, z.nc),
    )


class Box:
    pass


def layer_kernel(z, names, *refs):
    r = Box()
    for name, ref in zip(names, refs):
        setattr(r, name, ref)
    d, c, t = lax.axis_index("dp"), lax.axis_index("ctx"), lax.axis_index("tp")
    other = 1 - d
    nt, nc, rows, block, width, hw = z.nt, z.nc, z.rows, z.block, z.width, z.hw
    seqs, half = z.seqs, z.half

    def each(count, body, first=0):
        def step(i, carry):
            body(i)
            return carry

        lax.fori_loop(first, count, step, 0)

    def span(idx):
        return pl.ds(pl.multiple_of(idx * rows, rows), rows)

    def slot(ref, idx):
        return ref.at[:, span(idx), :]

    def piece(ref, s, idx):
        return ref.at[s, span(idx), :]

    def flat(x):
        return x.reshape(x.shape[0] * x.shape[1], x.shape[2])

    def lanes_of(shape, axis=1):
        return lax.broadcasted_iota(jnp.int32, shape, axis)

    local = []

    def fetch(src, dst):
        cp = pltpu.make_async_copy(src, dst, r.s_loc.at[len(local)])
        cp.start()
        local.append(cp)
        return cp

    my_half = pl.ds(pl.multiple_of(d * half, LANES), half)
    weights = [
        (r.wq_in, r.wqt.at[0:hw, my_half]),
        (r.wk_in, r.wkvt.at[0:hw, my_half]),
        (r.wv_in, r.wkvt.at[hw : z.kvw, my_half]),
        (r.wo_in, r.wot.at[z.voff : z.voff + hw, my_half]),
        (r.wu_in, r.wu.at[my_half, :]),
        (r.wd_in, r.wd.at[my_half, :]),
    ]
    first_cols = 2 * width
    cp_tok = fetch(r.tok_in, slot(r.tok, t))
    cp_wm1 = fetch(r.wm_in.at[:, 0:first_cols], r.wm.at[:, 0:first_cols])
    cp_w = [fetch(src, dst) for src, dst in weights]
    cp_wm2 = fetch(r.wm_in.at[:, first_cols : z.mod], r.wm.at[:, first_cols : z.mod])
    cp_cot = fetch(r.cot_in, slot(r.cot, t))

    r.wqt[hw:WIN, :] = jnp.zeros((WIN - hw, width), BF16)
    r.wot[0 : z.voff, :] = jnp.zeros((z.voff, width), BF16)

    bar = pltpu.get_barrier_semaphore()
    pl.semaphore_signal(bar, inc=1, device_id={"dp": other}, device_id_type=MESH)
    for k in range(1, nt):
        pl.semaphore_signal(bar, inc=1, device_id={"tp": (t + k) % nt}, device_id_type=MESH)

    def greet(k):
        pl.semaphore_signal(bar, inc=1, device_id={"ctx": (c + k) % nc}, device_id_type=MESH)

    each(nc, greet, 1)

    row8 = lanes_of((8, half), 0)
    step_of = jnp.where(
        row8 % 2 == 0, r.ts_in[0, 0].astype(F32), r.ts_in[0, 1].astype(F32)
    )
    angle = step_of * jnp.exp(
        lanes_of((8, half)).astype(F32) * (-math.log(10000.0) / half)
    )
    sin_e, cos_e = jnp.sin(angle), jnp.cos(angle)

    def silu_low(v):
        return (v / (1.0 + jnp.exp(-v))).astype(BF16).astype(F32)

    sin_e, cos_e = silu_low(sin_e), silu_low(cos_e)
    first = d == 0
    own_half = jnp.where(row8 < 2, jnp.where(first, sin_e, cos_e), 0.0)
    r.emb_s[...] = jnp.where(
        (row8 >= 2) & (row8 < 4), jnp.where(first, cos_e, sin_e), 0.0
    )
    pl.semaphore_wait(bar, 1 + (nt - 1) + (nc - 1))

    side = t // 2
    mate = t + 1 - 2 * (t % 2)
    cross = 2 - side
    outer = t % 3 == 0
    inner = t % 3 != 0

    def peer(i):
        far = i // 2
        return (1 - far) * (t + i * (1 - 2 * (t % 2))) + far * ((1 - side) * i + side * (3 - i))

    class Gather:
        def __init__(self, buf, send, recv):
            self.buf, self.sems, self.recv = buf, send, recv

        def copy(self, src, s, idx, k, to):
            return remote(
                src, piece(self.buf, s, idx), self.sems.at[s, k], self.recv.at[s, idx], tp=to
            )

        def open(self, src, s):
            self.copy(src, s, t, 1, cross).start()
            self.copy(src, s, t, 0, mate).start()

        def wait(self, s, idx):
            self.copy(piece(self.buf, s, idx), s, idx, 0, mate).wait_recv()

        def relay(self, s):
            @pl.when(inner)
            def _():
                def one(i):
                    idx = peer(i)
                    self.wait(s, idx)
                    self.copy(piece(self.buf, s, idx), s, idx, i, mate).start()

                each(4, one, 2)

        def collect(self, s, work):
            def one(i):
                idx = peer(i)

                @pl.when(outer | (i == 1))
                def _():
                    self.wait(s, idx)

                if work is not None:
                    work(s, idx, i)

            each(4, one, 1)

        def close(self, s):
            mine = piece(self.buf, s, t)
            self.copy(mine, s, t, 0, mate).wait_send()
            self.copy(mine, s, t, 1, cross).wait_send()

            @pl.when(inner)
            def _():
                each(4, lambda i: self.copy(mine, s, t, i, mate).wait_send(), 2)

    class Scatter:
        def __init__(self, part, merge, got, send, msem, gsem):
            self.part, self.merge, self.got = part, merge, got
            self.sems, self.msem, self.gsem = send, msem, gsem

        def to_got(self, s, idx, i, k):
            return remote(
                piece(self.part, s, idx),
                self.got.at[s, k],
                self.sems.at[s, i],
                self.gsem.at[s, k],
                tp=idx,
            )

        def to_merge(self, s, idx, i):
            return remote(
                piece(self.part, s, idx),
                self.merge.at[s, i - 2],
                self.sems.at[s, i],
                self.msem.at[s, i - 2],
                tp=mate,
            )

        def push(self, s, idx, i):
            @pl.when(i == 1)
            def _():
                self.to_got(s, idx, i, 0).start()

            @pl.when((i > 1) & outer)
            def _():
                self.to_merge(s, idx, i).start()

        def push_all(self, s):
            for i in (3, 2):
                self.push(s, peer(i), i)
            self.push(s, mate, 1)

        def join(self, s):
            @pl.when(inner)
            def _():
                def one(k):
                    i = 3 - k
                    idx = peer(i)
                    self.to_merge(s, idx, i).wait_recv()
                    at = span(idx)
                    self.part[s, at, :] = (
                        self.part[s, at, :].astype(F32) + self.merge[s, i - 2].astype(F32)
                    ).astype(BF16)
                    self.to_got(s, idx, i, 1).start()

                each(2, one)

        def total(self, s):
            for k in range(2):
                self.to_got(s, mate, 1, k).wait_recv()
            return (
                self.part[s, span(t), :].astype(F32)
                + self.got[s, 0].astype(F32)
                + self.got[s, 1].astype(F32)
            )

        def close(self, s):
            each(4, lambda i: self.to_got(s, mate, i, 0).wait_send(), 1)

    toks = Gather(r.tok, r.s_tok, r.r_tok)
    cots = Gather(r.cot, r.s_cot, r.r_cot)
    n2s = Gather(r.n2, r.s_n2, r.r_n2)
    bgs = Gather(r.bg, r.s_bg, r.r_bg)
    brs = Scatter(r.br, r.br_m, r.br_r, r.s_br, r.m_br, r.r_br)
    g2s = Scatter(r.g2, r.g2_m, r.g2_r, r.s_g2, r.m_g2, r.r_g2)
    mls = Scatter(r.ml, r.ml_m, r.ml_r, r.s_ml, r.m_ml, r.r_ml)
    n1s = Scatter(r.g2, r.n1_m, r.n1_r, r.s_n1, r.m_n1, r.r_n1)

    for s in range(seqs):
        toks.open(r.tok_in.at[s], s)

    @pl.when(outer)
    def _():
        for s in range(seqs):
            cots.open(r.cot_in.at[s], s)

    send_emb = remote(r.emb_s, r.emb_r, r.s_e.at[0], r.s_e.at[1], dp=other)
    send_emb.start()
    send_w = [
        remote(src, dst, r.s_w.at[0, i], r.s_w.at[1, i], dp=other)
        for i, (src, dst) in enumerate(weights)
    ]
    for cp in send_w[:3]:
        cp.start()

    send_emb.wait()
    emb4 = own_half + r.emb_r[...]
    r.emb[pl.ds(c, 1)] = emb4[None]
    emb_low = emb4.astype(BF16)

    def mod_part(lo, hi, which, ready):
        ready.wait()
        r.mod_s[:, lo:hi] = mm(emb_low, r.wm[:, lo:hi])
        cp = remote(
            r.mod_s.at[:, lo:hi], r.mod_r.at[:, lo:hi], r.s_m.at[0, which], r.s_m.at[1, which], dp=other
        )
        cp.start()
        return cp

    def mod_take(lo, hi, cp):
        cp.wait()
        for s in range(seqs):
            r.mod[s : s + 1, lo:hi] = r.mod_s[s : s + 1, lo:hi] + r.mod_r[s + 2 : s + 3, lo:hi]

    def vec(slot_idx, s):
        lo = slot_idx * width
        return r.mod[s : s + 1, lo : lo + width]

    mod1 = mod_part(0, first_cols, 0, cp_wm1)
    for cp in send_w[3:]:
        cp.start()

    def send_ctx_emb(k):
        to = (c + k) % nc
        remote(r.emb.at[c], r.emb.at[c], r.s_ec.at[0, to], r.s_ec.at[1, c], ctx=to).start()

    each(nc, send_ctx_emb, 1)

    place = (c * block + lanes_of((block, LANES), 0)).astype(F32)
    pair_of = (lanes_of((block, LANES)) % (HEAD_DIM // 2)).astype(F32)
    turn = place * jnp.exp(pair_of * (-2.0 * math.log(10000.0) / HEAD_DIM))
    low_lane = lanes_of((block, LANES)) % HEAD_DIM < HEAD_DIM // 2
    r.cosine[...] = jnp.cos(turn)
    r.sine[...] = jnp.where(low_lane, -jnp.sin(turn), jnp.sin(turn))

    def swap(x):
        low = lanes_of(x.shape) % HEAD_DIM < HEAD_DIM // 2
        return jnp.where(
            low,
            pltpu.roll(x, LANES - HEAD_DIM // 2, 1),
            pltpu.roll(x, HEAD_DIM // 2, 1),
        )

    for i in range(3):
        cp_w[i].wait()
        send_w[i].wait_recv()
    mod_take(0, first_cols, mod1)

    def make_qkv(s, idx, i):
        at = span(idx)
        unit, _ = norm_parts(r.tok[s, at, :].astype(F32))
        low = (unit * (1.0 + vec(1, s)) + vec(0, s)).astype(BF16)
        r.nrm[s, at, :] = low
        cos1, sin1 = r.cosine[at, :], r.sine[at, :]
        q_pre = mm(low, r.wqt[...], NT)
        kv_pre = mm(low, r.wkvt[...], NT)
        for j in range(WIN // LANES):
            x = q_pre[:, j * LANES : (j + 1) * LANES]
            x = (x * cos1 + swap(x) * sin1) * (HEAD_DIM ** -0.5)
            r.qd[s, at, j * LANES : (j + 1) * LANES] = x.astype(BF16)
        for j in range(z.kvw // LANES):
            x = kv_pre[:, j * LANES : (j + 1) * LANES]
            keys = min(max(hw - j * LANES, 0), LANES)
            if keys > 0:
                turned = x * cos1 + swap(x) * sin1
                x = turned if keys == LANES else jnp.where(lanes_of(x.shape) < keys, turned, x)
            r.kv[c, s, at, j * LANES : (j + 1) * LANES] = x.astype(BF16)

        def send_kv(to):
            mine = r.kv.at[c, s, at, :]
            remote(mine, mine, r.s_kv.at[to, s, idx], r.r_kv.at[c, s, idx], ctx=to).start()

        each(nc, send_kv, c + 1)

    cp_tok.wait()
    for s in range(seqs):
        make_qkv(s, t, 0)
    mod2 = mod_part(first_cols, z.mod, 1, cp_wm2)
    for s in range(seqs):
        toks.relay(s)
        toks.collect(s, make_qkv)

    @pl.when(inner)
    def _():
        for s in range(seqs):
            cots.open(r.cot_in.at[s], s)

    cp_cot.wait()
    mod_take(first_cols, z.mod, mod2)
    for i in range(3, 6):
        cp_w[i].wait()
        send_w[i].wait_recv()

    eye = (lanes_of((WIN, WIN), 0) == lanes_of((WIN, WIN))).astype(BF16)

    def head_of(x, h, off=0):
        lane = lanes_of(x.shape)
        lo = off + h * HEAD_DIM
        return jnp.where((lane >= lo) & (lane < lo + HEAD_DIM), x, jnp.zeros_like(x))

    def attend_seq(s):
        r.stat[0] = jnp.full((8, block), NEG, F32)
        r.stat[1] = jnp.zeros((8, block), F32)
        r.acc[...] = jnp.zeros((hw, block), F32)
        q = r.qd[s, :, 0:WIN]

        def one_block(back):
            j = c - back

            @pl.when(back > 0)
            def _():
                def take(idx):
                    there = r.kv.at[j, s, span(idx), :]
                    remote(
                        there, there, r.s_kv.at[j, s, idx], r.r_kv.at[j, s, idx], ctx=j
                    ).wait_recv()

                each(nt, take)

            keys = r.kv[j, s, :, 0:WIN]
            r.vt[...] = mm(eye, r.kv[j, s, :, z.vlo : z.vlo + WIN], NT).astype(BF16)
            for h in range(z.heads):
                scores = mm(keys, head_of(q, h), NT)
                old = r.stat[0, h : h + 1, :]
                top = jnp.maximum(old, jnp.max(scores, axis=0, keepdims=True))
                prob = jnp.exp(scores - top)
                fade = jnp.exp(old - top)
                r.stat[0, h : h + 1, :] = top
                r.stat[1, h : h + 1, :] = r.stat[1, h : h + 1, :] * fade + jnp.sum(
                    prob, axis=0, keepdims=True
                )
                lo = h * HEAD_DIM
                vt = r.vt[z.voff + lo : z.voff + lo + HEAD_DIM, :]
                r.acc[lo : lo + HEAD_DIM, :] = r.acc[lo : lo + HEAD_DIM, :] * fade + mm(
                    vt, prob.astype(BF16)
                )

        each(c + 1, one_block)
        for h in range(z.heads):
            lo = h * HEAD_DIM
            denom = r.stat[1, h : h + 1, :]
            r.lse[c, s, h : h + 1, :] = r.stat[0, h : h + 1, :] + jnp.log(denom)
            r.att[s, lo : lo + HEAD_DIM, :] = r.acc[lo : lo + HEAD_DIM, :] / denom
        low = jnp.transpose(r.att[s]).astype(BF16)
        r.attl[s, :, 0:hw] = low
        r.attl[s, :, hw:WIN] = jnp.zeros((block, WIN - hw), BF16)
        r.br[s] = mm(low, r.wot[z.voff : z.voff + hw, :]).astype(BF16)
        brs.push_all(s)

    each(seqs, attend_seq)

    def query_copy(j, s, to):
        return remote(
            r.qd.at[s, :, 0:LANES],
            r.kv.at[j, s, :, 0:LANES],
            r.s_q.at[to, s],
            r.r_q.at[j, s],
            ctx=to,
        )

    def stat_copy(buf, which, j, s, to):
        return remote(
            buf.at[j, s], buf.at[j, s], r.s_st.at[which, to, s], r.r_st.at[which, j, s], ctx=to
        )

    def send_queries(to):
        for s in range(seqs):
            query_copy(c, s, to).start()
            stat_copy(r.lse, 0, c, s, to).start()

    each(c, send_queries)
    for s in range(seqs):
        cots.relay(s)
    def middle_rows(s):
        branch = brs.total(s)
        r.branch[s] = branch
        middle = r.tok[s, span(t), :].astype(F32) + vec(2, s) * branch
        r.middle[s] = middle
        unit, _ = norm_parts(middle)
        r.n2[s, span(t), :] = (unit * (1.0 + vec(4, s)) + vec(3, s)).astype(BF16)
        n2s.open(piece(r.n2, s, t), s)

    brs.join(0)
    middle_rows(0)
    brs.join(1)
    n2s.relay(0)
    middle_rows(1)

    def feed(s, idx, i):
        at = span(idx)
        hid = mm(r.n2[s, at, :], r.wu[...])
        square = hid * hid
        tanh = jnp.tanh(GELU_C * (hid + GELU_A * (hid * square)))
        r.act[s, at, :] = (0.5 * hid * (1.0 + tanh)).astype(BF16)
        slope = 0.5 * (1.0 + tanh) + 0.5 * hid * (1.0 - tanh * tanh) * (
            GELU_C * (1.0 + 3.0 * GELU_A * square)
        )
        low = (vec(5, s) * r.cot[s, at, :].astype(F32)).astype(BF16)
        r.mgrad[s, at, :] = low
        hgrad = (slope * mm(low, r.wd[...])).astype(BF16)
        r.hgrad[s, at, :] = hgrad
        r.g2[s, at, :] = mm(hgrad, r.wu[...], NT).astype(BF16)
        g2s.push(s, idx, i)

    for s in range(seqs):
        feed(s, t, 0)
    for s in range(seqs):
        cots.collect(s, None)
        if s > 0:
            n2s.relay(s)
        n2s.collect(s, feed)
    g2s.join(0)

    class Reduction:
        def __init__(self, got, mine, theirs, buf, total, sems, sems_all):
            self.got, self.mine, self.theirs, self.buf, self.total = got, mine, theirs, buf, total
            self.sems, self.sems_all = sems, sems_all
            self.chunk = buf.shape[1]
            self.owners = mine.shape[0] // self.chunk

        def rows(self, o):
            return pl.ds(pl.multiple_of(o * self.chunk, 16), self.chunk)

        def part(self, o):
            return remote(
                self.mine.at[self.rows(o), :],
                self.buf.at[c],
                self.sems.at[0, o],
                self.sems.at[1, c],
                ctx=o,
            )

        def share(self, owner, to):
            here = self.total.at[self.rows(owner), :]
            return remote(here, here, self.sems_all.at[0, to], self.sems_all.at[1, owner], ctx=to)

        def to_owners(self, body):
            def one(k):
                o = (c + k) % nc

                @pl.when(o < self.owners)
                def _():
                    body(o)

            each(nc, one, 1)

        def as_owner(self, body):
            @pl.when(c < self.owners)
            def _():
                body()

        def pair(self):
            self.got.wait()
            self.mine[...] = (self.mine[...].astype(F32) + self.theirs[...].astype(F32)).astype(
                BF16
            )

        def step1(self):
            self.to_owners(lambda o: self.part(o).start())

        def step2(self):
            pass

        def step4(self):
            pass

        def step3(self):
            def body():
                def add(k, acc):
                    fr = (c + k) % nc
                    there = self.buf.at[fr]
                    remote(
                        there, there, self.sems.at[0, fr], self.sems.at[1, fr], ctx=fr
                    ).wait_recv()
                    return acc + self.buf[fr].astype(F32)

                acc = self.mine[self.rows(c), :].astype(F32)
                if nc <= 4:
                    for k in range(1, nc):
                        acc = add(k, acc)
                else:
                    acc = lax.fori_loop(1, nc, add, acc)
                self.total[self.rows(c), :] = acc.astype(BF16)
                each(nc, lambda k: self.share(c, (c + k) % nc).start(), 1)

            self.as_owner(body)

        def take(self):
            def one(o):
                self.share(o, o).wait_recv()
                self.part(o).wait_send()

            self.to_owners(one)
            self.as_owner(
                lambda: each(nc, lambda k: self.share(c, (c + k) % nc).wait_send(), 1)
            )

    class Square:
        def __init__(self, got, mine, theirs, buf, total, sems, sems_all):
            self.got, self.mine, self.theirs, self.buf, self.total = got, mine, theirs, buf, total
            self.sems = sems
            self.part = buf.shape[1] // 2
            by_x = c + 1 - 2 * (c % 2)
            by_y = (c + 2) % 4
            self.near = (by_x, by_y)
            self.next = (by_y, by_x)
            self.far = 3 - c

        def rows(self, o, h):
            return pl.ds(pl.multiple_of((2 * o + h) * self.part, 16), self.part)

        def first(self, h, k):
            o = (self.near[h], self.far)[k]
            return remote(
                self.mine.at[self.rows(o, h), :],
                self.buf.at[2 * h + k, 0 : self.part, :],
                self.sems.at[0, 2 * h + k],
                self.sems.at[1, 2 * h + k],
                ctx=self.near[h],
            )

        def second(self, h):
            o = self.next[h]
            return remote(
                self.mine.at[self.rows(o, h), :],
                self.buf.at[2 * h, self.part : 2 * self.part, :],
                self.sems.at[0, 4 + h],
                self.sems.at[1, 4 + h],
                ctx=o,
            )

        def spread(self, h, o, to, which, landed):
            at = self.total.at[self.rows(landed, h), :]
            src = self.total.at[self.rows(o, h), :]
            return remote(src, at, self.sems.at[0, which], self.sems.at[1, which], ctx=to)

        def third(self, h, landed):
            return self.spread(h, landed, self.next[h], 6 + h, landed)

        def fourth(self, h, k, landed):
            return self.spread(h, landed, self.near[h], 8 + 2 * h + k, landed)

        def pair(self):
            self.got.wait()
            self.mine[...] = (self.mine[...].astype(F32) + self.theirs[...].astype(F32)).astype(
                BF16
            )

        def step1(self):
            for k in (1, 0):
                for h in range(2):
                    self.first(h, k).start()

        def step2(self):
            for k in (1, 0):
                for h in range(2):
                    self.first(h, k).wait_recv()
                    at = self.rows((c, self.next[h])[k], h)
                    self.mine[at, :] = (
                        self.mine[at, :].astype(F32)
                        + self.buf[2 * h + k, 0 : self.part, :].astype(F32)
                    ).astype(BF16)
                    if k == 1:
                        self.second(h).start()

        def step3(self):
            for h in range(2):
                self.second(h).wait_recv()
                at = self.rows(c, h)
                self.total[at, :] = (
                    self.mine[at, :].astype(F32)
                    + self.buf[2 * h, self.part : 2 * self.part, :].astype(F32)
                ).astype(BF16)
                self.third(h, c).start()
            for h in range(2):
                self.fourth(h, 0, c).start()

        def step4(self):
            for h in range(2):
                self.third(h, self.next[h]).wait_recv()
                self.fourth(h, 1, self.next[h]).start()

        def take(self):
            for h in range(2):
                self.fourth(h, 0, self.near[h]).wait_recv()
                self.fourth(h, 1, self.far).wait_recv()
                for k in range(2):
                    self.first(h, k).wait_send()
                    self.fourth(h, k, c).wait_send()
                self.second(h).wait_send()
                self.third(h, c).wait_send()

    Sums = Square if nc == 4 else Reduction

    r.msum[...] = jnp.zeros((8, z.mod), F32)

    def keep_sum(slot_idx, s, value):
        lo = slot_idx * width
        r.msum[s : s + 1, lo : lo + width] = jnp.sum(value, axis=0, keepdims=True)

    def middle_back(s):
        grad2 = g2s.total(s)
        unit, rstd = norm_parts(r.middle[s])
        mid_grad = r.cot[s, span(t), :].astype(F32) + norm_back(grad2, unit, rstd, vec(4, s))
        r.midg[s] = mid_grad
        r.bg[s, span(t), :] = (vec(2, s) * mid_grad).astype(BF16)
        bgs.open(piece(r.bg, s, t), s)
        keep_sum(3, s, grad2)
        keep_sum(4, s, grad2 * unit)
        keep_sum(2, s, mid_grad * r.branch[s])

    middle_back(0)

    def pair_grads(lhs, rhs, mine, sent, lo, hi):
        right = flat(rhs[...])
        for which, dst in ((other, sent), (d, mine)):
            cols = pl.ds(pl.multiple_of(which * half, half), half)
            left = flat(lhs[:, :, cols])
            dst[:, lo:hi] = mm(left, right, TN).astype(BF16)

    pair_grads(r.mgrad, r.act, r.ga_o, r.ga_s, z.ff, 2 * z.ff)
    pair_grads(r.n2, r.hgrad, r.ga_o, r.ga_s, 0, z.ff)
    send_ga = remote(r.ga_s, r.ga_r, r.s_ga.at[0], r.s_ga.at[1], dp=other)
    send_ga.start()
    g2s.join(1)
    bgs.relay(0)
    red_a = Sums(send_ga, r.ga_o, r.ga_r, r.ga_c, r.ga_t, r.s_gac, r.s_gag)
    red_a.pair()
    red_a.step1()
    middle_back(1)
    for s in range(seqs):
        r.ml[s] = mm(r.act[s], r.wd[...], NT).astype(BF16)

    def grad_copy(j, s, idx, to):
        at = span(idx)
        return remote(
            r.qd.at[s, at, LANES : z.kvw],
            r.kv.at[j, s, at, LANES : z.kvw],
            r.s_do.at[to, s, idx],
            r.r_do.at[j, s, idx],
            ctx=to,
        )

    def out_grads(s, idx, i):
        at = span(idx)
        do = mm(r.bg[s, at, :], r.wot[...], NT).astype(BF16)
        over = WIN - z.vlo
        r.qd[s, at, z.vlo : WIN] = r.qd[s, at, z.vlo : WIN] + do[:, 0:over]
        r.qd[s, at, WIN : z.kvw] = do[:, over:WIN]
        each(c, lambda to: grad_copy(c, s, idx, to).start())

    def deltas(s):
        r.dot[...] = mm(eye, r.qd[s, :, z.vlo : z.vlo + WIN], NT).astype(BF16)
        for h in range(z.heads):
            lo = h * HEAD_DIM
            r.delta[c, s, h : h + 1, :] = jnp.sum(
                r.dot[z.voff + lo : z.voff + lo + HEAD_DIM, :].astype(F32)
                * r.att[s, lo : lo + HEAD_DIM, :],
                axis=0,
                keepdims=True,
            )
        each(c, lambda to: stat_copy(r.delta, 1, c, s, to).start())

    def query_back_copy(j, s, to):
        return remote(
            r.dq_s.at[to, s], r.dq_r.at[j, s], r.s_dq.at[to, s], r.r_dq.at[j, s], ctx=to
        )

    def back_seq(s):
        keys = r.kv[c, s, :, 0:WIN]
        vals = r.kv[c, s, :, z.vlo : z.vlo + WIN]
        r.vt[...] = mm(eye, keys, NT).astype(BF16)
        r.dkv[s] = jnp.zeros((block, z.kvw), F32)

        def one_block(k):
            j = c + (nc - c - k) % (nc - c)

            @pl.when(k == 0)
            def _():
                r.seen[...] = r.qd[s]

            @pl.when(k > 0)
            def _():
                query_copy(j, s, j).wait_recv()
                each(nt, lambda idx: grad_copy(j, s, idx, j).wait_recv())
                stat_copy(r.lse, 0, j, s, j).wait_recv()
                stat_copy(r.delta, 1, j, s, j).wait_recv()
                r.seen[...] = r.kv[j, s]

            q = r.seen[:, 0:WIN]
            do = r.seen[:, z.vlo : z.vlo + WIN]
            dk = jnp.zeros((block, WIN), F32)
            dv = jnp.zeros((block, WIN), F32)
            for h in range(z.heads):
                lo = h * HEAD_DIM
                qh = head_of(q, h)
                doh = head_of(do, h, z.voff)
                prob = jnp.exp(mm(keys, qh, NT) - r.lse[j, s, h : h + 1, :])
                dprob = mm(vals, doh, NT)
                dsc = (prob * (dprob - r.delta[j, s, h : h + 1, :])).astype(BF16)
                dv = dv + mm(prob.astype(BF16), doh)
                dk = dk + mm(dsc, qh)
                dqt = mm(r.vt[lo : lo + HEAD_DIM, :], dsc)

                @pl.when(k == 0)
                def _():
                    r.dqt[s, lo : lo + HEAD_DIM, :] = dqt

                @pl.when(k > 0)
                def _():
                    r.dq_s[j, s, lo : lo + HEAD_DIM, :] = dqt.astype(BF16)

            over = WIN - z.vlo
            r.dkv[s, :, 0 : z.vlo] += dk[:, 0 : z.vlo]
            r.dkv[s, :, z.vlo : WIN] += dk[:, z.vlo : WIN] + dv[:, 0:over]
            r.dkv[s, :, WIN : z.kvw] += dv[:, over:WIN]

            @pl.when(k > 0)
            def _():
                query_back_copy(c, s, j).start()

        each(nc - c, one_block)

    for s in range(seqs):
        out_grads(s, t, 0)
    bgs.collect(0, out_grads)
    deltas(0)
    red_a.step2()
    bgs.relay(1)
    for s in range(seqs):
        mls.push_all(s)
    back_seq(0)
    bgs.collect(1, out_grads)
    deltas(1)
    red_a.step3()
    back_seq(1)
    red_a.step4()
    for s in range(seqs):
        mls.join(s)

    for s in range(seqs):
        g2s.close(s)
    cos1, sin1 = r.cosine[...], r.sine[...]
    for s in range(seqs):

        def add_dq(j):
            query_back_copy(j, s, j).wait_recv()
            r.dqt[s] += r.dq_r[j, s].astype(F32)

        each(c, add_dq)
        r.dq[s, :, 0:hw] = jnp.transpose(r.dqt[s]) * (HEAD_DIM ** -0.5)
        r.dq[s, :, hw:WIN] = jnp.zeros((block, WIN - hw), F32)
        for j in range(WIN // LANES):
            x = r.dq[s, :, j * LANES : (j + 1) * LANES]
            r.qb[s, :, j * LANES : (j + 1) * LANES] = (x * cos1 - swap(x) * sin1).astype(BF16)
        for j in range(z.kvw // LANES):
            x = r.dkv[s, :, j * LANES : (j + 1) * LANES]
            keys = min(max(hw - j * LANES, 0), LANES)
            if keys > 0:
                turned = x * cos1 - swap(x) * sin1
                x = turned if keys == LANES else jnp.where(lanes_of(x.shape) < keys, turned, x)
            r.kvb[s, :, j * LANES : (j + 1) * LANES] = x.astype(BF16)
        r.g2[s] = (mm(r.qb[s], r.wqt[...]) + mm(r.kvb[s], r.wkvt[...])).astype(BF16)
        n1s.push_all(s)

    for which, dst in ((other, r.gb_s), (d, r.gb_o)):
        cols = pl.ds(pl.multiple_of(which * half, LANES), half)
        right = flat(r.nrm[:, :, cols])
        dst[0:hw, :] = mm(flat(r.qb[:, :, 0:hw]), right, TN).astype(BF16)
        dst[hw : 3 * hw, :] = mm(flat(r.kvb[...]), right, TN).astype(BF16)
        right = flat(r.bg[:, :, cols])
        dst[3 * hw : 4 * hw, :] = mm(flat(r.attl[:, :, 0:hw]), right, TN).astype(BF16)
    send_gb = remote(r.gb_s, r.gb_r, r.s_gb.at[0], r.s_gb.at[1], dp=other)
    send_gb.start()
    red_b = Sums(send_gb, r.gb_o, r.gb_r, r.gb_c, r.gb_t, r.s_gbc, r.s_gbg)
    n1s.join(0)
    red_b.pair()
    red_b.step1()
    n1s.join(1)
    red_b.step2()

    outs = []

    def store(src, dst):
        cp = pltpu.make_async_copy(src, dst, r.s_loc.at[len(local) + len(outs)])
        cp.start()
        outs.append(cp)

    for s in range(seqs):
        grad1 = n1s.total(s)
        unit, rstd = norm_parts(r.tok[s, span(t), :].astype(F32))
        keep_sum(0, s, grad1)
        keep_sum(1, s, grad1 * unit)
        r.gtok[s] = r.midg[s] + norm_back(grad1, unit, rstd, vec(1, s))
        if s == 0:
            red_b.step3()
        mlp = mls.total(s)
        r.res[s] = (r.middle[s] + vec(5, s) * mlp).astype(BF16)
        keep_sum(5, s, r.cot[s, span(t), :].astype(F32) * mlp)
    def mcol(idx):
        return pl.ds(pl.multiple_of(idx * z.mcols, LANES), z.mcols)

    for k in range(1, nt):
        to = (t + k) % nt
        remote(
            r.msum.at[:, mcol(to)], r.mt_r.at[t], r.s_mt.at[0, to], r.s_mt.at[1, t], tp=to
        ).start()
    store(r.res, r.res_out)
    store(r.gtok, r.gtok_out)
    red_b.step4()
    total = r.msum[:, mcol(t)]
    for k in range(1, nt):
        fr = (t + k) % nt
        there = r.mt_r.at[fr]
        remote(there, there, r.s_mt.at[0, fr], r.s_mt.at[1, fr], tp=fr).wait_recv()
        total = total + r.mt_r[fr]
    r.md_s[...] = total
    send_md = remote(r.md_s, r.md_r, r.s_md.at[0], r.s_md.at[1], dp=other)
    send_md.start()
    send_md.wait()
    r.mg[pl.ds(c, 1), 0:2, :] = total[None, 0:2, :]
    r.mg[pl.ds(c, 1), 2:4, :] = r.md_r[0:2, :][None]
    r.mg[pl.ds(c, 1), 4:8, :] = jnp.zeros((1, 4, z.mcols), F32)

    def send_mg(k):
        to = (c + k) % nc
        remote(r.mg.at[c], r.mg.at[c], r.s_mc.at[0, to], r.s_mc.at[1, c], ctx=to).start()

    each(nc, send_mg, 1)
    red_a.take()
    store(r.ga_t, r.ga_out)
    red_b.take()
    store(r.gb_t, r.gb_out)

    def take_small(k):
        fr = (c + k) % nc
        for buf, sems in ((r.mg, r.s_mc), (r.emb, r.s_ec)):
            remote(buf.at[fr], buf.at[fr], sems.at[0, fr], sems.at[1, fr], ctx=fr).wait_recv()
            remote(buf.at[c], buf.at[c], sems.at[0, fr], sems.at[1, c], ctx=fr).wait_send()

    each(nc, take_small, 1)
    store(r.mg, r.mg_out)
    store(r.emb, r.emb_out)

    for cp in send_w:
        cp.wait_send()
    for s in range(seqs):
        for group in (toks, cots, n2s, bgs, brs, mls, n1s):
            group.close(s)
    for k in range(1, nt):
        to = (t + k) % nt
        remote(
            r.msum.at[:, mcol(to)], r.mt_r.at[t], r.s_mt.at[0, to], r.s_mt.at[1, t], tp=to
        ).wait_send()

    def kv_sent(to):
        for s in range(seqs):

            def one(idx):
                mine = r.kv.at[c, s, span(idx), :]
                remote(
                    mine, mine, r.s_kv.at[to, s, idx], r.r_kv.at[c, s, idx], ctx=to
                ).wait_send()

            each(nt, one)
            query_back_copy(c, s, to).wait_send()

    each(nc, kv_sent, c + 1)

    def query_sent(to):
        for s in range(seqs):
            query_copy(c, s, to).wait_send()
            each(nt, lambda idx: grad_copy(c, s, idx, to).wait_send())
            stat_copy(r.lse, 0, c, s, to).wait_send()
            stat_copy(r.delta, 1, c, s, to).wait_send()

    each(c, query_sent)
    for cp in outs:
        cp.wait()


def finish_kernel(z, *refs):
    ins, outs, refs = refs[:6], refs[6:15], refs[15:]
    held, stage, sems = refs[:6], refs[6:15], refs[15]
    hw = z.hw
    fetches = [
        pltpu.make_async_copy(src, dst, sems.at[i]) for i, (src, dst) in enumerate(zip(ins, held))
    ]
    for cp in fetches:
        cp.start()
    ga, gb, emb, mg, res, gtok = held
    copies = []

    def put(i, value):
        stage[i][...] = value
        cp = pltpu.make_async_copy(stage[i], outs[i], sems.at[6 + i])
        cp.start()
        copies.append(cp)

    def through(i, src):
        cp = pltpu.make_async_copy(src, outs[i], sems.at[6 + i])
        cp.start()
        copies.append(cp)

    fetches[0].wait()
    put(6, ga[:, 0 : z.ff].astype(F32))
    put(7, ga[:, z.ff : 2 * z.ff].astype(F32))
    fetches[1].wait()
    for i in range(4):
        put(2 + i, gb[i * hw : (i + 1) * hw, :].astype(F32))
    fetches[2].wait()
    fetches[3].wait()
    e = emb[...].reshape(z.nc * 8, z.half).astype(BF16)
    rest = mg[...].reshape(z.nc * 8, z.mcols)
    terms = []
    for _ in range(3):
        terms.append(rest.astype(BF16))
        rest = rest - terms[-1].astype(F32)
    put(8, mm(jnp.concatenate([e] * 3, axis=0), jnp.concatenate(terms, axis=0), TN))
    fetches[4].wait()
    through(0, res)
    fetches[5].wait()
    through(1, gtok)
    for cp in copies:
        cp.wait()


IN_NAMES = (
    "tok_in",
    "ts_in",
    "wq_in",
    "wk_in",
    "wv_in",
    "wo_in",
    "wu_in",
    "wd_in",
    "wm_in",
    "cot_in",
)
OUT_NAMES = ("res_out", "gtok_out", "ga_out", "gb_out", "emb_out", "mg_out")


def solution(mesh):
    def shards(tokens, steps, wq, wk, wv, wo, wu, wd, wm, cot):
        wq, wk, wv, wo = wq.T, wk.T, wv.T, wo.T
        z = Dims(mesh, tokens.shape, wq.shape, wu.shape, wm.shape)
        table = scratch_table(z)
        names = list(IN_NAMES) + list(OUT_NAMES) + list(table)
        hbm = pl.BlockSpec(memory_space=pl.ANY)
        smem = pl.BlockSpec(memory_space=pltpu.SMEM)
        own = (z.seqs, z.rows, z.width)
        shape = jax.ShapeDtypeStruct
        outs = pl.pallas_call(
            functools.partial(layer_kernel, z, names),
            out_shape=(
                shape(own, BF16),
                shape(own, F32),
                shape((z.half, z.wide), BF16),
                shape((z.heads_rows, z.half), BF16),
                shape((z.nc, 8, z.half), F32),
                shape((z.nc, 8, z.mcols), F32),
            ),
            in_specs=[hbm, smem] + [hbm] * 8,
            out_specs=[hbm] * 6,
            scratch_shapes=list(table.values()),
            compiler_params=pltpu.CompilerParams(
                collective_id=0, has_side_effects=True, vmem_limit_bytes=VMEM_BYTES
            ),
            name="layer",
        )(tokens, steps.T, wq, wk, wv, wo, wu, wd, wm, cot)
        outs = outs[2:] + outs[:2]
        shapes = (
            (own, BF16),
            (own, F32),
            ((z.hw, z.half), F32),
            ((z.hw, z.half), F32),
            ((z.hw, z.half), F32),
            ((z.hw, z.half), F32),
            ((z.half, z.ff), F32),
            ((z.half, z.ff), F32),
            ((z.half, z.mcols), F32),
        )
        done = pl.pallas_call(
            functools.partial(finish_kernel, z),
            out_shape=tuple(shape(*o) for o in shapes),
            in_specs=[hbm] * 6,
            out_specs=[hbm] * 9,
            scratch_shapes=[pltpu.VMEM(o.shape, o.dtype) for o in outs]
            + [pltpu.VMEM(*o) for o in shapes]
            + [pltpu.SemaphoreType.DMA((15,))],
            compiler_params=pltpu.CompilerParams(vmem_limit_bytes=VMEM_BYTES),
            name="finish",
        )(*outs)
        return done[:2] + tuple(g.T for g in done[2:6]) + done[6:]

    rows = P("dp", ("ctx", "tp"), None)
    cols = P("dp", "tp")
    return jax.shard_map(
        shards,
        mesh=mesh,
        in_specs=(rows, P("dp", "ctx")) + (cols,) * 6 + (P("dp", None), rows),
        out_specs=(rows, rows) + (cols,) * 7,
        check_vma=False,
    )
```

```python
import functools
import math

import jax
import jax.numpy as jnp
from jax import lax
from jax.experimental import pallas as pl
from jax.experimental.pallas import tpu as pltpu
from jax.sharding import PartitionSpec as P

MESH = pl.DeviceIdType.MESH
HEAD_DIM = 64
WIN = 256
LANES = 128
EPS = 1e-06
NEG = -1e30
GELU_C = 0.7978845608028654
GELU_A = 0.044715
F32 = jnp.float32
BF16 = jnp.bfloat16
VMEM_BYTES = 62 * 1024 * 1024

NN = (((1,), (0,)), ((), ()))
NT = (((1,), (1,)), ((), ()))
TN = (((0,), (0,)), ((), ()))


def mm(a, b, dims=NN):
    return lax.dot_general(a, b, dims, preferred_element_type=F32)


def norm_parts(x):
    center = x - jnp.mean(x, axis=-1, keepdims=True)
    rstd = lax.rsqrt(jnp.mean(center * center, axis=-1, keepdims=True) + EPS)
    return center * rstd, rstd


def norm_back(grad, unit, rstd, scale):
    dn = grad * (1.0 + scale)
    return rstd * (
        dn
        - jnp.mean(dn, axis=-1, keepdims=True)
        - unit * jnp.mean(dn * unit, axis=-1, keepdims=True)
    )


def remote(src, dst, send, recv, **dev):
    return pltpu.make_async_remote_copy(
        src_ref=src, dst_ref=dst, send_sem=send, recv_sem=recv, device_id=dev, device_id_type=MESH
    )


def chunk_rows(count, devices):
    return 16 * -(-(count // 16) // devices)


class Dims:
    def __init__(self, mesh, tokens, query, up, mod):
        self.nc = mesh.shape["ctx"]
        self.nt = mesh.shape["tp"]
        self.seqs, self.rows, self.width = tokens
        self.block = self.rows * self.nt
        self.hw, self.half = query
        self.heads = self.hw // HEAD_DIM
        self.ff = up[1]
        self.mod = mod[1]
        self.kvw = 2 * self.hw
        self.vlo = self.kvw - WIN
        self.voff = self.hw - self.vlo
        self.wide = 2 * self.ff
        self.heads_rows = 4 * self.hw
        self.mcols = self.mod // self.nt
        self.thirds = self.mcols // self.half


def scratch_table(z):
    vm = lambda shape, dtype=BF16: pltpu.VMEM(shape, dtype)
    sem = lambda *shape: pltpu.SemaphoreType.DMA(shape)
    full = (z.seqs, z.block, z.width)
    own = (z.seqs, z.rows, z.width)
    pair = (z.seqs, 2, z.rows, z.width)
    return dict(
        tok=vm(full),
        cot=vm(full),
        wqt=vm((WIN, z.width)),
        wkvt=vm((z.kvw, z.width)),
        wot=vm((WIN, z.width)),
        wu=vm((z.width, z.ff)),
        wd=vm((z.width, z.ff)),
        wm=vm((z.half, z.mod)),
        emb_s=vm((8, z.half), F32),
        emb_r=vm((8, z.half), F32),
        emb=vm((z.nc, 8, z.half), F32),
        mod_s=vm((8, z.mod), F32),
        mod_r=vm((8, z.mod), F32),
        mod=vm((8, z.mod), F32),
        cosine=vm((z.block, LANES), F32),
        sine=vm((z.block, LANES), F32),
        nrm=vm(full),
        qd=vm((z.seqs, z.block, z.kvw)),
        kv=vm((z.nc, z.seqs, z.block, z.kvw)),
        vt=vm((WIN, z.block)),
        stat=vm((2, 8, z.block), F32),
        acc=vm((z.hw, z.block), F32),
        att=vm((z.seqs, z.hw, z.block), F32),
        attl=vm((z.seqs, z.block, WIN)),
        lse=vm((z.nc, z.seqs, 8, z.block), F32),
        delta=vm((z.nc, z.seqs, 8, z.block), F32),
        br=vm(full),
        br_m=vm(pair),
        br_r=vm(pair),
        branch=vm(own, F32),
        middle=vm(own, F32),
        n2=vm(full),
        act=vm((z.seqs, z.block, z.ff)),
        hgrad=vm((z.seqs, z.block, z.ff)),
        mgrad=vm(full),
        g2=vm(full),
        g2_m=vm(pair),
        g2_r=vm(pair),
        ml=vm(full),
        ml_m=vm(pair),
        ml_r=vm(pair),
        midg=vm(own, F32),
        bg=vm(full),
        seen=vm((z.block, z.kvw)),
        dot=vm((WIN, z.block)),
        dqt=vm((z.seqs, z.hw, z.block), F32),
        dq_s=vm((z.nc, z.seqs, z.hw, z.block)),
        dq_r=vm((z.nc, z.seqs, z.hw, z.block)),
        dq=vm((z.seqs, z.block, WIN), F32),
        dkv=vm((z.seqs, z.block, z.kvw), F32),
        qb=vm((z.seqs, z.block, WIN)),
        kvb=vm((z.seqs, z.block, z.kvw)),
        n1_m=vm(pair),
        n1_r=vm(pair),
        ga_s=vm((z.half, z.wide)),
        ga_o=vm((z.half, z.wide)),
        ga_r=vm((z.half, z.wide)),
        ga_c=vm((z.nc, chunk_rows(z.half, z.nc), z.wide)),
        ga_t=vm((z.half, z.wide)),
        gb_s=vm((z.heads_rows, z.half)),
        gb_o=vm((z.heads_rows, z.half)),
        gb_r=vm((z.heads_rows, z.half)),
        gb_c=vm((z.nc, chunk_rows(z.heads_rows, z.nc), z.half)),
        gb_t=vm((z.heads_rows, z.half)),
        msum=vm((z.nt, 8, z.half), F32),
        mt_r=vm((z.nt, 8, z.half), F32),
        md_s=vm((8, z.half), F32),
        md_r=vm((8, z.half), F32),
        mg=vm((z.nc, 2, 8, z.half), F32),
        res=vm(own),
        gtok=vm(own, F32),
        s_loc=sem(16),
        s_w=sem(2, 6),
        s_e=sem(2),
        s_ec=sem(2, z.nc),
        s_m=sem(2, 2),
        s_tok=sem(z.seqs, 4),
        r_tok=sem(z.seqs, z.nt),
        s_cot=sem(z.seqs, 4),
        r_cot=sem(z.seqs, z.nt),
        s_kv=sem(z.nc, z.seqs, z.nt),
        r_kv=sem(z.nc, z.seqs, z.nt),
        s_br=sem(z.seqs, 4),
        m_br=sem(z.seqs, 2),
        r_br=sem(z.seqs, 2),
        s_n2=sem(z.seqs, 4),
        r_n2=sem(z.seqs, z.nt),
        s_g2=sem(z.seqs, 4),
        m_g2=sem(z.seqs, 2),
        r_g2=sem(z.seqs, 2),
        s_ml=sem(z.seqs, 4),
        m_ml=sem(z.seqs, 2),
        r_ml=sem(z.seqs, 2),
        s_bg=sem(z.seqs, 4),
        r_bg=sem(z.seqs, z.nt),
        s_q=sem(z.nc, z.seqs),
        r_q=sem(z.nc, z.seqs),
        s_do=sem(z.nc, z.seqs, z.nt),
        r_do=sem(z.nc, z.seqs, z.nt),
        s_st=sem(2, z.nc, z.seqs),
        r_st=sem(2, z.nc, z.seqs),
        s_dq=sem(z.nc, z.seqs),
        r_dq=sem(z.nc, z.seqs),
        s_n1=sem(z.seqs, 4),
        m_n1=sem(z.seqs, 2),
        r_n1=sem(z.seqs, 2),
        s_ga=sem(2),
        s_gac=sem(2, max(z.nc, 12)),
        s_gag=sem(2, max(z.nc, 12)),
        s_gb=sem(2),
        s_gbc=sem(2, max(z.nc, 12)),
        s_gbg=sem(2, max(z.nc, 12)),
        s_mt=sem(2, z.nt),
        s_md=sem(2),
        s_mc=sem(2, z.nc),
    )


class Box:
    pass


def layer_kernel(z, names, *refs):
    r = Box()
    for name, ref in zip(names, refs):
        setattr(r, name, ref)
    d, c, t = lax.axis_index("dp"), lax.axis_index("ctx"), lax.axis_index("tp")
    other = 1 - d
    nt, nc, rows, block, width, hw = z.nt, z.nc, z.rows, z.block, z.width, z.hw
    seqs, half = z.seqs, z.half

    def each(count, body, first=0):
        def step(i, carry):
            body(i)
            return carry

        lax.fori_loop(first, count, step, 0)

    def span(idx):
        return pl.ds(pl.multiple_of(idx * rows, rows), rows)

    def slot(ref, idx):
        return ref.at[:, span(idx), :]

    def piece(ref, s, idx):
        return ref.at[s, span(idx), :]

    def flat(x):
        return x.reshape(x.shape[0] * x.shape[1], x.shape[2])

    def lanes_of(shape, axis=1):
        return lax.broadcasted_iota(jnp.int32, shape, axis)

    local = []

    def fetch(src, dst):
        cp = pltpu.make_async_copy(src, dst, r.s_loc.at[len(local)])
        cp.start()
        local.append(cp)
        return cp

    my_half = pl.ds(pl.multiple_of(d * half, LANES), half)
    weights = [
        (r.wq_in, r.wqt.at[0:hw, my_half]),
        (r.wk_in, r.wkvt.at[0:hw, my_half]),
        (r.wv_in, r.wkvt.at[hw : z.kvw, my_half]),
        (r.wo_in, r.wot.at[z.voff : z.voff + hw, my_half]),
        (r.wu_in, r.wu.at[my_half, :]),
        (r.wd_in, r.wd.at[my_half, :]),
    ]
    first_cols = 2 * width
    cp_tok = fetch(r.tok_in, slot(r.tok, t))
    cp_wm1 = fetch(r.wm_in.at[:, 0:first_cols], r.wm.at[:, 0:first_cols])
    cp_w = [fetch(src, dst) for src, dst in weights]
    cp_wm2 = fetch(r.wm_in.at[:, first_cols : z.mod], r.wm.at[:, first_cols : z.mod])
    cp_cot = fetch(r.cot_in, slot(r.cot, t))

    r.wqt[hw:WIN, :] = jnp.zeros((WIN - hw, width), BF16)
    r.wot[0 : z.voff, :] = jnp.zeros((z.voff, width), BF16)

    bar = pltpu.get_barrier_semaphore()
    pl.semaphore_signal(bar, inc=1, device_id={"dp": other}, device_id_type=MESH)
    for k in range(1, nt):
        pl.semaphore_signal(bar, inc=1, device_id={"tp": (t + k) % nt}, device_id_type=MESH)

    def greet(k):
        pl.semaphore_signal(bar, inc=1, device_id={"ctx": (c + k) % nc}, device_id_type=MESH)

    each(nc, greet, 1)

    row8 = lanes_of((8, half), 0)
    step_of = jnp.where(
        row8 % 2 == 0, r.ts_in[0, 0].astype(F32), r.ts_in[0, 1].astype(F32)
    )
    angle = step_of * jnp.exp(
        lanes_of((8, half)).astype(F32) * (-math.log(10000.0) / half)
    )
    sin_e, cos_e = jnp.sin(angle), jnp.cos(angle)

    def silu_low(v):
        return (v / (1.0 + jnp.exp(-v))).astype(BF16).astype(F32)

    sin_e, cos_e = silu_low(sin_e), silu_low(cos_e)
    first = d == 0
    own_half = jnp.where(row8 < 2, jnp.where(first, sin_e, cos_e), 0.0)
    r.emb_s[...] = jnp.where(
        (row8 >= 2) & (row8 < 4), jnp.where(first, cos_e, sin_e), 0.0
    )
    pl.semaphore_wait(bar, 1 + (nt - 1) + (nc - 1))

    side = t // 2
    mate = t + 1 - 2 * (t % 2)
    cross = 2 - side
    outer = t % 3 == 0
    inner = t % 3 != 0

    def peer(i):
        far = i // 2
        return (1 - far) * (t + i * (1 - 2 * (t % 2))) + far * ((1 - side) * i + side * (3 - i))

    class Gather:
        def __init__(self, buf, send, recv):
            self.buf, self.sems, self.recv = buf, send, recv

        def copy(self, src, s, idx, k, to):
            return remote(
                src, piece(self.buf, s, idx), self.sems.at[s, k], self.recv.at[s, idx], tp=to
            )

        def open(self, src, s):
            self.copy(src, s, t, 1, cross).start()
            self.copy(src, s, t, 0, mate).start()

        def wait(self, s, idx):
            self.copy(piece(self.buf, s, idx), s, idx, 0, mate).wait_recv()

        def relay(self, s):
            @pl.when(inner)
            def _():
                def one(i):
                    idx = peer(i)
                    self.wait(s, idx)
                    self.copy(piece(self.buf, s, idx), s, idx, i, mate).start()

                each(4, one, 2)

        def collect(self, s, work):
            def one(i):
                idx = peer(i)

                @pl.when(outer | (i == 1))
                def _():
                    self.wait(s, idx)

                if work is not None:
                    work(s, idx, i)

            each(4, one, 1)

        def close(self, s):
            mine = piece(self.buf, s, t)
            self.copy(mine, s, t, 0, mate).wait_send()
            self.copy(mine, s, t, 1, cross).wait_send()

            @pl.when(inner)
            def _():
                each(4, lambda i: self.copy(mine, s, t, i, mate).wait_send(), 2)

    class Scatter:
        def __init__(self, part, merge, got, send, msem, gsem):
            self.part, self.merge, self.got = part, merge, got
            self.sems, self.msem, self.gsem = send, msem, gsem

        def to_got(self, s, idx, i, k):
            return remote(
                piece(self.part, s, idx),
                self.got.at[s, k],
                self.sems.at[s, i],
                self.gsem.at[s, k],
                tp=idx,
            )

        def to_merge(self, s, idx, i):
            return remote(
                piece(self.part, s, idx),
                self.merge.at[s, i - 2],
                self.sems.at[s, i],
                self.msem.at[s, i - 2],
                tp=mate,
            )

        def push(self, s, idx, i):
            @pl.when(i == 1)
            def _():
                self.to_got(s, idx, i, 0).start()

            @pl.when((i > 1) & outer)
            def _():
                self.to_merge(s, idx, i).start()

        def push_all(self, s):
            for i in (3, 2):
                self.push(s, peer(i), i)
            self.push(s, mate, 1)

        def join(self, s):
            @pl.when(inner)
            def _():
                def one(k):
                    i = 3 - k
                    idx = peer(i)
                    self.to_merge(s, idx, i).wait_recv()
                    at = span(idx)
                    self.part[s, at, :] = (
                        self.part[s, at, :].astype(F32) + self.merge[s, i - 2].astype(F32)
                    ).astype(BF16)
                    self.to_got(s, idx, i, 1).start()

                each(2, one)

        def total(self, s):
            for k in range(2):
                self.to_got(s, mate, 1, k).wait_recv()
            return (
                self.part[s, span(t), :].astype(F32)
                + self.got[s, 0].astype(F32)
                + self.got[s, 1].astype(F32)
            )

        def close(self, s):
            each(4, lambda i: self.to_got(s, mate, i, 0).wait_send(), 1)

    toks = Gather(r.tok, r.s_tok, r.r_tok)
    cots = Gather(r.cot, r.s_cot, r.r_cot)
    n2s = Gather(r.n2, r.s_n2, r.r_n2)
    bgs = Gather(r.bg, r.s_bg, r.r_bg)
    brs = Scatter(r.br, r.br_m, r.br_r, r.s_br, r.m_br, r.r_br)
    g2s = Scatter(r.g2, r.g2_m, r.g2_r, r.s_g2, r.m_g2, r.r_g2)
    mls = Scatter(r.ml, r.ml_m, r.ml_r, r.s_ml, r.m_ml, r.r_ml)
    n1s = Scatter(r.g2, r.n1_m, r.n1_r, r.s_n1, r.m_n1, r.r_n1)

    for s in range(seqs):
        toks.open(r.tok_in.at[s], s)

    @pl.when(outer)
    def _():
        for s in range(seqs):
            cots.open(r.cot_in.at[s], s)

    send_emb = remote(r.emb_s, r.emb_r, r.s_e.at[0], r.s_e.at[1], dp=other)
    send_emb.start()
    send_w = [
        remote(src, dst, r.s_w.at[0, i], r.s_w.at[1, i], dp=other)
        for i, (src, dst) in enumerate(weights)
    ]
    for cp in send_w[:3]:
        cp.start()

    send_emb.wait()
    emb4 = own_half + r.emb_r[...]
    r.emb[pl.ds(c, 1)] = emb4[None]
    emb_low = emb4.astype(BF16)

    def mod_part(lo, hi, which, ready):
        ready.wait()
        r.mod_s[:, lo:hi] = mm(emb_low, r.wm[:, lo:hi])
        cp = remote(
            r.mod_s.at[:, lo:hi], r.mod_r.at[:, lo:hi], r.s_m.at[0, which], r.s_m.at[1, which], dp=other
        )
        cp.start()
        return cp

    def mod_take(lo, hi, cp):
        cp.wait()
        for s in range(seqs):
            r.mod[s : s + 1, lo:hi] = r.mod_s[s : s + 1, lo:hi] + r.mod_r[s + 2 : s + 3, lo:hi]

    def vec(slot_idx, s):
        lo = slot_idx * width
        return r.mod[s : s + 1, lo : lo + width]

    mod1 = mod_part(0, first_cols, 0, cp_wm1)
    for cp in send_w[3:]:
        cp.start()

    def send_ctx_emb(k):
        to = (c + k) % nc
        remote(r.emb.at[c], r.emb.at[c], r.s_ec.at[0, to], r.s_ec.at[1, c], ctx=to).start()

    each(nc, send_ctx_emb, 1)

    place = (c * block + lanes_of((block, LANES), 0)).astype(F32)
    pair_of = (lanes_of((block, LANES)) % (HEAD_DIM // 2)).astype(F32)
    turn = place * jnp.exp(pair_of * (-2.0 * math.log(10000.0) / HEAD_DIM))
    low_lane = lanes_of((block, LANES)) % HEAD_DIM < HEAD_DIM // 2
    r.cosine[...] = jnp.cos(turn)
    r.sine[...] = jnp.where(low_lane, -jnp.sin(turn), jnp.sin(turn))

    def swap(x):
        low = lanes_of(x.shape) % HEAD_DIM < HEAD_DIM // 2
        return jnp.where(
            low,
            pltpu.roll(x, LANES - HEAD_DIM // 2, 1),
            pltpu.roll(x, HEAD_DIM // 2, 1),
        )

    for i in range(3):
        cp_w[i].wait()
        send_w[i].wait_recv()
    mod_take(0, first_cols, mod1)

    def make_qkv(s, idx, i):
        at = span(idx)
        unit, _ = norm_parts(r.tok[s, at, :].astype(F32))
        low = (unit * (1.0 + vec(1, s)) + vec(0, s)).astype(BF16)
        r.nrm[s, at, :] = low
        cos1, sin1 = r.cosine[at, :], r.sine[at, :]
        q_pre = mm(low, r.wqt[...], NT)
        kv_pre = mm(low, r.wkvt[...], NT)
        for j in range(WIN // LANES):
            x = q_pre[:, j * LANES : (j + 1) * LANES]
            x = (x * cos1 + swap(x) * sin1) * (HEAD_DIM ** -0.5)
            r.qd[s, at, j * LANES : (j + 1) * LANES] = x.astype(BF16)
        for j in range(z.kvw // LANES):
            x = kv_pre[:, j * LANES : (j + 1) * LANES]
            keys = min(max(hw - j * LANES, 0), LANES)
            if keys > 0:
                turned = x * cos1 + swap(x) * sin1
                x = turned if keys == LANES else jnp.where(lanes_of(x.shape) < keys, turned, x)
            r.kv[c, s, at, j * LANES : (j + 1) * LANES] = x.astype(BF16)

        def send_kv(to):
            mine = r.kv.at[c, s, at, :]
            remote(mine, mine, r.s_kv.at[to, s, idx], r.r_kv.at[c, s, idx], ctx=to).start()

        each(nc, send_kv, c + 1)

    cp_tok.wait()
    for s in range(seqs):
        make_qkv(s, t, 0)
    mod2 = mod_part(first_cols, z.mod, 1, cp_wm2)
    for s in range(seqs):
        toks.relay(s)
        toks.collect(s, make_qkv)

    @pl.when(inner)
    def _():
        for s in range(seqs):
            cots.open(r.cot_in.at[s], s)

    cp_cot.wait()
    mod_take(first_cols, z.mod, mod2)
    for i in range(3, 6):
        cp_w[i].wait()
        send_w[i].wait_recv()

    eye = (lanes_of((WIN, WIN), 0) == lanes_of((WIN, WIN))).astype(BF16)

    def head_of(x, h, off=0):
        lane = lanes_of(x.shape)
        lo = off + h * HEAD_DIM
        return jnp.where((lane >= lo) & (lane < lo + HEAD_DIM), x, jnp.zeros_like(x))

    def attend_seq(s):
        r.stat[0] = jnp.full((8, block), NEG, F32)
        r.stat[1] = jnp.zeros((8, block), F32)
        r.acc[...] = jnp.zeros((hw, block), F32)
        q = r.qd[s, :, 0:WIN]

        def one_block(back):
            j = c - back

            @pl.when(back > 0)
            def _():
                def take(idx):
                    there = r.kv.at[j, s, span(idx), :]
                    remote(
                        there, there, r.s_kv.at[j, s, idx], r.r_kv.at[j, s, idx], ctx=j
                    ).wait_recv()

                each(nt, take)

            keys = r.kv[j, s, :, 0:WIN]
            r.vt[...] = mm(eye, r.kv[j, s, :, z.vlo : z.vlo + WIN], NT).astype(BF16)
            for h in range(z.heads):
                scores = mm(keys, head_of(q, h), NT)
                old = r.stat[0, h : h + 1, :]
                top = jnp.maximum(old, jnp.max(scores, axis=0, keepdims=True))
                prob = jnp.exp(scores - top)
                fade = jnp.exp(old - top)
                r.stat[0, h : h + 1, :] = top
                r.stat[1, h : h + 1, :] = r.stat[1, h : h + 1, :] * fade + jnp.sum(
                    prob, axis=0, keepdims=True
                )
                lo = h * HEAD_DIM
                vt = r.vt[z.voff + lo : z.voff + lo + HEAD_DIM, :]
                r.acc[lo : lo + HEAD_DIM, :] = r.acc[lo : lo + HEAD_DIM, :] * fade + mm(
                    vt, prob.astype(BF16)
                )

        each(c + 1, one_block)
        for h in range(z.heads):
            lo = h * HEAD_DIM
            denom = r.stat[1, h : h + 1, :]
            r.lse[c, s, h : h + 1, :] = r.stat[0, h : h + 1, :] + jnp.log(denom)
            r.att[s, lo : lo + HEAD_DIM, :] = r.acc[lo : lo + HEAD_DIM, :] / denom
        low = jnp.transpose(r.att[s]).astype(BF16)
        r.attl[s, :, 0:hw] = low
        r.attl[s, :, hw:WIN] = jnp.zeros((block, WIN - hw), BF16)
        r.br[s] = mm(low, r.wot[z.voff : z.voff + hw, :]).astype(BF16)
        brs.push_all(s)

    each(seqs, attend_seq)

    split = nc == 4
    last = c == nc - 1
    skip = c // (nc - 1) if split else 0

    def query_copy(j, s, to):
        return remote(
            r.qd.at[s, :, 0:LANES],
            r.kv.at[j, s, :, 0:LANES],
            r.s_q.at[to, s],
            r.r_q.at[j, s],
            ctx=to,
        )

    def stat_copy(buf, which, j, s, to):
        return remote(
            buf.at[j, s], buf.at[j, s], r.s_st.at[which, to, s], r.r_st.at[which, j, s], ctx=to
        )

    def send_queries(to):
        for s in range(seqs):
            query_copy(c, s, to).start()
            stat_copy(r.lse, 0, c, s, to).start()

    each(c, send_queries, skip)
    for s in range(seqs):
        cots.relay(s)
    def middle_rows(s):
        branch = brs.total(s)
        r.branch[s] = branch
        middle = r.tok[s, span(t), :].astype(F32) + vec(2, s) * branch
        r.middle[s] = middle
        unit, _ = norm_parts(middle)
        r.n2[s, span(t), :] = (unit * (1.0 + vec(4, s)) + vec(3, s)).astype(BF16)
        n2s.open(piece(r.n2, s, t), s)

    brs.join(0)
    middle_rows(0)
    brs.join(1)
    n2s.relay(0)
    middle_rows(1)

    def feed(s, idx, i):
        at = span(idx)
        hid = mm(r.n2[s, at, :], r.wu[...])
        square = hid * hid
        tanh = jnp.tanh(GELU_C * (hid + GELU_A * (hid * square)))
        r.act[s, at, :] = (0.5 * hid * (1.0 + tanh)).astype(BF16)
        slope = 0.5 * (1.0 + tanh) + 0.5 * hid * (1.0 - tanh * tanh) * (
            GELU_C * (1.0 + 3.0 * GELU_A * square)
        )
        low = (vec(5, s) * r.cot[s, at, :].astype(F32)).astype(BF16)
        r.mgrad[s, at, :] = low
        hgrad = (slope * mm(low, r.wd[...])).astype(BF16)
        r.hgrad[s, at, :] = hgrad
        r.g2[s, at, :] = mm(hgrad, r.wu[...], NT).astype(BF16)
        g2s.push(s, idx, i)

    for s in range(seqs):
        feed(s, t, 0)
    for s in range(seqs):
        cots.collect(s, None)
        if s > 0:
            n2s.relay(s)
        n2s.collect(s, feed)
    g2s.join(0)

    class Reduction:
        def __init__(self, got, mine, theirs, buf, total, sems, sems_all):
            self.got, self.mine, self.theirs, self.buf, self.total = got, mine, theirs, buf, total
            self.sems, self.sems_all = sems, sems_all
            self.chunk = buf.shape[1]
            self.owners = mine.shape[0] // self.chunk

        def rows(self, o):
            return pl.ds(pl.multiple_of(o * self.chunk, 16), self.chunk)

        def part(self, o):
            return remote(
                self.mine.at[self.rows(o), :],
                self.buf.at[c],
                self.sems.at[0, o],
                self.sems.at[1, c],
                ctx=o,
            )

        def share(self, owner, to):
            here = self.total.at[self.rows(owner), :]
            return remote(here, here, self.sems_all.at[0, to], self.sems_all.at[1, owner], ctx=to)

        def to_owners(self, body):
            def one(k):
                o = (c + k) % nc

                @pl.when(o < self.owners)
                def _():
                    body(o)

            each(nc, one, 1)

        def as_owner(self, body):
            @pl.when(c < self.owners)
            def _():
                body()

        def pair(self):
            self.got.wait()
            self.mine[...] = (self.mine[...].astype(F32) + self.theirs[...].astype(F32)).astype(
                BF16
            )

        def step1(self):
            self.to_owners(lambda o: self.part(o).start())

        def step2(self):
            pass

        def step4(self):
            pass

        def step3(self):
            def body():
                def add(k, acc):
                    fr = (c + k) % nc
                    there = self.buf.at[fr]
                    remote(
                        there, there, self.sems.at[0, fr], self.sems.at[1, fr], ctx=fr
                    ).wait_recv()
                    return acc + self.buf[fr].astype(F32)

                acc = self.mine[self.rows(c), :].astype(F32)
                if nc <= 4:
                    for k in range(1, nc):
                        acc = add(k, acc)
                else:
                    acc = lax.fori_loop(1, nc, add, acc)
                self.total[self.rows(c), :] = acc.astype(BF16)
                each(nc, lambda k: self.share(c, (c + k) % nc).start(), 1)

            self.as_owner(body)

        def take(self):
            def one(o):
                self.share(o, o).wait_recv()
                self.part(o).wait_send()

            self.to_owners(one)
            self.as_owner(
                lambda: each(nc, lambda k: self.share(c, (c + k) % nc).wait_send(), 1)
            )

    class Square:
        def __init__(self, got, mine, theirs, buf, total, sems, sems_all):
            self.got, self.mine, self.theirs, self.buf, self.total = got, mine, theirs, buf, total
            self.sems = sems
            self.part = buf.shape[1] // 2
            by_x = c + 1 - 2 * (c % 2)
            by_y = (c + 2) % 4
            self.near = (by_x, by_y)
            self.next = (by_y, by_x)
            self.far = 3 - c

        def rows(self, o, h):
            return pl.ds(pl.multiple_of((2 * o + h) * self.part, 16), self.part)

        def first(self, h, k):
            o = (self.near[h], self.far)[k]
            return remote(
                self.mine.at[self.rows(o, h), :],
                self.buf.at[2 * h + k, 0 : self.part, :],
                self.sems.at[0, 2 * h + k],
                self.sems.at[1, 2 * h + k],
                ctx=self.near[h],
            )

        def second(self, h):
            o = self.next[h]
            return remote(
                self.mine.at[self.rows(o, h), :],
                self.buf.at[2 * h, self.part : 2 * self.part, :],
                self.sems.at[0, 4 + h],
                self.sems.at[1, 4 + h],
                ctx=o,
            )

        def spread(self, h, o, to, which, landed):
            at = self.total.at[self.rows(landed, h), :]
            src = self.total.at[self.rows(o, h), :]
            return remote(src, at, self.sems.at[0, which], self.sems.at[1, which], ctx=to)

        def third(self, h, landed):
            return self.spread(h, landed, self.next[h], 6 + h, landed)

        def fourth(self, h, k, landed):
            return self.spread(h, landed, self.near[h], 8 + 2 * h + k, landed)

        def pair(self):
            self.got.wait()
            self.mine[...] = (self.mine[...].astype(F32) + self.theirs[...].astype(F32)).astype(
                BF16
            )

        def step1(self):
            for k in (1, 0):
                for h in range(2):
                    self.first(h, k).start()

        def step2(self):
            for k in (1, 0):
                for h in range(2):
                    self.first(h, k).wait_recv()
                    at = self.rows((c, self.next[h])[k], h)
                    self.mine[at, :] = (
                        self.mine[at, :].astype(F32)
                        + self.buf[2 * h + k, 0 : self.part, :].astype(F32)
                    ).astype(BF16)
                    if k == 1:
                        self.second(h).start()

        def step3(self):
            for h in range(2):
                self.second(h).wait_recv()
                at = self.rows(c, h)
                self.total[at, :] = (
                    self.mine[at, :].astype(F32)
                    + self.buf[2 * h, self.part : 2 * self.part, :].astype(F32)
                ).astype(BF16)
                self.third(h, c).start()

        def step4(self):
            for h in range(2):
                self.fourth(h, 0, c).start()
            for h in range(2):
                self.third(h, self.next[h]).wait_recv()
                self.fourth(h, 1, self.next[h]).start()

        def take(self):
            for h in range(2):
                self.fourth(h, 0, self.near[h]).wait_recv()
                self.fourth(h, 1, self.far).wait_recv()
                for k in range(2):
                    self.first(h, k).wait_send()
                    self.fourth(h, k, c).wait_send()
                self.second(h).wait_send()
                self.third(h, c).wait_send()

    Sums = Square if nc == 4 else Reduction

    r.msum[...] = jnp.zeros((nt, 8, half), F32)

    def keep_sum(slot_idx, s, value):
        value = jnp.sum(value, axis=0, keepdims=True)
        for k in range(width // half):
            to, row = divmod(slot_idx * (width // half) + k, z.thirds)
            row = s * z.thirds + row
            r.msum[to, row : row + 1, :] = value[:, k * half : (k + 1) * half]

    def middle_back(s):
        grad2 = g2s.total(s)
        unit, rstd = norm_parts(r.middle[s])
        mid_grad = r.cot[s, span(t), :].astype(F32) + norm_back(grad2, unit, rstd, vec(4, s))
        r.midg[s] = mid_grad
        r.bg[s, span(t), :] = (vec(2, s) * mid_grad).astype(BF16)
        bgs.open(piece(r.bg, s, t), s)
        keep_sum(3, s, grad2)
        keep_sum(4, s, grad2 * unit)
        keep_sum(2, s, mid_grad * r.branch[s])

    middle_back(0)

    def pair_grads(lhs, rhs, mine, sent, lo, hi):
        right = flat(rhs[...])
        for which, dst in ((other, sent), (d, mine)):
            cols = pl.ds(pl.multiple_of(which * half, half), half)
            left = flat(lhs[:, :, cols])
            dst[:, lo:hi] = mm(left, right, TN).astype(BF16)

    pair_grads(r.mgrad, r.act, r.ga_o, r.ga_s, z.ff, 2 * z.ff)
    pair_grads(r.n2, r.hgrad, r.ga_o, r.ga_s, 0, z.ff)
    send_ga = remote(r.ga_s, r.ga_r, r.s_ga.at[0], r.s_ga.at[1], dp=other)
    send_ga.start()
    g2s.join(1)
    bgs.relay(0)
    red_a = Sums(send_ga, r.ga_o, r.ga_r, r.ga_c, r.ga_t, r.s_gac, r.s_gag)
    red_a.pair()
    red_a.step1()
    middle_back(1)
    for s in range(seqs):
        r.ml[s] = mm(r.act[s], r.wd[...], NT).astype(BF16)

    def grad_copy(j, s, idx, to):
        at = span(idx)
        return remote(
            r.qd.at[s, at, LANES : z.kvw],
            r.kv.at[j, s, at, LANES : z.kvw],
            r.s_do.at[to, s, idx],
            r.r_do.at[j, s, idx],
            ctx=to,
        )

    def out_grads(s, idx, i):
        at = span(idx)
        do = mm(r.bg[s, at, :], r.wot[...], NT).astype(BF16)
        over = WIN - z.vlo
        r.qd[s, at, z.vlo : WIN] = r.qd[s, at, z.vlo : WIN] + do[:, 0:over]
        r.qd[s, at, WIN : z.kvw] = do[:, over:WIN]
        each(c, lambda to: grad_copy(c, s, idx, to).start(), skip)

    def deltas(s):
        r.dot[...] = mm(eye, r.qd[s, :, z.vlo : z.vlo + WIN], NT).astype(BF16)
        for h in range(z.heads):
            lo = h * HEAD_DIM
            r.delta[c, s, h : h + 1, :] = jnp.sum(
                r.dot[z.voff + lo : z.voff + lo + HEAD_DIM, :].astype(F32)
                * r.att[s, lo : lo + HEAD_DIM, :],
                axis=0,
                keepdims=True,
            )
        each(c, lambda to: stat_copy(r.delta, 1, c, s, to).start(), skip)

    def query_back_copy(j, s, to):
        return remote(
            r.dq_s.at[to, s], r.dq_r.at[j, s], r.s_dq.at[to, s], r.r_dq.at[j, s], ctx=to
        )

    over = WIN - z.vlo

    def pair_back(s, keys, vals, q, do, j, keep):
        dk = jnp.zeros((block, WIN), F32)
        dv = jnp.zeros((block, WIN), F32)
        for h in range(z.heads):
            lo = h * HEAD_DIM
            qh = head_of(q, h)
            doh = head_of(do, h, z.voff)
            prob = jnp.exp(mm(keys, qh, NT) - r.lse[j, s, h : h + 1, :])
            dprob = mm(vals, doh, NT)
            dsc = (prob * (dprob - r.delta[j, s, h : h + 1, :])).astype(BF16)
            dv = dv + mm(prob.astype(BF16), doh)
            dk = dk + mm(dsc, qh)
            keep(lo, mm(r.vt[lo : lo + HEAD_DIM, :], dsc))
        return (
            (0, z.vlo, dk[:, 0 : z.vlo]),
            (z.vlo, WIN, dk[:, z.vlo : WIN] + dv[:, 0:over]),
            (WIN, z.kvw, dv[:, over:WIN]),
        )

    def far_copy(s):
        return remote(
            r.kv.at[0, s], r.kv.at[nc - 1, s], r.s_q.at[0, s], r.r_q.at[nc - 1, s], ctx=0
        )

    def back_seq(s, after_own):
        r.dkv[s] = jnp.zeros((block, z.kvw), F32)
        r.dqt[s] = jnp.zeros((hw, block), F32)
        if split:

            @pl.when(last)
            def _():
                keys = r.kv[0, s, :, 0:WIN]
                vals = r.kv[0, s, :, z.vlo : z.vlo + WIN]
                r.vt[...] = mm(eye, keys, NT).astype(BF16)

                def keep(lo, dqt):
                    r.dqt[s, lo : lo + HEAD_DIM, :] += dqt

                q = r.qd[s, :, 0:WIN]
                do = r.qd[s, :, z.vlo : z.vlo + WIN]
                for lo, hi, value in pair_back(s, keys, vals, q, do, c, keep):
                    r.kv[0, s, :, lo:hi] = value.astype(BF16)
                far_copy(s).start()

        keys = r.kv[c, s, :, 0:WIN]
        vals = r.kv[c, s, :, z.vlo : z.vlo + WIN]
        r.vt[...] = mm(eye, keys, NT).astype(BF16)

        def one_block(k):
            j = c + k

            @pl.when(k == 0)
            def _():
                r.seen[...] = r.qd[s]

            @pl.when(k == 1)
            def _():
                after_own()

            @pl.when(k > 0)
            def _():
                query_copy(j, s, j).wait_recv()
                each(nt, lambda idx: grad_copy(j, s, idx, j).wait_recv())
                stat_copy(r.lse, 0, j, s, j).wait_recv()
                stat_copy(r.delta, 1, j, s, j).wait_recv()
                r.seen[...] = r.kv[j, s]

            def keep(lo, dqt):
                @pl.when(k == 0)
                def _():
                    r.dqt[s, lo : lo + HEAD_DIM, :] += dqt

                @pl.when(k > 0)
                def _():
                    r.dq_s[j, s, lo : lo + HEAD_DIM, :] = dqt.astype(BF16)

            q = r.seen[:, 0:WIN]
            do = r.seen[:, z.vlo : z.vlo + WIN]
            for lo, hi, value in pair_back(s, keys, vals, q, do, j, keep):
                r.dkv[s, :, lo:hi] += value

            @pl.when(k > 0)
            def _():
                query_back_copy(c, s, j).start()

        each(nc - c - ((nc - 1 - c) // (nc - 1) if split else 0), one_block)

        @pl.when(last)
        def _():
            after_own()

    for s in range(seqs):
        out_grads(s, t, 0)
    def input_back(s):
        g2s.close(s)
        if split:

            @pl.when(c == 0)
            def _():
                far_copy(s).wait_recv()
                r.dkv[s] += r.kv[nc - 1, s].astype(F32)

        def add_dq(j):
            query_back_copy(j, s, j).wait_recv()
            r.dqt[s] += r.dq_r[j, s].astype(F32)

        each(c, add_dq, skip)
        r.dq[s, :, 0:hw] = jnp.transpose(r.dqt[s]) * (HEAD_DIM ** -0.5)
        r.dq[s, :, hw:WIN] = jnp.zeros((block, WIN - hw), F32)
        cos1, sin1 = r.cosine[...], r.sine[...]
        for j in range(WIN // LANES):
            x = r.dq[s, :, j * LANES : (j + 1) * LANES]
            r.qb[s, :, j * LANES : (j + 1) * LANES] = (x * cos1 - swap(x) * sin1).astype(BF16)
        for j in range(z.kvw // LANES):
            x = r.dkv[s, :, j * LANES : (j + 1) * LANES]
            keys = min(max(hw - j * LANES, 0), LANES)
            if keys > 0:
                turned = x * cos1 - swap(x) * sin1
                x = turned if keys == LANES else jnp.where(lanes_of(x.shape) < keys, turned, x)
            r.kvb[s, :, j * LANES : (j + 1) * LANES] = x.astype(BF16)
        r.g2[s] = (mm(r.qb[s], r.wqt[...]) + mm(r.kvb[s], r.wkvt[...])).astype(BF16)
        n1s.push_all(s)

    bgs.collect(0, out_grads)
    deltas(0)
    bgs.relay(1)

    @pl.when(outer)
    def _():
        for s in range(seqs):
            mls.push_all(s)

    back_seq(0, red_a.step2)
    bgs.collect(1, out_grads)
    deltas(1)

    @pl.when(inner)
    def _():
        for s in range(seqs):
            mls.push_all(s)

    @pl.when(c < nc - 1)
    def _():
        input_back(0)

    mls.join(0)
    back_seq(1, red_a.step3)
    mls.join(1)

    @pl.when(last)
    def _():
        input_back(0)

    input_back(1)
    red_a.step4()
    n1s.join(0)

    for which, dst in ((other, r.gb_s), (d, r.gb_o)):
        cols = pl.ds(pl.multiple_of(which * half, LANES), half)
        right = flat(r.nrm[:, :, cols])
        dst[0:hw, :] = mm(flat(r.qb[:, :, 0:hw]), right, TN).astype(BF16)
        dst[hw : 3 * hw, :] = mm(flat(r.kvb[...]), right, TN).astype(BF16)
        right = flat(r.bg[:, :, cols])
        dst[3 * hw : 4 * hw, :] = mm(flat(r.attl[:, :, 0:hw]), right, TN).astype(BF16)
    send_gb = remote(r.gb_s, r.gb_r, r.s_gb.at[0], r.s_gb.at[1], dp=other)
    send_gb.start()
    red_b = Sums(send_gb, r.gb_o, r.gb_r, r.gb_c, r.gb_t, r.s_gbc, r.s_gbg)
    red_b.pair()
    red_b.step1()
    n1s.join(1)

    outs = []

    def store(src, dst):
        cp = pltpu.make_async_copy(src, dst, r.s_loc.at[len(local) + len(outs)])
        cp.start()
        outs.append(cp)

    red_b.step2()
    for s in range(seqs):
        mlp = mls.total(s)
        r.res[s] = (r.middle[s] + vec(5, s) * mlp).astype(BF16)
        keep_sum(5, s, r.cot[s, span(t), :].astype(F32) * mlp)
    store(r.res, r.res_out)
    for s in range(seqs):
        grad1 = n1s.total(s)
        unit, rstd = norm_parts(r.tok[s, span(t), :].astype(F32))
        keep_sum(0, s, grad1)
        keep_sum(1, s, grad1 * unit)
        r.gtok[s] = r.midg[s] + norm_back(grad1, unit, rstd, vec(1, s))

    for k in range(1, nt):
        to = (t + k) % nt
        remote(r.msum.at[to], r.mt_r.at[t], r.s_mt.at[0, to], r.s_mt.at[1, t], tp=to).start()
    store(r.gtok, r.gtok_out)
    red_b.step3()
    red_b.step4()
    total = r.msum[t]
    for k in range(1, nt):
        fr = (t + k) % nt
        there = r.mt_r.at[fr]
        remote(there, there, r.s_mt.at[0, fr], r.s_mt.at[1, fr], tp=fr).wait_recv()
        total = total + r.mt_r[fr]
    r.md_s[...] = total
    send_md = remote(r.md_s, r.md_r, r.s_md.at[0], r.s_md.at[1], dp=other)
    send_md.start()
    r.mg[c, 0] = total
    send_md.wait()
    r.mg[c, 1] = r.md_r[...]

    def send_mg(k):
        to = (c + k) % nc
        remote(r.mg.at[c], r.mg.at[c], r.s_mc.at[0, to], r.s_mc.at[1, c], ctx=to).start()

    each(nc, send_mg, 1)
    red_a.take()
    store(r.ga_t, r.ga_out)
    red_b.take()
    store(r.gb_t, r.gb_out)

    def take_small(k):
        fr = (c + k) % nc
        for buf, sems in ((r.mg, r.s_mc), (r.emb, r.s_ec)):
            remote(buf.at[fr], buf.at[fr], sems.at[0, fr], sems.at[1, fr], ctx=fr).wait_recv()
            remote(buf.at[c], buf.at[c], sems.at[0, fr], sems.at[1, c], ctx=fr).wait_send()

    each(nc, take_small, 1)
    store(r.mg, r.mg_out)
    store(r.emb, r.emb_out)

    for cp in send_w:
        cp.wait_send()
    for s in range(seqs):
        for group in (toks, cots, n2s, bgs, brs, mls, n1s):
            group.close(s)
    for k in range(1, nt):
        to = (t + k) % nt
        remote(
            r.msum.at[to], r.mt_r.at[t], r.s_mt.at[0, to], r.s_mt.at[1, t], tp=to
        ).wait_send()

    def kv_sent(to):
        for s in range(seqs):

            def one(idx):
                mine = r.kv.at[c, s, span(idx), :]
                remote(
                    mine, mine, r.s_kv.at[to, s, idx], r.r_kv.at[c, s, idx], ctx=to
                ).wait_send()

            each(nt, one)

    each(nc, kv_sent, c + 1)

    def parts_sent(to):
        for s in range(seqs):
            query_back_copy(c, s, to).wait_send()

    each(nc - ((nc - 1 - c) // (nc - 1) if split else 0), parts_sent, c + 1)
    if split:

        @pl.when(last)
        def _():
            for s in range(seqs):
                far_copy(s).wait_send()

    def query_sent(to):
        for s in range(seqs):
            query_copy(c, s, to).wait_send()
            each(nt, lambda idx: grad_copy(c, s, idx, to).wait_send())
            stat_copy(r.lse, 0, c, s, to).wait_send()
            stat_copy(r.delta, 1, c, s, to).wait_send()

    each(c, query_sent, skip)
    for cp in outs:
        cp.wait()


def finish_kernel(z, *refs):
    ins, outs, refs = refs[:6], refs[6:15], refs[15:]
    held, stage, sems = refs[:6], refs[6:15], refs[15]
    hw = z.hw
    fetches = [
        pltpu.make_async_copy(src, dst, sems.at[i]) for i, (src, dst) in enumerate(zip(ins, held))
    ]
    for cp in fetches:
        cp.start()
    ga, gb, emb, mg, res, gtok = held
    copies = []

    def put(i, value):
        stage[i][...] = value
        cp = pltpu.make_async_copy(stage[i], outs[i], sems.at[6 + i])
        cp.start()
        copies.append(cp)

    def through(i, src):
        cp = pltpu.make_async_copy(src, outs[i], sems.at[6 + i])
        cp.start()
        copies.append(cp)

    fetches[0].wait()
    put(6, ga[:, 0 : z.ff].astype(F32))
    put(7, ga[:, z.ff : 2 * z.ff].astype(F32))
    fetches[1].wait()
    for i in range(4):
        put(2 + i, gb[i * hw : (i + 1) * hw, :].astype(F32))
    fetches[2].wait()
    fetches[3].wait()
    rest = mg[...].reshape(z.nc * 16, z.half)
    terms = []
    for _ in range(3):
        terms.append(rest.astype(BF16))
        rest = rest - terms[-1].astype(F32)
    terms = jnp.concatenate(terms, axis=0)
    row = lax.broadcasted_iota(jnp.int32, (8, z.half), 0)
    columns = []
    for k in range(z.thirds):
        left = []
        for c in range(z.nc):
            for d in range(2):
                one, two = emb[c, 2 * d : 2 * d + 1, :], emb[c, 2 * d + 1 : 2 * d + 2, :]
                left.append(
                    jnp.where(row == k, one, jnp.where(row == z.thirds + k, two, 0.0))
                )
        left = jnp.concatenate(left, axis=0).astype(BF16)
        columns.append(mm(jnp.concatenate([left] * 3, axis=0), terms, TN))
    put(8, jnp.concatenate(columns, axis=1))
    fetches[4].wait()
    through(0, res)
    fetches[5].wait()
    through(1, gtok)
    for cp in copies:
        cp.wait()


IN_NAMES = (
    "tok_in",
    "ts_in",
    "wq_in",
    "wk_in",
    "wv_in",
    "wo_in",
    "wu_in",
    "wd_in",
    "wm_in",
    "cot_in",
)
OUT_NAMES = ("res_out", "gtok_out", "ga_out", "gb_out", "emb_out", "mg_out")


def solution(mesh):
    def shards(tokens, steps, wq, wk, wv, wo, wu, wd, wm, cot):
        wq, wk, wv, wo = wq.T, wk.T, wv.T, wo.T
        z = Dims(mesh, tokens.shape, wq.shape, wu.shape, wm.shape)
        table = scratch_table(z)
        names = list(IN_NAMES) + list(OUT_NAMES) + list(table)
        hbm = pl.BlockSpec(memory_space=pl.ANY)
        smem = pl.BlockSpec(memory_space=pltpu.SMEM)
        own = (z.seqs, z.rows, z.width)
        shape = jax.ShapeDtypeStruct
        outs = pl.pallas_call(
            functools.partial(layer_kernel, z, names),
            out_shape=(
                shape(own, BF16),
                shape(own, F32),
                shape((z.half, z.wide), BF16),
                shape((z.heads_rows, z.half), BF16),
                shape((z.nc, 8, z.half), F32),
                shape((z.nc, 2, 8, z.half), F32),
            ),
            in_specs=[hbm, smem] + [hbm] * 8,
            out_specs=[hbm] * 6,
            scratch_shapes=list(table.values()),
            compiler_params=pltpu.CompilerParams(
                collective_id=0, has_side_effects=True, vmem_limit_bytes=VMEM_BYTES
            ),
            name="layer",
        )(tokens, steps.T, wq, wk, wv, wo, wu, wd, wm, cot)
        outs = outs[2:] + outs[:2]
        shapes = (
            (own, BF16),
            (own, F32),
            ((z.hw, z.half), F32),
            ((z.hw, z.half), F32),
            ((z.hw, z.half), F32),
            ((z.hw, z.half), F32),
            ((z.half, z.ff), F32),
            ((z.half, z.ff), F32),
            ((z.half, z.mcols), F32),
        )
        done = pl.pallas_call(
            functools.partial(finish_kernel, z),
            out_shape=tuple(shape(*o) for o in shapes),
            in_specs=[hbm] * 6,
            out_specs=[hbm] * 9,
            scratch_shapes=[pltpu.VMEM(o.shape, o.dtype) for o in outs]
            + [pltpu.VMEM(*o) for o in shapes]
            + [pltpu.SemaphoreType.DMA((15,))],
            compiler_params=pltpu.CompilerParams(vmem_limit_bytes=VMEM_BYTES),
            name="finish",
        )(*outs)
        return done[:2] + tuple(g.T for g in done[2:6]) + done[6:]

    rows = P("dp", ("ctx", "tp"), None)
    cols = P("dp", "tp")
    return jax.shard_map(
        shards,
        mesh=mesh,
        in_specs=(rows, P("dp", "ctx")) + (cols,) * 6 + (P("dp", None), rows),
        out_specs=(rows, rows) + (cols,) * 7,
        check_vma=False,
    )
```

```python
import functools
import math

import jax
import jax.numpy as jnp
from jax import lax
from jax.experimental import pallas as pl
from jax.experimental.pallas import tpu as pltpu
from jax.sharding import PartitionSpec as P

MESH = pl.DeviceIdType.MESH
HEAD_DIM = 64
WIN = 256
LANES = 128
EPS = 1e-06
NEG = -1e30
GELU_C = 0.7978845608028654
GELU_A = 0.044715
F32 = jnp.float32
BF16 = jnp.bfloat16
VMEM_BYTES = 62 * 1024 * 1024

NN = (((1,), (0,)), ((), ()))
NT = (((1,), (1,)), ((), ()))
TN = (((0,), (0,)), ((), ()))


def mm(a, b, dims=NN):
    return lax.dot_general(a, b, dims, preferred_element_type=F32)


def norm_parts(x):
    center = x - jnp.mean(x, axis=-1, keepdims=True)
    rstd = lax.rsqrt(jnp.mean(center * center, axis=-1, keepdims=True) + EPS)
    return center * rstd, rstd


def norm_back(grad, unit, rstd, scale):
    dn = grad * (1.0 + scale)
    return rstd * (
        dn
        - jnp.mean(dn, axis=-1, keepdims=True)
        - unit * jnp.mean(dn * unit, axis=-1, keepdims=True)
    )


def remote(src, dst, send, recv, **dev):
    return pltpu.make_async_remote_copy(
        src_ref=src, dst_ref=dst, send_sem=send, recv_sem=recv, device_id=dev, device_id_type=MESH
    )


def chunk_rows(count, devices):
    return 16 * -(-(count // 16) // devices)


class Dims:
    def __init__(self, mesh, tokens, query, up, mod):
        self.nc = mesh.shape["ctx"]
        self.nt = mesh.shape["tp"]
        self.seqs, self.rows, self.width = tokens
        self.block = self.rows * self.nt
        self.hw, self.half = query
        self.heads = self.hw // HEAD_DIM
        self.ff = up[1]
        self.mod = mod[1]
        self.kvw = 2 * self.hw
        self.vlo = self.kvw - WIN
        self.voff = self.hw - self.vlo
        self.wide = 2 * self.ff
        self.heads_rows = 4 * self.hw
        self.mcols = self.mod // self.nt
        self.thirds = self.mcols // self.half


def scratch_table(z):
    vm = lambda shape, dtype=BF16: pltpu.VMEM(shape, dtype)
    sem = lambda *shape: pltpu.SemaphoreType.DMA(shape)
    full = (z.seqs, z.block, z.width)
    own = (z.seqs, z.rows, z.width)
    pair = (z.seqs, 2, z.rows, z.width)
    return dict(
        tok=vm(full),
        cot=vm(full),
        wqt=vm((WIN, z.width)),
        wkvt=vm((z.kvw, z.width)),
        wot=vm((WIN, z.width)),
        wu=vm((z.width, z.ff)),
        wd=vm((z.width, z.ff)),
        wm=vm((z.half, z.mod)),
        emb_s=vm((8, z.half), F32),
        emb_r=vm((8, z.half), F32),
        emb=vm((z.nc, 8, z.half), F32),
        mod_s=vm((8, z.mod), F32),
        mod_r=vm((8, z.mod), F32),
        mod=vm((8, z.mod), F32),
        cosine=vm((z.block, LANES), F32),
        sine=vm((z.block, LANES), F32),
        nrm=vm(full),
        qd=vm((z.seqs, z.block, z.kvw)),
        kv=vm((z.nc, z.seqs, z.block, z.kvw)),
        vt=vm((WIN, z.block)),
        stat=vm((2, 8, z.block), F32),
        acc=vm((z.hw, z.block), F32),
        att=vm((z.seqs, z.hw, z.block), F32),
        attl=vm((z.seqs, z.block, WIN)),
        lse=vm((z.nc, z.seqs, 8, z.block), F32),
        delta=vm((z.nc, z.seqs, 8, z.block), F32),
        br=vm(full),
        br_m=vm(pair),
        br_r=vm(pair),
        branch=vm(own, F32),
        middle=vm(own, F32),
        n2=vm(full),
        act=vm((z.seqs, z.block, z.ff)),
        hgrad=vm((z.seqs, z.block, z.ff)),
        mgrad=vm(full),
        g2=vm(full),
        g2_m=vm(pair),
        g2_r=vm(pair),
        ml=vm(full),
        ml_m=vm(pair),
        ml_r=vm(pair),
        midg=vm(own, F32),
        bg=vm(full),
        seen=vm((z.block, z.kvw)),
        dot=vm((WIN, z.block)),
        dqt=vm((z.seqs, z.hw, z.block), F32),
        dq_s=vm((z.nc, z.seqs, z.hw, z.block)),
        dq_r=vm((z.nc, z.seqs, z.hw, z.block)),
        dq=vm((z.seqs, z.block, WIN), F32),
        dkv=vm((z.seqs, z.block, z.kvw), F32),
        qb=vm((z.seqs, z.block, WIN)),
        kvb=vm((z.seqs, z.block, z.kvw)),
        n1_m=vm(pair),
        n1_r=vm(pair),
        ga_s=vm((z.half, z.wide)),
        ga_o=vm((z.half, z.wide)),
        ga_r=vm((z.half, z.wide)),
        ga_c=vm((z.nc, chunk_rows(z.half, z.nc), z.wide)),
        ga_t=vm((z.half, z.wide)),
        gb_s=vm((z.heads_rows, z.half)),
        gb_o=vm((z.heads_rows, z.half)),
        gb_r=vm((z.heads_rows, z.half)),
        gb_c=vm((z.nc, chunk_rows(z.heads_rows, z.nc), z.half)),
        gb_t=vm((z.heads_rows, z.half)),
        msum=vm((z.nt, 8, z.half), F32),
        mt_r=vm((z.nt, 8, z.half), F32),
        md_s=vm((8, z.half), F32),
        md_r=vm((8, z.half), F32),
        mg=vm((z.nc, 2, 8, z.half), F32),
        res=vm(own),
        gtok=vm(own, F32),
        s_loc=sem(16),
        s_w=sem(2, 6),
        s_e=sem(2),
        s_ec=sem(z.nc),
        s_all=sem(3),
        s_m=sem(2, 2),
        s_tok=sem(z.seqs),
        r_tok=sem(z.seqs, z.nt),
        s_cot=sem(z.seqs),
        r_cot=sem(z.seqs, z.nt),
        s_kv=sem(z.nc),
        r_kv=sem(z.nc, z.seqs),
        s_br=sem(z.seqs),
        m_br=sem(z.seqs, 2),
        r_br=sem(z.seqs, 2),
        s_n2=sem(z.seqs),
        r_n2=sem(z.seqs, z.nt),
        s_g2=sem(z.seqs),
        m_g2=sem(z.seqs, 2),
        r_g2=sem(z.seqs, 2),
        s_ml=sem(z.seqs),
        m_ml=sem(z.seqs, 2),
        r_ml=sem(z.seqs, 2),
        s_bg=sem(z.seqs),
        r_bg=sem(z.seqs, z.nt),
        s_q=sem(z.nc),
        r_q=sem(z.nc, z.seqs),
        s_do=sem(z.nc),
        r_do=sem(z.nc, z.seqs),
        s_st=sem(2, z.nc),
        r_st=sem(2, z.nc, z.seqs),
        s_dq=sem(z.nc),
        r_dq=sem(z.nc, z.seqs),
        s_n1=sem(z.seqs),
        m_n1=sem(z.seqs, 2),
        r_n1=sem(z.seqs, 2),
        s_ga=sem(2),
        s_gac=sem(12) if z.nc == 4 else sem(2, z.nc),
        s_gag=sem(2) if z.nc == 4 else sem(2, z.nc),
        s_gb=sem(2),
        s_gbc=sem(12) if z.nc == 4 else sem(2, z.nc),
        s_gbg=sem(2) if z.nc == 4 else sem(2, z.nc),
        s_mt=sem(z.nt),
        s_md=sem(2),
        s_mc=sem(z.nc),
    )


class Box:
    pass


def layer_kernel(z, names, *refs):
    r = Box()
    for name, ref in zip(names, refs):
        setattr(r, name, ref)
    d, c, t = lax.axis_index("dp"), lax.axis_index("ctx"), lax.axis_index("tp")
    other = 1 - d
    nt, nc, rows, block, width, hw = z.nt, z.nc, z.rows, z.block, z.width, z.hw
    seqs, half = z.seqs, z.half

    def each(count, body, first=0):
        def step(i, carry):
            body(i)
            return carry

        lax.fori_loop(first, count, step, 0)

    def span(idx):
        return pl.ds(pl.multiple_of(idx * rows, rows), rows)

    def slot(ref, idx):
        return ref.at[:, span(idx), :]

    def piece(ref, s, idx):
        return ref.at[s, span(idx), :]

    def flat(x):
        return x.reshape(x.shape[0] * x.shape[1], x.shape[2])

    def lanes_of(shape, axis=1):
        return lax.broadcasted_iota(jnp.int32, shape, axis)

    local = []

    def fetch(src, dst):
        cp = pltpu.make_async_copy(src, dst, r.s_loc.at[len(local)])
        cp.start()
        local.append(cp)
        return cp

    my_half = pl.ds(pl.multiple_of(d * half, LANES), half)
    weights = [
        (r.wq_in, r.wqt.at[0:hw, my_half]),
        (r.wk_in, r.wkvt.at[0:hw, my_half]),
        (r.wv_in, r.wkvt.at[hw : z.kvw, my_half]),
        (r.wo_in, r.wot.at[z.voff : z.voff + hw, my_half]),
        (r.wu_in, r.wu.at[my_half, :]),
        (r.wd_in, r.wd.at[my_half, :]),
    ]
    first_cols = 2 * width
    cp_tok = fetch(r.tok_in, slot(r.tok, t))
    cp_wm1 = fetch(r.wm_in.at[:, 0:first_cols], r.wm.at[:, 0:first_cols])
    cp_w = [fetch(src, dst) for src, dst in weights]
    cp_wm2 = fetch(r.wm_in.at[:, first_cols : z.mod], r.wm.at[:, first_cols : z.mod])
    cp_cot = fetch(r.cot_in, slot(r.cot, t))

    r.wqt[hw:WIN, :] = jnp.zeros((WIN - hw, width), BF16)
    r.wot[0 : z.voff, :] = jnp.zeros((z.voff, width), BF16)

    bar = pltpu.get_barrier_semaphore()
    pl.semaphore_signal(bar, inc=1, device_id={"dp": other}, device_id_type=MESH)
    for k in range(1, nt):
        pl.semaphore_signal(bar, inc=1, device_id={"tp": (t + k) % nt}, device_id_type=MESH)

    def greet(k):
        pl.semaphore_signal(bar, inc=1, device_id={"ctx": (c + k) % nc}, device_id_type=MESH)

    each(nc, greet, 1)

    row8 = lanes_of((8, half), 0)
    step_of = jnp.where(
        row8 % 2 == 0, r.ts_in[0, 0].astype(F32), r.ts_in[0, 1].astype(F32)
    )
    angle = step_of * jnp.exp(
        lanes_of((8, half)).astype(F32) * (-math.log(10000.0) / half)
    )
    sin_e, cos_e = jnp.sin(angle), jnp.cos(angle)

    def silu_low(v):
        return (v / (1.0 + jnp.exp(-v))).astype(BF16).astype(F32)

    sin_e, cos_e = silu_low(sin_e), silu_low(cos_e)
    first = d == 0
    own_half = jnp.where(row8 < 2, jnp.where(first, sin_e, cos_e), 0.0)
    r.emb_s[...] = jnp.where(
        (row8 >= 2) & (row8 < 4), jnp.where(first, cos_e, sin_e), 0.0
    )
    pl.semaphore_wait(bar, 1 + (nt - 1) + (nc - 1))

    side = t // 2
    mate = t + 1 - 2 * (t % 2)
    cross = 2 - side
    outer = t % 3 == 0
    inner = t % 3 != 0

    def peer(i):
        far = i // 2
        return (1 - far) * (t + i * (1 - 2 * (t % 2))) + far * ((1 - side) * i + side * (3 - i))

    class Gather:
        def __init__(self, buf, send, recv):
            self.buf, self.sems, self.recv = buf, send, recv

        def copy(self, src, s, idx, to):
            return remote(
                src, piece(self.buf, s, idx), self.sems.at[s], self.recv.at[s, idx], tp=to
            )

        def open(self, src, s):
            self.copy(src, s, t, cross).start()
            self.copy(src, s, t, mate).start()

        def wait(self, s, idx):
            self.copy(piece(self.buf, s, idx), s, idx, mate).wait_recv()

        def relay(self, s):
            @pl.when(inner)
            def _():
                def one(i):
                    idx = peer(i)
                    self.wait(s, idx)
                    self.copy(piece(self.buf, s, idx), s, idx, mate).start()

                each(4, one, 2)

        def collect(self, s, work):
            def one(i):
                idx = peer(i)

                @pl.when(outer | (i == 1))
                def _():
                    self.wait(s, idx)

                if work is not None:
                    work(s, idx, i)

            each(4, one, 1)

        def close(self, s):
            def sent(count):
                all_sent = self.buf.at[s, 0 : count * rows, :]
                remote(all_sent, all_sent, self.sems.at[s], self.recv.at[s, t], tp=mate).wait_send()

            @pl.when(outer)
            def _():
                sent(2)

            @pl.when(inner)
            def _():
                sent(4)

    class Scatter:
        def __init__(self, part, merge, got, send, msem, gsem):
            self.part, self.merge, self.got = part, merge, got
            self.sems, self.msem, self.gsem = send, msem, gsem

        def to_got(self, s, idx, k):
            return remote(
                piece(self.part, s, idx),
                self.got.at[s, k],
                self.sems.at[s],
                self.gsem.at[s, k],
                tp=idx,
            )

        def to_merge(self, s, idx, i):
            return remote(
                piece(self.part, s, idx),
                self.merge.at[s, i - 2],
                self.sems.at[s],
                self.msem.at[s, i - 2],
                tp=mate,
            )

        def push(self, s, idx, i):
            @pl.when(i == 1)
            def _():
                self.to_got(s, idx, 0).start()

            @pl.when((i > 1) & outer)
            def _():
                self.to_merge(s, idx, i).start()

        def push_all(self, s):
            for i in (3, 2):
                self.push(s, peer(i), i)
            self.push(s, mate, 1)

        def join(self, s):
            @pl.when(inner)
            def _():
                def one(k):
                    i = 3 - k
                    idx = peer(i)
                    self.to_merge(s, idx, i).wait_recv()
                    at = span(idx)
                    self.part[s, at, :] = (
                        self.part[s, at, :].astype(F32) + self.merge[s, i - 2].astype(F32)
                    ).astype(BF16)
                    self.to_got(s, idx, 1).start()

                each(2, one)

        def total(self, s):
            for k in range(2):
                self.to_got(s, mate, k).wait_recv()
            return (
                self.part[s, span(t), :].astype(F32)
                + self.got[s, 0].astype(F32)
                + self.got[s, 1].astype(F32)
            )

        def close(self, s):
            all_sent = self.part.at[s, 0 : 3 * rows, :]
            remote(all_sent, all_sent, self.sems.at[s], self.gsem.at[s, 0], tp=mate).wait_send()

    toks = Gather(r.tok, r.s_tok, r.r_tok)
    cots = Gather(r.cot, r.s_cot, r.r_cot)
    n2s = Gather(r.n2, r.s_n2, r.r_n2)
    bgs = Gather(r.bg, r.s_bg, r.r_bg)
    brs = Scatter(r.br, r.br_m, r.br_r, r.s_br, r.m_br, r.r_br)
    g2s = Scatter(r.g2, r.g2_m, r.g2_r, r.s_g2, r.m_g2, r.r_g2)
    mls = Scatter(r.ml, r.ml_m, r.ml_r, r.s_ml, r.m_ml, r.r_ml)
    n1s = Scatter(r.g2, r.n1_m, r.n1_r, r.s_n1, r.m_n1, r.r_n1)

    for s in range(seqs):
        toks.open(r.tok_in.at[s], s)

    @pl.when(outer)
    def _():
        for s in range(seqs):
            cots.open(r.cot_in.at[s], s)

    send_emb = remote(r.emb_s, r.emb_r, r.s_e.at[0], r.s_e.at[1], dp=other)
    send_emb.start()
    send_w = [
        remote(src, dst, r.s_w.at[0, i], r.s_w.at[1, i], dp=other)
        for i, (src, dst) in enumerate(weights)
    ]
    for cp in send_w[:3]:
        cp.start()

    send_emb.wait()
    emb4 = own_half + r.emb_r[...]
    r.emb[pl.ds(c, 1)] = emb4[None]
    emb_low = emb4.astype(BF16)

    def mod_part(lo, hi, which, ready):
        ready.wait()
        r.mod_s[:, lo:hi] = mm(emb_low, r.wm[:, lo:hi])
        cp = remote(
            r.mod_s.at[:, lo:hi], r.mod_r.at[:, lo:hi], r.s_m.at[0, which], r.s_m.at[1, which], dp=other
        )
        cp.start()
        return cp

    def mod_take(lo, hi, cp):
        cp.wait()
        for s in range(seqs):
            r.mod[s : s + 1, lo:hi] = r.mod_s[s : s + 1, lo:hi] + r.mod_r[s + 2 : s + 3, lo:hi]

    def vec(slot_idx, s):
        lo = slot_idx * width
        return r.mod[s : s + 1, lo : lo + width]

    mod1 = mod_part(0, first_cols, 0, cp_wm1)
    for cp in send_w[3:]:
        cp.start()

    def send_ctx_emb(k):
        to = (c + k) % nc
        remote(r.emb.at[c], r.emb.at[c], r.s_all.at[2], r.s_ec.at[c], ctx=to).start()

    each(nc, send_ctx_emb, 1)

    place = (c * block + lanes_of((block, LANES), 0)).astype(F32)
    pair_of = (lanes_of((block, LANES)) % (HEAD_DIM // 2)).astype(F32)
    turn = place * jnp.exp(pair_of * (-2.0 * math.log(10000.0) / HEAD_DIM))
    low_lane = lanes_of((block, LANES)) % HEAD_DIM < HEAD_DIM // 2
    r.cosine[...] = jnp.cos(turn)
    r.sine[...] = jnp.where(low_lane, -jnp.sin(turn), jnp.sin(turn))

    def swap(x):
        low = lanes_of(x.shape) % HEAD_DIM < HEAD_DIM // 2
        return jnp.where(
            low,
            pltpu.roll(x, LANES - HEAD_DIM // 2, 1),
            pltpu.roll(x, HEAD_DIM // 2, 1),
        )

    for i in range(3):
        cp_w[i].wait()
        send_w[i].wait_recv()
    mod_take(0, first_cols, mod1)

    def make_qkv(s, idx, i):
        at = span(idx)
        unit, _ = norm_parts(r.tok[s, at, :].astype(F32))
        low = (unit * (1.0 + vec(1, s)) + vec(0, s)).astype(BF16)
        r.nrm[s, at, :] = low
        cos1, sin1 = r.cosine[at, :], r.sine[at, :]
        q_pre = mm(low, r.wqt[...], NT)
        kv_pre = mm(low, r.wkvt[...], NT)
        for j in range(WIN // LANES):
            x = q_pre[:, j * LANES : (j + 1) * LANES]
            x = (x * cos1 + swap(x) * sin1) * (HEAD_DIM ** -0.5)
            r.qd[s, at, j * LANES : (j + 1) * LANES] = x.astype(BF16)
        for j in range(z.kvw // LANES):
            x = kv_pre[:, j * LANES : (j + 1) * LANES]
            keys = min(max(hw - j * LANES, 0), LANES)
            if keys > 0:
                turned = x * cos1 + swap(x) * sin1
                x = turned if keys == LANES else jnp.where(lanes_of(x.shape) < keys, turned, x)
            r.kv[c, s, at, j * LANES : (j + 1) * LANES] = x.astype(BF16)

        def send_kv(to):
            mine = r.kv.at[c, s, at, :]
            remote(mine, mine, r.s_kv.at[to], r.r_kv.at[c, s], ctx=to).start()

        each(nc, send_kv, c + 1)

    cp_tok.wait()
    for s in range(seqs):
        make_qkv(s, t, 0)
    mod2 = mod_part(first_cols, z.mod, 1, cp_wm2)
    for s in range(seqs):
        toks.relay(s)
        toks.collect(s, make_qkv)

    @pl.when(inner)
    def _():
        for s in range(seqs):
            cots.open(r.cot_in.at[s], s)

    cp_cot.wait()
    mod_take(first_cols, z.mod, mod2)
    for i in range(3, 6):
        cp_w[i].wait()
        send_w[i].wait_recv()

    eye = (lanes_of((WIN, WIN), 0) == lanes_of((WIN, WIN))).astype(BF16)

    def head_of(x, h, off=0):
        lane = lanes_of(x.shape)
        lo = off + h * HEAD_DIM
        return jnp.where((lane >= lo) & (lane < lo + HEAD_DIM), x, jnp.zeros_like(x))

    def attend_seq(s):
        r.stat[0] = jnp.full((8, block), NEG, F32)
        r.stat[1] = jnp.zeros((8, block), F32)
        r.acc[...] = jnp.zeros((hw, block), F32)
        q = r.qd[s, :, 0:WIN]

        def one_block(back):
            j = c - back

            @pl.when(back > 0)
            def _():
                there = r.kv.at[j, s]
                remote(there, there, r.s_kv.at[j], r.r_kv.at[j, s], ctx=j).wait_recv()

            keys = r.kv[j, s, :, 0:WIN]
            r.vt[...] = mm(eye, r.kv[j, s, :, z.vlo : z.vlo + WIN], NT).astype(BF16)
            for h in range(z.heads):
                scores = mm(keys, head_of(q, h), NT)
                old = r.stat[0, h : h + 1, :]
                top = jnp.maximum(old, jnp.max(scores, axis=0, keepdims=True))
                prob = jnp.exp(scores - top)
                fade = jnp.exp(old - top)
                r.stat[0, h : h + 1, :] = top
                r.stat[1, h : h + 1, :] = r.stat[1, h : h + 1, :] * fade + jnp.sum(
                    prob, axis=0, keepdims=True
                )
                lo = h * HEAD_DIM
                vt = r.vt[z.voff + lo : z.voff + lo + HEAD_DIM, :]
                r.acc[lo : lo + HEAD_DIM, :] = r.acc[lo : lo + HEAD_DIM, :] * fade + mm(
                    vt, prob.astype(BF16)
                )

        each(c + 1, one_block)
        for h in range(z.heads):
            lo = h * HEAD_DIM
            denom = r.stat[1, h : h + 1, :]
            r.lse[c, s, h : h + 1, :] = r.stat[0, h : h + 1, :] + jnp.log(denom)
            r.att[s, lo : lo + HEAD_DIM, :] = r.acc[lo : lo + HEAD_DIM, :] / denom
        low = jnp.transpose(r.att[s]).astype(BF16)
        r.attl[s, :, 0:hw] = low
        r.attl[s, :, hw:WIN] = jnp.zeros((block, WIN - hw), BF16)
        r.br[s] = mm(low, r.wot[z.voff : z.voff + hw, :]).astype(BF16)
        brs.push_all(s)

    each(seqs, attend_seq)

    split = nc == 4
    last = c == nc - 1
    skip = c // (nc - 1) if split else 0

    def query_copy(j, s, to):
        return remote(
            r.qd.at[s, :, 0:LANES],
            r.kv.at[j, s, :, 0:LANES],
            r.s_q.at[to],
            r.r_q.at[j, s],
            ctx=to,
        )

    def stat_copy(buf, which, j, s, to):
        return remote(
            buf.at[j, s], buf.at[j, s], r.s_st.at[which, to], r.r_st.at[which, j, s], ctx=to
        )

    def send_queries(to):
        for s in range(seqs):
            query_copy(c, s, to).start()
            stat_copy(r.lse, 0, c, s, to).start()

    each(c, send_queries, skip)
    for s in range(seqs):
        cots.relay(s)
    def middle_rows(s):
        branch = brs.total(s)
        r.branch[s] = branch
        middle = r.tok[s, span(t), :].astype(F32) + vec(2, s) * branch
        r.middle[s] = middle
        unit, _ = norm_parts(middle)
        r.n2[s, span(t), :] = (unit * (1.0 + vec(4, s)) + vec(3, s)).astype(BF16)
        n2s.open(piece(r.n2, s, t), s)

    brs.join(0)
    middle_rows(0)
    brs.join(1)
    n2s.relay(0)
    middle_rows(1)

    def feed(s, idx, i):
        at = span(idx)
        hid = mm(r.n2[s, at, :], r.wu[...])
        square = hid * hid
        tanh = jnp.tanh(GELU_C * (hid + GELU_A * (hid * square)))
        r.act[s, at, :] = (0.5 * hid * (1.0 + tanh)).astype(BF16)
        slope = 0.5 * (1.0 + tanh) + 0.5 * hid * (1.0 - tanh * tanh) * (
            GELU_C * (1.0 + 3.0 * GELU_A * square)
        )
        low = (vec(5, s) * r.cot[s, at, :].astype(F32)).astype(BF16)
        r.mgrad[s, at, :] = low
        hgrad = (slope * mm(low, r.wd[...])).astype(BF16)
        r.hgrad[s, at, :] = hgrad
        r.g2[s, at, :] = mm(hgrad, r.wu[...], NT).astype(BF16)
        g2s.push(s, idx, i)

    for s in range(seqs):
        feed(s, t, 0)
    for s in range(seqs):
        cots.collect(s, None)
        if s > 0:
            n2s.relay(s)
        n2s.collect(s, feed)
    g2s.join(0)

    class Reduction:
        def __init__(self, got, mine, theirs, buf, total, sems, sems_all):
            self.got, self.mine, self.theirs, self.buf, self.total = got, mine, theirs, buf, total
            self.sems, self.sems_all = sems, sems_all
            self.chunk = buf.shape[1]
            self.owners = mine.shape[0] // self.chunk

        def rows(self, o):
            return pl.ds(pl.multiple_of(o * self.chunk, 16), self.chunk)

        def part(self, o):
            return remote(
                self.mine.at[self.rows(o), :],
                self.buf.at[c],
                self.sems.at[0, o],
                self.sems.at[1, c],
                ctx=o,
            )

        def share(self, owner, to):
            here = self.total.at[self.rows(owner), :]
            return remote(here, here, self.sems_all.at[0, to], self.sems_all.at[1, owner], ctx=to)

        def to_owners(self, body):
            def one(k):
                o = (c + k) % nc

                @pl.when(o < self.owners)
                def _():
                    body(o)

            each(nc, one, 1)

        def as_owner(self, body):
            @pl.when(c < self.owners)
            def _():
                body()

        def pair(self):
            self.got.wait()
            self.mine[...] = (self.mine[...].astype(F32) + self.theirs[...].astype(F32)).astype(
                BF16
            )

        def step1(self):
            self.to_owners(lambda o: self.part(o).start())

        def step2(self):
            pass

        def step4(self):
            pass

        def step3(self):
            def body():
                def add(k, acc):
                    fr = (c + k) % nc
                    there = self.buf.at[fr]
                    remote(
                        there, there, self.sems.at[0, fr], self.sems.at[1, fr], ctx=fr
                    ).wait_recv()
                    return acc + self.buf[fr].astype(F32)

                acc = self.mine[self.rows(c), :].astype(F32)
                if nc <= 4:
                    for k in range(1, nc):
                        acc = add(k, acc)
                else:
                    acc = lax.fori_loop(1, nc, add, acc)
                self.total[self.rows(c), :] = acc.astype(BF16)
                each(nc, lambda k: self.share(c, (c + k) % nc).start(), 1)

            self.as_owner(body)

        def take(self):
            def one(o):
                self.share(o, o).wait_recv()
                self.part(o).wait_send()

            self.to_owners(one)
            self.as_owner(
                lambda: each(nc, lambda k: self.share(c, (c + k) % nc).wait_send(), 1)
            )

    class Square:
        def __init__(self, got, mine, theirs, buf, total, sems, sems_all):
            self.got, self.mine, self.theirs, self.buf, self.total = got, mine, theirs, buf, total
            self.sems, self.sems_all = sems, sems_all
            self.part = buf.shape[1] // 2
            by_x = c + 1 - 2 * (c % 2)
            by_y = (c + 2) % 4
            self.near = (by_x, by_y)
            self.next = (by_y, by_x)
            self.far = 3 - c

        def rows(self, o, h):
            return pl.ds(pl.multiple_of((2 * o + h) * self.part, 16), self.part)

        def first(self, h, k):
            o = (self.near[h], self.far)[k]
            return remote(
                self.mine.at[self.rows(o, h), :],
                self.buf.at[2 * h + k, 0 : self.part, :],
                self.sems_all.at[0],
                self.sems.at[2 * h + k],
                ctx=self.near[h],
            )

        def second(self, h):
            o = self.next[h]
            return remote(
                self.mine.at[self.rows(o, h), :],
                self.buf.at[2 * h, self.part : 2 * self.part, :],
                self.sems_all.at[0],
                self.sems.at[4 + h],
                ctx=o,
            )

        def spread(self, h, o, to, which, landed):
            at = self.total.at[self.rows(landed, h), :]
            src = self.total.at[self.rows(o, h), :]
            return remote(src, at, self.sems_all.at[1], self.sems.at[which], ctx=to)

        def third(self, h, landed):
            return self.spread(h, landed, self.next[h], 6 + h, landed)

        def fourth(self, h, k, landed):
            return self.spread(h, landed, self.near[h], 8 + 2 * h + k, landed)

        def pair(self):
            self.got.wait()
            self.mine[...] = (self.mine[...].astype(F32) + self.theirs[...].astype(F32)).astype(
                BF16
            )

        def step1(self):
            for k in (1, 0):
                for h in range(2):
                    self.first(h, k).start()

        def step2(self):
            for k in (1, 0):
                for h in range(2):
                    self.first(h, k).wait_recv()
                    at = self.rows((c, self.next[h])[k], h)
                    self.mine[at, :] = (
                        self.mine[at, :].astype(F32)
                        + self.buf[2 * h + k, 0 : self.part, :].astype(F32)
                    ).astype(BF16)
                    if k == 1:
                        self.second(h).start()

        def step3(self):
            for h in range(2):
                self.second(h).wait_recv()
                at = self.rows(c, h)
                self.total[at, :] = (
                    self.mine[at, :].astype(F32)
                    + self.buf[2 * h, self.part : 2 * self.part, :].astype(F32)
                ).astype(BF16)
                self.third(h, c).start()

        def step4(self):
            for h in range(2):
                self.fourth(h, 0, c).start()
            for h in range(2):
                self.third(h, self.next[h]).wait_recv()
                self.fourth(h, 1, self.next[h]).start()

        def take(self):
            for h in range(2):
                self.fourth(h, 0, self.near[h]).wait_recv()
                self.fourth(h, 1, self.far).wait_recv()
            for k, ref in enumerate((self.mine, self.total)):
                part = ref.at[0 : 6 * self.part, :]
                remote(part, part, self.sems_all.at[k], self.sems.at[0], ctx=self.far).wait_send()

    Sums = Square if nc == 4 else Reduction

    r.msum[...] = jnp.zeros((nt, 8, half), F32)

    def keep_sum(slot_idx, s, value):
        value = jnp.sum(value, axis=0, keepdims=True)
        for k in range(width // half):
            to, row = divmod(slot_idx * (width // half) + k, z.thirds)
            row = s * z.thirds + row
            r.msum[to, row : row + 1, :] = value[:, k * half : (k + 1) * half]

    def middle_back(s):
        grad2 = g2s.total(s)
        unit, rstd = norm_parts(r.middle[s])
        mid_grad = r.cot[s, span(t), :].astype(F32) + norm_back(grad2, unit, rstd, vec(4, s))
        r.midg[s] = mid_grad
        r.bg[s, span(t), :] = (vec(2, s) * mid_grad).astype(BF16)
        bgs.open(piece(r.bg, s, t), s)
        keep_sum(3, s, grad2)
        keep_sum(4, s, grad2 * unit)
        keep_sum(2, s, mid_grad * r.branch[s])

    middle_back(0)

    def pair_grads(lhs, rhs, mine, sent, lo, hi):
        right = flat(rhs[...])
        for which, dst in ((other, sent), (d, mine)):
            cols = pl.ds(pl.multiple_of(which * half, half), half)
            left = flat(lhs[:, :, cols])
            dst[:, lo:hi] = mm(left, right, TN).astype(BF16)

    pair_grads(r.mgrad, r.act, r.ga_o, r.ga_s, z.ff, 2 * z.ff)
    pair_grads(r.n2, r.hgrad, r.ga_o, r.ga_s, 0, z.ff)
    send_ga = remote(r.ga_s, r.ga_r, r.s_ga.at[0], r.s_ga.at[1], dp=other)
    send_ga.start()
    g2s.join(1)
    bgs.relay(0)
    red_a = Sums(send_ga, r.ga_o, r.ga_r, r.ga_c, r.ga_t, r.s_gac, r.s_gag)
    red_a.pair()
    red_a.step1()
    middle_back(1)
    for s in range(seqs):
        r.ml[s] = mm(r.act[s], r.wd[...], NT).astype(BF16)

    def grad_copy(j, s, idx, to):
        at = span(idx)
        return remote(
            r.qd.at[s, at, LANES : z.kvw],
            r.kv.at[j, s, at, LANES : z.kvw],
            r.s_do.at[to],
            r.r_do.at[j, s],
            ctx=to,
        )

    def out_grads(s, idx, i):
        at = span(idx)
        do = mm(r.bg[s, at, :], r.wot[...], NT).astype(BF16)
        over = WIN - z.vlo
        r.qd[s, at, z.vlo : WIN] = r.qd[s, at, z.vlo : WIN] + do[:, 0:over]
        r.qd[s, at, WIN : z.kvw] = do[:, over:WIN]
        each(c, lambda to: grad_copy(c, s, idx, to).start(), skip)

    def deltas(s):
        r.dot[...] = mm(eye, r.qd[s, :, z.vlo : z.vlo + WIN], NT).astype(BF16)
        for h in range(z.heads):
            lo = h * HEAD_DIM
            r.delta[c, s, h : h + 1, :] = jnp.sum(
                r.dot[z.voff + lo : z.voff + lo + HEAD_DIM, :].astype(F32)
                * r.att[s, lo : lo + HEAD_DIM, :],
                axis=0,
                keepdims=True,
            )
        each(c, lambda to: stat_copy(r.delta, 1, c, s, to).start(), skip)

    def query_back_copy(j, s, to):
        return remote(
            r.dq_s.at[to, s], r.dq_r.at[j, s], r.s_dq.at[to], r.r_dq.at[j, s], ctx=to
        )

    over = WIN - z.vlo

    def pair_back(s, keys, vals, q, do, j, keep):
        dk = jnp.zeros((block, WIN), F32)
        dv = jnp.zeros((block, WIN), F32)
        for h in range(z.heads):
            lo = h * HEAD_DIM
            qh = head_of(q, h)
            doh = head_of(do, h, z.voff)
            prob = jnp.exp(mm(keys, qh, NT) - r.lse[j, s, h : h + 1, :])
            dprob = mm(vals, doh, NT)
            dsc = (prob * (dprob - r.delta[j, s, h : h + 1, :])).astype(BF16)
            dv = dv + mm(prob.astype(BF16), doh)
            dk = dk + mm(dsc, qh)
            keep(lo, mm(r.vt[lo : lo + HEAD_DIM, :], dsc))
        return (
            (0, z.vlo, dk[:, 0 : z.vlo]),
            (z.vlo, WIN, dk[:, z.vlo : WIN] + dv[:, 0:over]),
            (WIN, z.kvw, dv[:, over:WIN]),
        )

    def far_copy(s):
        return remote(
            r.kv.at[0, s], r.kv.at[nc - 1, s], r.s_q.at[0], r.r_q.at[nc - 1, s], ctx=0
        )

    def back_seq(s, after_own):
        r.dkv[s] = jnp.zeros((block, z.kvw), F32)
        r.dqt[s] = jnp.zeros((hw, block), F32)
        if split:

            @pl.when(last)
            def _():
                keys = r.kv[0, s, :, 0:WIN]
                vals = r.kv[0, s, :, z.vlo : z.vlo + WIN]
                r.vt[...] = mm(eye, keys, NT).astype(BF16)

                def keep(lo, dqt):
                    r.dqt[s, lo : lo + HEAD_DIM, :] += dqt

                q = r.qd[s, :, 0:WIN]
                do = r.qd[s, :, z.vlo : z.vlo + WIN]
                for lo, hi, value in pair_back(s, keys, vals, q, do, c, keep):
                    r.kv[0, s, :, lo:hi] = value.astype(BF16)
                far_copy(s).start()

        keys = r.kv[c, s, :, 0:WIN]
        vals = r.kv[c, s, :, z.vlo : z.vlo + WIN]
        r.vt[...] = mm(eye, keys, NT).astype(BF16)

        def one_block(k):
            j = c + k

            @pl.when(k == 0)
            def _():
                r.seen[...] = r.qd[s]

            @pl.when(k == 1)
            def _():
                after_own()

            @pl.when(k > 0)
            def _():
                query_copy(j, s, j).wait_recv()
                there = r.kv.at[j, s, :, LANES : z.kvw]
                remote(there, there, r.s_do.at[j], r.r_do.at[j, s], ctx=j).wait_recv()
                stat_copy(r.lse, 0, j, s, j).wait_recv()
                stat_copy(r.delta, 1, j, s, j).wait_recv()
                r.seen[...] = r.kv[j, s]

            def keep(lo, dqt):
                @pl.when(k == 0)
                def _():
                    r.dqt[s, lo : lo + HEAD_DIM, :] += dqt

                @pl.when(k > 0)
                def _():
                    r.dq_s[j, s, lo : lo + HEAD_DIM, :] = dqt.astype(BF16)

            q = r.seen[:, 0:WIN]
            do = r.seen[:, z.vlo : z.vlo + WIN]
            for lo, hi, value in pair_back(s, keys, vals, q, do, j, keep):
                r.dkv[s, :, lo:hi] += value

            @pl.when(k > 0)
            def _():
                query_back_copy(c, s, j).start()

        each(nc - c - ((nc - 1 - c) // (nc - 1) if split else 0), one_block)

        @pl.when(last)
        def _():
            after_own()

    for s in range(seqs):
        out_grads(s, t, 0)
    def input_back(s):
        g2s.close(s)
        if split:

            @pl.when(c == 0)
            def _():
                far_copy(s).wait_recv()
                r.dkv[s] += r.kv[nc - 1, s].astype(F32)

        def add_dq(j):
            query_back_copy(j, s, j).wait_recv()
            r.dqt[s] += r.dq_r[j, s].astype(F32)

        each(c, add_dq, skip)
        r.dq[s, :, 0:hw] = jnp.transpose(r.dqt[s]) * (HEAD_DIM ** -0.5)
        r.dq[s, :, hw:WIN] = jnp.zeros((block, WIN - hw), F32)
        cos1, sin1 = r.cosine[...], r.sine[...]
        for j in range(WIN // LANES):
            x = r.dq[s, :, j * LANES : (j + 1) * LANES]
            r.qb[s, :, j * LANES : (j + 1) * LANES] = (x * cos1 - swap(x) * sin1).astype(BF16)
        for j in range(z.kvw // LANES):
            x = r.dkv[s, :, j * LANES : (j + 1) * LANES]
            keys = min(max(hw - j * LANES, 0), LANES)
            if keys > 0:
                turned = x * cos1 - swap(x) * sin1
                x = turned if keys == LANES else jnp.where(lanes_of(x.shape) < keys, turned, x)
            r.kvb[s, :, j * LANES : (j + 1) * LANES] = x.astype(BF16)
        r.g2[s] = (mm(r.qb[s], r.wqt[...]) + mm(r.kvb[s], r.wkvt[...])).astype(BF16)
        n1s.push_all(s)

    bgs.collect(0, out_grads)
    deltas(0)
    bgs.relay(1)

    @pl.when(outer)
    def _():
        for s in range(seqs):
            mls.push_all(s)

    back_seq(0, red_a.step2)
    bgs.collect(1, out_grads)
    deltas(1)

    @pl.when(inner)
    def _():
        for s in range(seqs):
            mls.push_all(s)

    @pl.when(c < nc - 1)
    def _():
        input_back(0)

    mls.join(0)
    back_seq(1, red_a.step3)
    mls.join(1)
    red_a.step4()

    @pl.when(last)
    def _():
        input_back(0)

    input_back(1)
    n1s.join(0)

    for which, dst in ((other, r.gb_s), (d, r.gb_o)):
        cols = pl.ds(pl.multiple_of(which * half, LANES), half)
        right = flat(r.nrm[:, :, cols])
        dst[0:hw, :] = mm(flat(r.qb[:, :, 0:hw]), right, TN).astype(BF16)
        dst[hw : 3 * hw, :] = mm(flat(r.kvb[...]), right, TN).astype(BF16)
        right = flat(r.bg[:, :, cols])
        dst[3 * hw : 4 * hw, :] = mm(flat(r.attl[:, :, 0:hw]), right, TN).astype(BF16)
    send_gb = remote(r.gb_s, r.gb_r, r.s_gb.at[0], r.s_gb.at[1], dp=other)
    send_gb.start()
    red_b = Sums(send_gb, r.gb_o, r.gb_r, r.gb_c, r.gb_t, r.s_gbc, r.s_gbg)
    red_b.pair()
    red_b.step1()
    n1s.join(1)

    outs = []

    def store(src, dst):
        cp = pltpu.make_async_copy(src, dst, r.s_loc.at[len(local) + len(outs)])
        cp.start()
        outs.append(cp)

    red_b.step2()
    for s in range(seqs):
        mlp = mls.total(s)
        r.res[s] = (r.middle[s] + vec(5, s) * mlp).astype(BF16)
        keep_sum(5, s, r.cot[s, span(t), :].astype(F32) * mlp)
    store(r.res, r.res_out)
    for s in range(seqs):
        grad1 = n1s.total(s)
        unit, rstd = norm_parts(r.tok[s, span(t), :].astype(F32))
        keep_sum(0, s, grad1)
        keep_sum(1, s, grad1 * unit)
        r.gtok[s] = r.midg[s] + norm_back(grad1, unit, rstd, vec(1, s))

    for k in range(1, nt):
        to = (t + k) % nt
        remote(r.msum.at[to], r.mt_r.at[t], r.s_all.at[0], r.s_mt.at[t], tp=to).start()
    store(r.gtok, r.gtok_out)
    red_b.step3()
    red_b.step4()
    total = r.msum[t]
    for k in range(1, nt):
        fr = (t + k) % nt
        there = r.mt_r.at[fr]
        remote(there, there, r.s_all.at[0], r.s_mt.at[fr], tp=fr).wait_recv()
        total = total + r.mt_r[fr]
    r.md_s[...] = total
    send_md = remote(r.md_s, r.md_r, r.s_md.at[0], r.s_md.at[1], dp=other)
    send_md.start()
    r.mg[c, 0] = total
    send_md.wait()
    r.mg[c, 1] = r.md_r[...]

    def send_mg(k):
        to = (c + k) % nc
        remote(r.mg.at[c], r.mg.at[c], r.s_all.at[1], r.s_mc.at[c], ctx=to).start()

    each(nc, send_mg, 1)
    red_a.take()
    store(r.ga_t, r.ga_out)
    red_b.take()
    store(r.gb_t, r.gb_out)

    def take_small(k):
        fr = (c + k) % nc
        for buf, sems in ((r.mg, r.s_mc), (r.emb, r.s_ec)):
            remote(buf.at[fr], buf.at[fr], r.s_all.at[1], sems.at[fr], ctx=fr).wait_recv()

    each(nc, take_small, 1)
    store(r.mg, r.mg_out)
    store(r.emb, r.emb_out)

    for cp in send_w:
        cp.wait_send()
    for s in range(seqs):
        for group in (toks, cots, n2s, bgs, brs, mls, n1s):
            group.close(s)
    for k, (buf, count) in enumerate(((r.msum, nt), (r.mg, nc), (r.emb, nc))):
        part = buf.at[0 : count - 1]
        remote(part, part, r.s_all.at[k], r.s_mc.at[c], dp=other).wait_send()

    def kv_sent(to):
        mine = r.kv.at[c]
        remote(mine, mine, r.s_kv.at[to], r.r_kv.at[c, 0], ctx=to).wait_send()

    each(nc, kv_sent, c + 1)

    def parts_sent(to):
        mine = r.dq_s.at[to]
        remote(mine, mine, r.s_dq.at[to], r.r_dq.at[c, 0], ctx=to).wait_send()

    each(nc - ((nc - 1 - c) // (nc - 1) if split else 0), parts_sent, c + 1)
    if split:

        @pl.when(last)
        def _():
            mine = r.kv.at[0]
            remote(mine, mine, r.s_q.at[0], r.r_q.at[nc - 1, 0], ctx=0).wait_send()

    def query_sent(to):
        for src, sems, recv in (
            (r.qd.at[:, :, 0:LANES], r.s_q.at[to], r.r_q.at[c, 0]),
            (r.qd.at[:, :, LANES : z.kvw], r.s_do.at[to], r.r_do.at[c, 0]),
            (r.lse.at[c], r.s_st.at[0, to], r.r_st.at[0, c, 0]),
            (r.delta.at[c], r.s_st.at[1, to], r.r_st.at[1, c, 0]),
        ):
            remote(src, src, sems, recv, ctx=to).wait_send()

    each(c, query_sent, skip)
    for cp in outs:
        cp.wait()


def finish_kernel(z, *refs):
    ins, outs, refs = refs[:6], refs[6:15], refs[15:]
    held, stage, sems = refs[:6], refs[6:15], refs[15]
    hw = z.hw
    fetches = [
        pltpu.make_async_copy(src, dst, sems.at[i]) for i, (src, dst) in enumerate(zip(ins, held))
    ]
    for cp in fetches:
        cp.start()
    ga, gb, emb, mg, res, gtok = held
    copies = []

    def put(i, value):
        stage[i][...] = value
        cp = pltpu.make_async_copy(stage[i], outs[i], sems.at[6 + i])
        cp.start()
        copies.append(cp)

    def through(i, src):
        cp = pltpu.make_async_copy(src, outs[i], sems.at[6 + i])
        cp.start()
        copies.append(cp)

    fetches[0].wait()
    put(6, ga[:, 0 : z.ff].astype(F32))
    put(7, ga[:, z.ff : 2 * z.ff].astype(F32))
    fetches[1].wait()
    for i in range(4):
        put(2 + i, gb[i * hw : (i + 1) * hw, :].astype(F32))
    fetches[2].wait()
    fetches[3].wait()
    rest = mg[...].reshape(z.nc * 16, z.half)
    terms = []
    for _ in range(3):
        terms.append(rest.astype(BF16))
        rest = rest - terms[-1].astype(F32)
    terms = jnp.concatenate(terms, axis=0)
    row = lax.broadcasted_iota(jnp.int32, (8, z.half), 0)
    columns = []
    for k in range(z.thirds):
        left = []
        for c in range(z.nc):
            for d in range(2):
                one, two = emb[c, 2 * d : 2 * d + 1, :], emb[c, 2 * d + 1 : 2 * d + 2, :]
                left.append(
                    jnp.where(row == k, one, jnp.where(row == z.thirds + k, two, 0.0))
                )
        left = jnp.concatenate(left, axis=0).astype(BF16)
        columns.append(mm(jnp.concatenate([left] * 3, axis=0), terms, TN))
    put(8, jnp.concatenate(columns, axis=1))
    fetches[4].wait()
    through(0, res)
    fetches[5].wait()
    through(1, gtok)
    for cp in copies:
        cp.wait()


IN_NAMES = (
    "tok_in",
    "ts_in",
    "wq_in",
    "wk_in",
    "wv_in",
    "wo_in",
    "wu_in",
    "wd_in",
    "wm_in",
    "cot_in",
)
OUT_NAMES = ("res_out", "gtok_out", "ga_out", "gb_out", "emb_out", "mg_out")


def solution(mesh):
    def shards(tokens, steps, wq, wk, wv, wo, wu, wd, wm, cot):
        wq, wk, wv, wo = wq.T, wk.T, wv.T, wo.T
        z = Dims(mesh, tokens.shape, wq.shape, wu.shape, wm.shape)
        table = scratch_table(z)
        names = list(IN_NAMES) + list(OUT_NAMES) + list(table)
        hbm = pl.BlockSpec(memory_space=pl.ANY)
        smem = pl.BlockSpec(memory_space=pltpu.SMEM)
        own = (z.seqs, z.rows, z.width)
        shape = jax.ShapeDtypeStruct
        outs = pl.pallas_call(
            functools.partial(layer_kernel, z, names),
            out_shape=(
                shape(own, BF16),
                shape(own, F32),
                shape((z.half, z.wide), BF16),
                shape((z.heads_rows, z.half), BF16),
                shape((z.nc, 8, z.half), F32),
                shape((z.nc, 2, 8, z.half), F32),
            ),
            in_specs=[hbm, smem] + [hbm] * 8,
            out_specs=[hbm] * 6,
            scratch_shapes=list(table.values()),
            compiler_params=pltpu.CompilerParams(
                collective_id=0, has_side_effects=True, vmem_limit_bytes=VMEM_BYTES
            ),
            name="layer",
        )(tokens, steps.T, wq, wk, wv, wo, wu, wd, wm, cot)
        outs = outs[2:] + outs[:2]
        shapes = (
            (own, BF16),
            (own, F32),
            ((z.hw, z.half), F32),
            ((z.hw, z.half), F32),
            ((z.hw, z.half), F32),
            ((z.hw, z.half), F32),
            ((z.half, z.ff), F32),
            ((z.half, z.ff), F32),
            ((z.half, z.mcols), F32),
        )
        done = pl.pallas_call(
            functools.partial(finish_kernel, z),
            out_shape=tuple(shape(*o) for o in shapes),
            in_specs=[hbm] * 6,
            out_specs=[hbm] * 9,
            scratch_shapes=[pltpu.VMEM(o.shape, o.dtype) for o in outs]
            + [pltpu.VMEM(*o) for o in shapes]
            + [pltpu.SemaphoreType.DMA((15,))],
            compiler_params=pltpu.CompilerParams(vmem_limit_bytes=VMEM_BYTES),
            name="finish",
        )(*outs)
        return done[:2] + tuple(g.T for g in done[2:6]) + done[6:]

    rows = P("dp", ("ctx", "tp"), None)
    cols = P("dp", "tp")
    return jax.shard_map(
        shards,
        mesh=mesh,
        in_specs=(rows, P("dp", "ctx")) + (cols,) * 6 + (P("dp", None), rows),
        out_specs=(rows, rows) + (cols,) * 7,
        check_vma=False,
    )
```

```python
import functools
import math

import jax
import jax.numpy as jnp
from jax import lax
from jax.experimental import pallas as pl
from jax.experimental.pallas import tpu as pltpu
from jax.sharding import PartitionSpec as P

MESH = pl.DeviceIdType.MESH
HEAD_DIM = 64
WIN = 256
LANES = 128
EPS = 1e-06
NEG = -1e30
GELU_C = 0.7978845608028654
GELU_A = 0.044715
F32 = jnp.float32
BF16 = jnp.bfloat16
VMEM_BYTES = 62 * 1024 * 1024

NN = (((1,), (0,)), ((), ()))
NT = (((1,), (1,)), ((), ()))
TN = (((0,), (0,)), ((), ()))


def mm(a, b, dims=NN):
    return lax.dot_general(a, b, dims, preferred_element_type=F32)


def norm_parts(x):
    center = x - jnp.mean(x, axis=-1, keepdims=True)
    rstd = lax.rsqrt(jnp.mean(center * center, axis=-1, keepdims=True) + EPS)
    return center * rstd, rstd


def norm_back(grad, unit, rstd, scale):
    dn = grad * (1.0 + scale)
    return rstd * (
        dn
        - jnp.mean(dn, axis=-1, keepdims=True)
        - unit * jnp.mean(dn * unit, axis=-1, keepdims=True)
    )


def remote(src, dst, send, recv, **dev):
    return pltpu.make_async_remote_copy(
        src_ref=src, dst_ref=dst, send_sem=send, recv_sem=recv, device_id=dev, device_id_type=MESH
    )


def chunk_rows(count, devices):
    return 16 * -(-(count // 16) // devices)


class Dims:
    def __init__(self, mesh, tokens, query, up, mod):
        self.nc = mesh.shape["ctx"]
        self.nt = mesh.shape["tp"]
        self.seqs, self.rows, self.width = tokens
        self.block = self.rows * self.nt
        self.hw, self.half = query
        self.heads = self.hw // HEAD_DIM
        self.ff = up[1]
        self.mod = mod[1]
        self.kvw = 2 * self.hw
        self.vlo = self.kvw - WIN
        self.voff = self.hw - self.vlo
        self.wide = 2 * self.ff
        self.heads_rows = 4 * self.hw
        self.mcols = self.mod // self.nt
        self.thirds = self.mcols // self.half


def scratch_table(z):
    vm = lambda shape, dtype=BF16: pltpu.VMEM(shape, dtype)
    sem = lambda *shape: pltpu.SemaphoreType.DMA(shape)
    full = (z.seqs, z.block, z.width)
    own = (z.seqs, z.rows, z.width)
    pair = (z.seqs, 2, z.rows, z.width)
    return dict(
        tok=vm(full),
        cot=vm(full),
        wqt=vm((WIN, z.width)),
        wkvt=vm((z.kvw, z.width)),
        wot=vm((WIN, z.width)),
        wu=vm((z.width, z.ff)),
        wd=vm((z.width, z.ff)),
        wm=vm((z.half, z.mod)),
        emb_s=vm((8, z.half), F32),
        emb_r=vm((8, z.half), F32),
        emb=vm((z.nc, 8, z.half), F32),
        mod_s=vm((8, z.mod), F32),
        mod_r=vm((8, z.mod), F32),
        mod=vm((8, z.mod), F32),
        cosine=vm((z.block, LANES), F32),
        sine=vm((z.block, LANES), F32),
        nrm=vm(full),
        qd=vm((z.seqs, z.block, z.kvw)),
        kv=vm((z.nc, z.seqs, z.block, z.kvw)),
        vt=vm((WIN, z.block)),
        stat=vm((2, 8, z.block), F32),
        acc=vm((z.hw, z.block), F32),
        att=vm((z.seqs, z.hw, z.block), F32),
        attl=vm((z.seqs, z.block, WIN)),
        lse=vm((z.nc, z.seqs, 8, z.block), F32),
        delta=vm((z.nc, z.seqs, 8, z.block), F32),
        br=vm(full),
        br_m=vm(pair),
        br_r=vm(pair),
        branch=vm(own, F32),
        middle=vm(own, F32),
        n2=vm(full),
        act=vm((z.seqs, z.block, z.ff)),
        hgrad=vm((z.seqs, z.block, z.ff)),
        mgrad=vm(full),
        g2=vm(full),
        g2_m=vm(pair),
        g2_r=vm(pair),
        ml=vm(full),
        ml_m=vm(pair),
        ml_r=vm(pair),
        midg=vm(own, F32),
        bg=vm(full),
        seen=vm((z.block, z.kvw)),
        dot=vm((WIN, z.block)),
        dqt=vm((z.seqs, z.hw, z.block), F32),
        dq_s=vm((z.nc, z.seqs, z.hw, z.block)),
        dq_r=vm((z.nc, z.seqs, z.hw, z.block)),
        dq=vm((z.seqs, z.block, WIN), F32),
        dkv=vm((z.seqs, z.block, z.kvw), F32),
        qb=vm((z.seqs, z.block, WIN)),
        kvb=vm((z.seqs, z.block, z.kvw)),
        n1_m=vm(pair),
        n1_r=vm(pair),
        ga_s=vm((z.half, z.wide)),
        ga_o=vm((z.half, z.wide)),
        ga_r=vm((z.half, z.wide)),
        ga_c=vm((z.nc, chunk_rows(z.half, z.nc), z.wide)),
        ga_t=vm((z.half, z.wide)),
        gb_s=vm((z.heads_rows, z.half)),
        gb_o=vm((z.heads_rows, z.half)),
        gb_r=vm((z.heads_rows, z.half)),
        gb_c=vm((z.nc, chunk_rows(z.heads_rows, z.nc), z.half)),
        gb_t=vm((z.heads_rows, z.half)),
        msum=vm((z.nt, 8, z.half), F32),
        mt_r=vm((z.nt, 8, z.half), F32),
        md_s=vm((8, z.half), F32),
        md_r=vm((8, z.half), F32),
        mg=vm((z.nc, 2, 8, z.half), F32),
        res=vm(own),
        gtok=vm(own, F32),
        s_loc=sem(16),
        s_w=sem(2, 6),
        s_e=sem(2),
        s_ec=sem(z.nc),
        s_all=sem(3),
        s_m=sem(2, 2),
        s_tok=sem(z.seqs),
        r_tok=sem(z.seqs, z.nt),
        s_cot=sem(z.seqs),
        r_cot=sem(z.seqs, z.nt),
        s_kv=sem(z.nc),
        r_kv=sem(z.nc, z.seqs),
        s_br=sem(z.seqs),
        m_br=sem(z.seqs, 2),
        r_br=sem(z.seqs, 2),
        s_n2=sem(z.seqs),
        r_n2=sem(z.seqs, z.nt),
        s_g2=sem(z.seqs),
        m_g2=sem(z.seqs, 2),
        r_g2=sem(z.seqs, 2),
        s_ml=sem(z.seqs),
        m_ml=sem(z.seqs, 2),
        r_ml=sem(z.seqs, 2),
        s_bg=sem(z.seqs),
        r_bg=sem(z.seqs, z.nt),
        s_q=sem(z.nc),
        r_q=sem(z.nc, z.seqs),
        s_do=sem(z.nc),
        r_do=sem(z.nc, z.seqs),
        s_st=sem(2, z.nc),
        r_st=sem(2, z.nc, z.seqs),
        s_dq=sem(z.nc),
        r_dq=sem(z.nc, z.seqs),
        s_n1=sem(z.seqs),
        m_n1=sem(z.seqs, 2),
        r_n1=sem(z.seqs, 2),
        s_ga=sem(2),
        s_gac=sem(12) if z.nc == 4 else sem(2, z.nc),
        s_gag=sem(2) if z.nc == 4 else sem(2, z.nc),
        s_gb=sem(2),
        s_gbc=sem(12) if z.nc == 4 else sem(2, z.nc),
        s_gbg=sem(2) if z.nc == 4 else sem(2, z.nc),
        s_mt=sem(z.nt),
        s_md=sem(2),
        s_mc=sem(z.nc),
    )


class Box:
    pass


def layer_kernel(z, names, *refs):
    r = Box()
    for name, ref in zip(names, refs):
        setattr(r, name, ref)
    d, c, t = lax.axis_index("dp"), lax.axis_index("ctx"), lax.axis_index("tp")
    other = 1 - d
    nt, nc, rows, block, width, hw = z.nt, z.nc, z.rows, z.block, z.width, z.hw
    seqs, half = z.seqs, z.half

    def each(count, body, first=0):
        def step(i, carry):
            body(i)
            return carry

        lax.fori_loop(first, count, step, 0)

    def span(idx):
        return pl.ds(pl.multiple_of(idx * rows, rows), rows)

    def slot(ref, idx):
        return ref.at[:, span(idx), :]

    def piece(ref, s, idx):
        return ref.at[s, span(idx), :]

    def flat(x):
        return x.reshape(x.shape[0] * x.shape[1], x.shape[2])

    def lanes_of(shape, axis=1):
        return lax.broadcasted_iota(jnp.int32, shape, axis)

    bar = pltpu.get_barrier_semaphore()
    pl.semaphore_signal(bar, inc=1, device_id={"dp": other}, device_id_type=MESH)
    for k in range(1, nt):
        pl.semaphore_signal(bar, inc=1, device_id={"tp": (t + k) % nt}, device_id_type=MESH)

    def greet(k):
        pl.semaphore_signal(bar, inc=1, device_id={"ctx": (c + k) % nc}, device_id_type=MESH)

    each(nc, greet, 1)

    local = []

    def fetch(src, dst):
        cp = pltpu.make_async_copy(src, dst, r.s_loc.at[len(local)])
        cp.start()
        local.append(cp)
        return cp

    my_half = pl.ds(pl.multiple_of(d * half, LANES), half)
    weights = [
        (r.wq_in, r.wqt.at[0:hw, my_half]),
        (r.wk_in, r.wkvt.at[0:hw, my_half]),
        (r.wv_in, r.wkvt.at[hw : z.kvw, my_half]),
        (r.wo_in, r.wot.at[z.voff : z.voff + hw, my_half]),
        (r.wu_in, r.wu.at[my_half, :]),
        (r.wd_in, r.wd.at[my_half, :]),
    ]
    first_cols = 2 * width
    cp_tok = fetch(r.tok_in, slot(r.tok, t))
    cp_wm1 = fetch(r.wm_in.at[:, 0:first_cols], r.wm.at[:, 0:first_cols])
    cp_w = [fetch(src, dst) for src, dst in weights]
    cp_wm2 = fetch(r.wm_in.at[:, first_cols : z.mod], r.wm.at[:, first_cols : z.mod])
    cp_cot = fetch(r.cot_in, slot(r.cot, t))

    r.wqt[hw:WIN, :] = jnp.zeros((WIN - hw, width), BF16)
    r.wot[0 : z.voff, :] = jnp.zeros((z.voff, width), BF16)

    row8 = lanes_of((8, half), 0)
    step_of = jnp.where(
        row8 % 2 == 0, r.ts_in[0, 0].astype(F32), r.ts_in[0, 1].astype(F32)
    )
    angle = step_of * jnp.exp(
        lanes_of((8, half)).astype(F32) * (-math.log(10000.0) / half)
    )
    sin_e, cos_e = jnp.sin(angle), jnp.cos(angle)

    def silu_low(v):
        return (v / (1.0 + jnp.exp(-v))).astype(BF16).astype(F32)

    sin_e, cos_e = silu_low(sin_e), silu_low(cos_e)
    first = d == 0
    own_half = jnp.where(row8 < 2, jnp.where(first, sin_e, cos_e), 0.0)
    r.emb_s[...] = jnp.where(
        (row8 >= 2) & (row8 < 4), jnp.where(first, cos_e, sin_e), 0.0
    )
    pl.semaphore_wait(bar, 1 + (nt - 1) + (nc - 1))

    side = t // 2
    mate = t + 1 - 2 * (t % 2)
    cross = 2 - side
    outer = t % 3 == 0
    inner = t % 3 != 0

    def peer(i):
        far = i // 2
        return (1 - far) * (t + i * (1 - 2 * (t % 2))) + far * ((1 - side) * i + side * (3 - i))

    class Gather:
        def __init__(self, buf, send, recv):
            self.buf, self.sems, self.recv = buf, send, recv

        def copy(self, src, s, idx, to):
            return remote(
                src, piece(self.buf, s, idx), self.sems.at[s], self.recv.at[s, idx], tp=to
            )

        def open(self, src, s):
            self.copy(src, s, t, cross).start()
            self.copy(src, s, t, mate).start()

        def wait(self, s, idx):
            self.copy(piece(self.buf, s, idx), s, idx, mate).wait_recv()

        def relay(self, s):
            @pl.when(inner)
            def _():
                def one(i):
                    idx = peer(i)
                    self.wait(s, idx)
                    self.copy(piece(self.buf, s, idx), s, idx, mate).start()

                each(4, one, 2)

        def collect(self, s, work):
            def one(i):
                idx = peer(i)

                @pl.when(outer | (i == 1))
                def _():
                    self.wait(s, idx)

                if work is not None:
                    work(s, idx, i)

            each(4, one, 1)

        def close(self, s):
            def sent(count):
                all_sent = self.buf.at[s, 0 : count * rows, :]
                remote(all_sent, all_sent, self.sems.at[s], self.recv.at[s, t], tp=mate).wait_send()

            @pl.when(outer)
            def _():
                sent(2)

            @pl.when(inner)
            def _():
                sent(4)

    class Scatter:
        def __init__(self, part, merge, got, send, msem, gsem):
            self.part, self.merge, self.got = part, merge, got
            self.sems, self.msem, self.gsem = send, msem, gsem

        def to_got(self, s, idx, k):
            return remote(
                piece(self.part, s, idx),
                self.got.at[s, k],
                self.sems.at[s],
                self.gsem.at[s, k],
                tp=idx,
            )

        def to_merge(self, s, idx, i):
            return remote(
                piece(self.part, s, idx),
                self.merge.at[s, i - 2],
                self.sems.at[s],
                self.msem.at[s, i - 2],
                tp=mate,
            )

        def push(self, s, idx, i):
            @pl.when(i == 1)
            def _():
                self.to_got(s, idx, 0).start()

            @pl.when((i > 1) & outer)
            def _():
                self.to_merge(s, idx, i).start()

        def push_all(self, s):
            for i in (3, 2):
                self.push(s, peer(i), i)
            self.push(s, mate, 1)

        def join(self, s):
            @pl.when(inner)
            def _():
                def one(k):
                    i = 3 - k
                    idx = peer(i)
                    self.to_merge(s, idx, i).wait_recv()
                    at = span(idx)
                    self.part[s, at, :] = (
                        self.part[s, at, :].astype(F32) + self.merge[s, i - 2].astype(F32)
                    ).astype(BF16)
                    self.to_got(s, idx, 1).start()

                each(2, one)

        def total(self, s):
            for k in range(2):
                self.to_got(s, mate, k).wait_recv()
            return (
                self.part[s, span(t), :].astype(F32)
                + self.got[s, 0].astype(F32)
                + self.got[s, 1].astype(F32)
            )

        def close(self, s):
            all_sent = self.part.at[s, 0 : 3 * rows, :]
            remote(all_sent, all_sent, self.sems.at[s], self.gsem.at[s, 0], tp=mate).wait_send()

    toks = Gather(r.tok, r.s_tok, r.r_tok)
    cots = Gather(r.cot, r.s_cot, r.r_cot)
    n2s = Gather(r.n2, r.s_n2, r.r_n2)
    bgs = Gather(r.bg, r.s_bg, r.r_bg)
    brs = Scatter(r.br, r.br_m, r.br_r, r.s_br, r.m_br, r.r_br)
    g2s = Scatter(r.g2, r.g2_m, r.g2_r, r.s_g2, r.m_g2, r.r_g2)
    mls = Scatter(r.ml, r.ml_m, r.ml_r, r.s_ml, r.m_ml, r.r_ml)
    n1s = Scatter(r.g2, r.n1_m, r.n1_r, r.s_n1, r.m_n1, r.r_n1)

    for s in range(seqs):
        toks.open(r.tok_in.at[s], s)

    @pl.when(outer)
    def _():
        for s in range(seqs):
            cots.open(r.cot_in.at[s], s)

    send_emb = remote(r.emb_s, r.emb_r, r.s_e.at[0], r.s_e.at[1], dp=other)
    send_emb.start()
    send_w = [
        remote(src, dst, r.s_w.at[0, i], r.s_w.at[1, i], dp=other)
        for i, (src, dst) in enumerate(weights)
    ]
    for cp in send_w[:3]:
        cp.start()

    send_emb.wait()
    emb4 = own_half + r.emb_r[...]
    r.emb[pl.ds(c, 1)] = emb4[None]
    emb_low = emb4.astype(BF16)

    def mod_part(lo, hi, which, ready):
        ready.wait()
        r.mod_s[:, lo:hi] = mm(emb_low, r.wm[:, lo:hi])
        cp = remote(
            r.mod_s.at[:, lo:hi], r.mod_r.at[:, lo:hi], r.s_m.at[0, which], r.s_m.at[1, which], dp=other
        )
        cp.start()
        return cp

    def mod_take(lo, hi, cp):
        cp.wait()
        for s in range(seqs):
            r.mod[s : s + 1, lo:hi] = r.mod_s[s : s + 1, lo:hi] + r.mod_r[s + 2 : s + 3, lo:hi]

    def vec(slot_idx, s):
        lo = slot_idx * width
        return r.mod[s : s + 1, lo : lo + width]

    mod1 = mod_part(0, first_cols, 0, cp_wm1)
    for cp in send_w[3:]:
        cp.start()

    def send_ctx_emb(k):
        to = (c + k) % nc
        remote(r.emb.at[c], r.emb.at[c], r.s_all.at[2], r.s_ec.at[c], ctx=to).start()

    each(nc, send_ctx_emb, 1)

    place = (c * block + lanes_of((block, LANES), 0)).astype(F32)
    pair_of = (lanes_of((block, LANES)) % (HEAD_DIM // 2)).astype(F32)
    turn = place * jnp.exp(pair_of * (-2.0 * math.log(10000.0) / HEAD_DIM))
    low_lane = lanes_of((block, LANES)) % HEAD_DIM < HEAD_DIM // 2
    r.cosine[...] = jnp.cos(turn)
    r.sine[...] = jnp.where(low_lane, -jnp.sin(turn), jnp.sin(turn))

    def swap(x):
        low = lanes_of(x.shape) % HEAD_DIM < HEAD_DIM // 2
        return jnp.where(
            low,
            pltpu.roll(x, LANES - HEAD_DIM // 2, 1),
            pltpu.roll(x, HEAD_DIM // 2, 1),
        )

    for i in range(3):
        cp_w[i].wait()
        send_w[i].wait_recv()
    mod_take(0, first_cols, mod1)

    def make_qkv(s, idx, i):
        at = span(idx)
        unit, _ = norm_parts(r.tok[s, at, :].astype(F32))
        low = (unit * (1.0 + vec(1, s)) + vec(0, s)).astype(BF16)
        r.nrm[s, at, :] = low
        cos1, sin1 = r.cosine[at, :], r.sine[at, :]
        q_pre = mm(low, r.wqt[...], NT)
        kv_pre = mm(low, r.wkvt[...], NT)
        for j in range(WIN // LANES):
            x = q_pre[:, j * LANES : (j + 1) * LANES]
            x = (x * cos1 + swap(x) * sin1) * (HEAD_DIM ** -0.5)
            r.qd[s, at, j * LANES : (j + 1) * LANES] = x.astype(BF16)
        for j in range(z.kvw // LANES):
            x = kv_pre[:, j * LANES : (j + 1) * LANES]
            keys = min(max(hw - j * LANES, 0), LANES)
            if keys > 0:
                turned = x * cos1 + swap(x) * sin1
                x = turned if keys == LANES else jnp.where(lanes_of(x.shape) < keys, turned, x)
            r.kv[c, s, at, j * LANES : (j + 1) * LANES] = x.astype(BF16)

        def send_kv(to):
            mine = r.kv.at[c, s, at, :]
            remote(mine, mine, r.s_kv.at[to], r.r_kv.at[c, s], ctx=to).start()

        each(nc, send_kv, c + 1)

    cp_tok.wait()
    for s in range(seqs):
        make_qkv(s, t, 0)
    mod2 = mod_part(first_cols, z.mod, 1, cp_wm2)
    toks.relay(0)
    toks.collect(0, make_qkv)
    toks.relay(1)

    @pl.when(inner)
    def _():
        for s in range(seqs):
            cots.open(r.cot_in.at[s], s)

    toks.collect(1, make_qkv)
    cp_cot.wait()
    mod_take(first_cols, z.mod, mod2)
    for i in range(3, 6):
        cp_w[i].wait()
        send_w[i].wait_recv()

    eye = (lanes_of((WIN, WIN), 0) == lanes_of((WIN, WIN))).astype(BF16)

    def head_of(x, h, off=0):
        lane = lanes_of(x.shape)
        lo = off + h * HEAD_DIM
        return jnp.where((lane >= lo) & (lane < lo + HEAD_DIM), x, jnp.zeros_like(x))

    def attend_seq(s):
        r.stat[0] = jnp.full((8, block), NEG, F32)
        r.stat[1] = jnp.zeros((8, block), F32)
        r.acc[...] = jnp.zeros((hw, block), F32)
        q = r.qd[s, :, 0:WIN]

        def one_block(back):
            j = c - back

            @pl.when(back > 0)
            def _():
                there = r.kv.at[j, s]
                remote(there, there, r.s_kv.at[j], r.r_kv.at[j, s], ctx=j).wait_recv()

            keys = r.kv[j, s, :, 0:WIN]
            r.vt[...] = mm(eye, r.kv[j, s, :, z.vlo : z.vlo + WIN], NT).astype(BF16)
            for h in range(z.heads):
                scores = mm(keys, head_of(q, h), NT)
                old = r.stat[0, h : h + 1, :]
                top = jnp.maximum(old, jnp.max(scores, axis=0, keepdims=True))
                prob = jnp.exp(scores - top)
                fade = jnp.exp(old - top)
                r.stat[0, h : h + 1, :] = top
                r.stat[1, h : h + 1, :] = r.stat[1, h : h + 1, :] * fade + jnp.sum(
                    prob, axis=0, keepdims=True
                )
                lo = h * HEAD_DIM
                vt = r.vt[z.voff + lo : z.voff + lo + HEAD_DIM, :]
                r.acc[lo : lo + HEAD_DIM, :] = r.acc[lo : lo + HEAD_DIM, :] * fade + mm(
                    vt, prob.astype(BF16)
                )

        each(c + 1, one_block)
        for h in range(z.heads):
            lo = h * HEAD_DIM
            denom = r.stat[1, h : h + 1, :]
            r.lse[c, s, h : h + 1, :] = r.stat[0, h : h + 1, :] + jnp.log(denom)
            r.att[s, lo : lo + HEAD_DIM, :] = r.acc[lo : lo + HEAD_DIM, :] / denom
        low = jnp.transpose(r.att[s]).astype(BF16)
        r.attl[s, :, 0:hw] = low
        r.attl[s, :, hw:WIN] = jnp.zeros((block, WIN - hw), BF16)
        r.br[s] = mm(low, r.wot[z.voff : z.voff + hw, :]).astype(BF16)
        brs.push_all(s)

    each(seqs, attend_seq)

    split = nc == 4
    last = c == nc - 1
    skip = c // (nc - 1) if split else 0

    def query_copy(j, s, to):
        return remote(
            r.qd.at[s, :, 0:LANES],
            r.kv.at[j, s, :, 0:LANES],
            r.s_q.at[to],
            r.r_q.at[j, s],
            ctx=to,
        )

    def stat_copy(buf, which, j, s, to):
        return remote(
            buf.at[j, s], buf.at[j, s], r.s_st.at[which, to], r.r_st.at[which, j, s], ctx=to
        )

    def send_queries(to):
        for s in range(seqs):
            query_copy(c, s, to).start()
            stat_copy(r.lse, 0, c, s, to).start()

    each(c, send_queries, skip)
    for s in range(seqs):
        cots.relay(s)
    def middle_rows(s):
        branch = brs.total(s)
        r.branch[s] = branch
        middle = r.tok[s, span(t), :].astype(F32) + vec(2, s) * branch
        r.middle[s] = middle
        unit, _ = norm_parts(middle)
        r.n2[s, span(t), :] = (unit * (1.0 + vec(4, s)) + vec(3, s)).astype(BF16)
        n2s.open(piece(r.n2, s, t), s)

    brs.join(0)
    middle_rows(0)
    brs.join(1)
    n2s.relay(0)
    middle_rows(1)

    def feed(s, idx, i):
        at = span(idx)
        hid = mm(r.n2[s, at, :], r.wu[...])
        square = hid * hid
        tanh = jnp.tanh(GELU_C * (hid + GELU_A * (hid * square)))
        r.act[s, at, :] = (0.5 * hid * (1.0 + tanh)).astype(BF16)
        slope = 0.5 * (1.0 + tanh) + 0.5 * hid * (1.0 - tanh * tanh) * (
            GELU_C * (1.0 + 3.0 * GELU_A * square)
        )
        low = (vec(5, s) * r.cot[s, at, :].astype(F32)).astype(BF16)
        r.mgrad[s, at, :] = low
        hgrad = (slope * mm(low, r.wd[...])).astype(BF16)
        r.hgrad[s, at, :] = hgrad
        r.g2[s, at, :] = mm(hgrad, r.wu[...], NT).astype(BF16)
        g2s.push(s, idx, i)

    for s in range(seqs):
        feed(s, t, 0)
    for s in range(seqs):
        cots.collect(s, None)
        if s > 0:
            n2s.relay(s)
        n2s.collect(s, feed)
    g2s.join(0)

    class Reduction:
        def __init__(self, got, mine, theirs, buf, total, sems, sems_all):
            self.got, self.mine, self.theirs, self.buf, self.total = got, mine, theirs, buf, total
            self.sems, self.sems_all = sems, sems_all
            self.chunk = buf.shape[1]
            self.owners = mine.shape[0] // self.chunk

        def rows(self, o):
            return pl.ds(pl.multiple_of(o * self.chunk, 16), self.chunk)

        def part(self, o):
            return remote(
                self.mine.at[self.rows(o), :],
                self.buf.at[c],
                self.sems.at[0, o],
                self.sems.at[1, c],
                ctx=o,
            )

        def share(self, owner, to):
            here = self.total.at[self.rows(owner), :]
            return remote(here, here, self.sems_all.at[0, to], self.sems_all.at[1, owner], ctx=to)

        def to_owners(self, body):
            def one(k):
                o = (c + k) % nc

                @pl.when(o < self.owners)
                def _():
                    body(o)

            each(nc, one, 1)

        def as_owner(self, body):
            @pl.when(c < self.owners)
            def _():
                body()

        def pair(self):
            self.got.wait()
            self.mine[...] = (self.mine[...].astype(F32) + self.theirs[...].astype(F32)).astype(
                BF16
            )

        def step1(self):
            self.to_owners(lambda o: self.part(o).start())

        def step2(self):
            pass

        def step4(self):
            pass

        def step3(self):
            def body():
                def add(k, acc):
                    fr = (c + k) % nc
                    there = self.buf.at[fr]
                    remote(
                        there, there, self.sems.at[0, fr], self.sems.at[1, fr], ctx=fr
                    ).wait_recv()
                    return acc + self.buf[fr].astype(F32)

                acc = self.mine[self.rows(c), :].astype(F32)
                if nc <= 4:
                    for k in range(1, nc):
                        acc = add(k, acc)
                else:
                    acc = lax.fori_loop(1, nc, add, acc)
                self.total[self.rows(c), :] = acc.astype(BF16)
                each(nc, lambda k: self.share(c, (c + k) % nc).start(), 1)

            self.as_owner(body)

        def take(self):
            def one(o):
                self.share(o, o).wait_recv()
                self.part(o).wait_send()

            self.to_owners(one)
            self.as_owner(
                lambda: each(nc, lambda k: self.share(c, (c + k) % nc).wait_send(), 1)
            )

    class Square:
        def __init__(self, got, mine, theirs, buf, total, sems, sems_all):
            self.got, self.mine, self.theirs, self.buf, self.total = got, mine, theirs, buf, total
            self.sems, self.sems_all = sems, sems_all
            self.part = buf.shape[1] // 2
            by_x = c + 1 - 2 * (c % 2)
            by_y = (c + 2) % 4
            self.near = (by_x, by_y)
            self.next = (by_y, by_x)
            self.far = 3 - c

        def rows(self, o, h):
            return pl.ds(pl.multiple_of((2 * o + h) * self.part, 16), self.part)

        def first(self, h, k):
            o = (self.near[h], self.far)[k]
            return remote(
                self.mine.at[self.rows(o, h), :],
                self.buf.at[2 * h + k, 0 : self.part, :],
                self.sems_all.at[0],
                self.sems.at[2 * h + k],
                ctx=self.near[h],
            )

        def second(self, h):
            o = self.next[h]
            return remote(
                self.mine.at[self.rows(o, h), :],
                self.buf.at[2 * h, self.part : 2 * self.part, :],
                self.sems_all.at[0],
                self.sems.at[4 + h],
                ctx=o,
            )

        def spread(self, h, o, to, which, landed):
            at = self.total.at[self.rows(landed, h), :]
            src = self.total.at[self.rows(o, h), :]
            return remote(src, at, self.sems_all.at[1], self.sems.at[which], ctx=to)

        def third(self, h, landed):
            return self.spread(h, landed, self.next[h], 6 + h, landed)

        def fourth(self, h, k, landed):
            return self.spread(h, landed, self.near[h], 8 + 2 * h + k, landed)

        def pair(self):
            self.got.wait()
            self.mine[...] = (self.mine[...].astype(F32) + self.theirs[...].astype(F32)).astype(
                BF16
            )

        def step1(self):
            for k in (1, 0):
                for h in range(2):
                    self.first(h, k).start()

        def step2(self):
            for k in (1, 0):
                for h in range(2):
                    self.first(h, k).wait_recv()
                    at = self.rows((c, self.next[h])[k], h)
                    self.mine[at, :] = (
                        self.mine[at, :].astype(F32)
                        + self.buf[2 * h + k, 0 : self.part, :].astype(F32)
                    ).astype(BF16)
                    if k == 1:
                        self.second(h).start()

        def step3(self):
            for h in range(2):
                self.second(h).wait_recv()
                at = self.rows(c, h)
                self.total[at, :] = (
                    self.mine[at, :].astype(F32)
                    + self.buf[2 * h, self.part : 2 * self.part, :].astype(F32)
                ).astype(BF16)
                self.third(h, c).start()

        def step4(self):
            for h in range(2):
                self.fourth(h, 0, c).start()
            for h in range(2):
                self.third(h, self.next[h]).wait_recv()
                self.fourth(h, 1, self.next[h]).start()

        def take(self):
            for h in range(2):
                self.fourth(h, 0, self.near[h]).wait_recv()
                self.fourth(h, 1, self.far).wait_recv()
            for k, ref in enumerate((self.mine, self.total)):
                part = ref.at[0 : 6 * self.part, :]
                remote(part, part, self.sems_all.at[k], self.sems.at[0], ctx=self.far).wait_send()

    Sums = Square if nc == 4 else Reduction

    r.msum[...] = jnp.zeros((nt, 8, half), F32)

    def keep_sum(slot_idx, s, value):
        value = jnp.sum(value, axis=0, keepdims=True)
        for k in range(width // half):
            to, row = divmod(slot_idx * (width // half) + k, z.thirds)
            row = s * z.thirds + row
            r.msum[to, row : row + 1, :] = value[:, k * half : (k + 1) * half]

    def middle_back(s):
        grad2 = g2s.total(s)
        unit, rstd = norm_parts(r.middle[s])
        mid_grad = r.cot[s, span(t), :].astype(F32) + norm_back(grad2, unit, rstd, vec(4, s))
        r.midg[s] = mid_grad
        r.bg[s, span(t), :] = (vec(2, s) * mid_grad).astype(BF16)
        bgs.open(piece(r.bg, s, t), s)
        keep_sum(3, s, grad2)
        keep_sum(4, s, grad2 * unit)
        keep_sum(2, s, mid_grad * r.branch[s])

    middle_back(0)

    def pair_grads(which, dst):
        cols = pl.ds(pl.multiple_of(which * half, half), half)
        for k, (lhs, rhs) in enumerate(((r.n2, r.hgrad), (r.mgrad, r.act))):
            grad = mm(flat(lhs[:, :, cols]), flat(rhs[...]), TN)
            dst[:, k * z.ff : (k + 1) * z.ff] = grad.astype(BF16)

    send_ga = remote(r.ga_s, r.ga_r, r.s_ga.at[0], r.s_ga.at[1], dp=other)
    pair_grads(other, r.ga_s)
    send_ga.start()
    pair_grads(d, r.ga_o)
    g2s.join(1)
    bgs.relay(0)
    red_a = Sums(send_ga, r.ga_o, r.ga_r, r.ga_c, r.ga_t, r.s_gac, r.s_gag)
    red_a.pair()
    red_a.step1()
    middle_back(1)
    for s in range(seqs):
        r.ml[s] = mm(r.act[s], r.wd[...], NT).astype(BF16)

    def grad_copy(j, s, idx, to):
        at = span(idx)
        return remote(
            r.qd.at[s, at, LANES : z.kvw],
            r.kv.at[j, s, at, LANES : z.kvw],
            r.s_do.at[to],
            r.r_do.at[j, s],
            ctx=to,
        )

    def out_grads(s, idx, i):
        at = span(idx)
        do = mm(r.bg[s, at, :], r.wot[...], NT).astype(BF16)
        over = WIN - z.vlo
        r.qd[s, at, z.vlo : WIN] = r.qd[s, at, z.vlo : WIN] + do[:, 0:over]
        r.qd[s, at, WIN : z.kvw] = do[:, over:WIN]
        each(c, lambda to: grad_copy(c, s, idx, to).start(), skip)

    def deltas(s):
        r.dot[...] = mm(eye, r.qd[s, :, z.vlo : z.vlo + WIN], NT).astype(BF16)
        for h in range(z.heads):
            lo = h * HEAD_DIM
            r.delta[c, s, h : h + 1, :] = jnp.sum(
                r.dot[z.voff + lo : z.voff + lo + HEAD_DIM, :].astype(F32)
                * r.att[s, lo : lo + HEAD_DIM, :],
                axis=0,
                keepdims=True,
            )
        each(c, lambda to: stat_copy(r.delta, 1, c, s, to).start(), skip)

    def query_back_copy(j, s, to):
        return remote(
            r.dq_s.at[to, s], r.dq_r.at[j, s], r.s_dq.at[to], r.r_dq.at[j, s], ctx=to
        )

    over = WIN - z.vlo

    def pair_back(s, keys, vals, q, do, j, keep):
        dk = jnp.zeros((block, WIN), F32)
        dv = jnp.zeros((block, WIN), F32)
        for h in range(z.heads):
            lo = h * HEAD_DIM
            qh = head_of(q, h)
            doh = head_of(do, h, z.voff)
            prob = jnp.exp(mm(keys, qh, NT) - r.lse[j, s, h : h + 1, :])
            dprob = mm(vals, doh, NT)
            dsc = (prob * (dprob - r.delta[j, s, h : h + 1, :])).astype(BF16)
            dv = dv + mm(prob.astype(BF16), doh)
            dk = dk + mm(dsc, qh)
            keep(lo, mm(r.vt[lo : lo + HEAD_DIM, :], dsc))
        return (
            (0, z.vlo, dk[:, 0 : z.vlo]),
            (z.vlo, WIN, dk[:, z.vlo : WIN] + dv[:, 0:over]),
            (WIN, z.kvw, dv[:, over:WIN]),
        )

    def far_copy(s):
        return remote(
            r.kv.at[0, s], r.kv.at[nc - 1, s], r.s_q.at[0], r.r_q.at[nc - 1, s], ctx=0
        )

    def back_seq(s, after_own):
        r.dkv[s] = jnp.zeros((block, z.kvw), F32)
        r.dqt[s] = jnp.zeros((hw, block), F32)
        if split:

            @pl.when(last)
            def _():
                keys = r.kv[0, s, :, 0:WIN]
                vals = r.kv[0, s, :, z.vlo : z.vlo + WIN]
                r.vt[...] = mm(eye, keys, NT).astype(BF16)

                def keep(lo, dqt):
                    r.dqt[s, lo : lo + HEAD_DIM, :] += dqt

                q = r.qd[s, :, 0:WIN]
                do = r.qd[s, :, z.vlo : z.vlo + WIN]
                for lo, hi, value in pair_back(s, keys, vals, q, do, c, keep):
                    r.kv[0, s, :, lo:hi] = value.astype(BF16)
                far_copy(s).start()

        keys = r.kv[c, s, :, 0:WIN]
        vals = r.kv[c, s, :, z.vlo : z.vlo + WIN]
        r.vt[...] = mm(eye, keys, NT).astype(BF16)

        def one_block(k):
            j = c + k

            @pl.when(k == 0)
            def _():
                r.seen[...] = r.qd[s]

            @pl.when(k == 1)
            def _():
                after_own()

            @pl.when(k > 0)
            def _():
                query_copy(j, s, j).wait_recv()
                there = r.kv.at[j, s, :, LANES : z.kvw]
                remote(there, there, r.s_do.at[j], r.r_do.at[j, s], ctx=j).wait_recv()
                stat_copy(r.lse, 0, j, s, j).wait_recv()
                stat_copy(r.delta, 1, j, s, j).wait_recv()
                r.seen[...] = r.kv[j, s]

            def keep(lo, dqt):
                @pl.when(k == 0)
                def _():
                    r.dqt[s, lo : lo + HEAD_DIM, :] += dqt

                @pl.when(k > 0)
                def _():
                    r.dq_s[j, s, lo : lo + HEAD_DIM, :] = dqt.astype(BF16)

            q = r.seen[:, 0:WIN]
            do = r.seen[:, z.vlo : z.vlo + WIN]
            for lo, hi, value in pair_back(s, keys, vals, q, do, j, keep):
                r.dkv[s, :, lo:hi] += value

            @pl.when(k > 0)
            def _():
                query_back_copy(c, s, j).start()

        each(nc - c - ((nc - 1 - c) // (nc - 1) if split else 0), one_block)

        @pl.when(last)
        def _():
            after_own()

    for s in range(seqs):
        out_grads(s, t, 0)
    def input_back(s):
        g2s.close(s)
        if split:

            @pl.when(c == 0)
            def _():
                far_copy(s).wait_recv()
                r.dkv[s] += r.kv[nc - 1, s].astype(F32)

        def add_dq(j):
            query_back_copy(j, s, j).wait_recv()
            r.dqt[s] += r.dq_r[j, s].astype(F32)

        each(c, add_dq, skip)
        r.dq[s, :, 0:hw] = jnp.transpose(r.dqt[s]) * (HEAD_DIM ** -0.5)
        r.dq[s, :, hw:WIN] = jnp.zeros((block, WIN - hw), F32)
        cos1, sin1 = r.cosine[...], r.sine[...]
        for j in range(WIN // LANES):
            x = r.dq[s, :, j * LANES : (j + 1) * LANES]
            r.qb[s, :, j * LANES : (j + 1) * LANES] = (x * cos1 - swap(x) * sin1).astype(BF16)
        for j in range(z.kvw // LANES):
            x = r.dkv[s, :, j * LANES : (j + 1) * LANES]
            keys = min(max(hw - j * LANES, 0), LANES)
            if keys > 0:
                turned = x * cos1 - swap(x) * sin1
                x = turned if keys == LANES else jnp.where(lanes_of(x.shape) < keys, turned, x)
            r.kvb[s, :, j * LANES : (j + 1) * LANES] = x.astype(BF16)
        r.g2[s] = (mm(r.qb[s], r.wqt[...]) + mm(r.kvb[s], r.wkvt[...])).astype(BF16)
        n1s.push_all(s)

    bgs.collect(0, out_grads)
    deltas(0)
    bgs.relay(1)

    @pl.when(outer)
    def _():
        for s in range(seqs):
            mls.push_all(s)

    back_seq(0, red_a.step2)
    bgs.collect(1, out_grads)
    deltas(1)

    @pl.when(inner)
    def _():
        for s in range(seqs):
            mls.push_all(s)

    @pl.when(c < nc - 1)
    def _():
        input_back(0)

    mls.join(0)
    back_seq(1, red_a.step3)
    mls.join(1)
    red_a.step4()

    @pl.when(last)
    def _():
        input_back(0)

    input_back(1)
    n1s.join(0)

    def head_grads(which, dst):
        cols = pl.ds(pl.multiple_of(which * half, LANES), half)
        right = flat(r.nrm[:, :, cols])
        dst[0:hw, :] = mm(flat(r.qb[:, :, 0:hw]), right, TN).astype(BF16)
        dst[hw : 3 * hw, :] = mm(flat(r.kvb[...]), right, TN).astype(BF16)
        right = flat(r.bg[:, :, cols])
        dst[3 * hw : 4 * hw, :] = mm(flat(r.attl[:, :, 0:hw]), right, TN).astype(BF16)

    send_gb = remote(r.gb_s, r.gb_r, r.s_gb.at[0], r.s_gb.at[1], dp=other)
    head_grads(other, r.gb_s)
    send_gb.start()
    head_grads(d, r.gb_o)
    red_b = Sums(send_gb, r.gb_o, r.gb_r, r.gb_c, r.gb_t, r.s_gbc, r.s_gbg)
    red_b.pair()
    red_b.step1()
    n1s.join(1)

    outs = []

    def store(src, dst):
        cp = pltpu.make_async_copy(src, dst, r.s_loc.at[len(local) + len(outs)])
        cp.start()
        outs.append(cp)

    red_b.step2()
    for s in range(seqs):
        mlp = mls.total(s)
        r.res[s] = (r.middle[s] + vec(5, s) * mlp).astype(BF16)
        keep_sum(5, s, r.cot[s, span(t), :].astype(F32) * mlp)
    store(r.res, r.res_out)
    for s in range(seqs):
        grad1 = n1s.total(s)
        unit, rstd = norm_parts(r.tok[s, span(t), :].astype(F32))
        keep_sum(0, s, grad1)
        keep_sum(1, s, grad1 * unit)
        r.gtok[s] = r.midg[s] + norm_back(grad1, unit, rstd, vec(1, s))

    for k in range(1, nt):
        to = (t + k) % nt
        remote(r.msum.at[to], r.mt_r.at[t], r.s_all.at[0], r.s_mt.at[t], tp=to).start()
    store(r.gtok, r.gtok_out)
    red_b.step3()
    red_b.step4()
    total = r.msum[t]
    for k in range(1, nt):
        fr = (t + k) % nt
        there = r.mt_r.at[fr]
        remote(there, there, r.s_all.at[0], r.s_mt.at[fr], tp=fr).wait_recv()
        total = total + r.mt_r[fr]
    r.md_s[...] = total
    send_md = remote(r.md_s, r.md_r, r.s_md.at[0], r.s_md.at[1], dp=other)
    send_md.start()
    r.mg[c, 0] = total
    send_md.wait()
    r.mg[c, 1] = r.md_r[...]

    def send_mg(k):
        to = (c + k) % nc
        remote(r.mg.at[c], r.mg.at[c], r.s_all.at[1], r.s_mc.at[c], ctx=to).start()

    each(nc, send_mg, 1)
    red_a.take()
    store(r.ga_t, r.ga_out)
    red_b.take()
    store(r.gb_t, r.gb_out)

    def take_small(k):
        fr = (c + k) % nc
        for buf, sems in ((r.mg, r.s_mc), (r.emb, r.s_ec)):
            remote(buf.at[fr], buf.at[fr], r.s_all.at[1], sems.at[fr], ctx=fr).wait_recv()

    each(nc, take_small, 1)
    store(r.mg, r.mg_out)
    store(r.emb, r.emb_out)

    for cp in send_w:
        cp.wait_send()
    for s in range(seqs):
        for group in (toks, cots, n2s, bgs, brs, mls, n1s):
            group.close(s)
    for k, (buf, count) in enumerate(((r.msum, nt), (r.mg, nc), (r.emb, nc))):
        part = buf.at[0 : count - 1]
        remote(part, part, r.s_all.at[k], r.s_mc.at[c], dp=other).wait_send()

    def kv_sent(to):
        mine = r.kv.at[c]
        remote(mine, mine, r.s_kv.at[to], r.r_kv.at[c, 0], ctx=to).wait_send()

    each(nc, kv_sent, c + 1)

    def parts_sent(to):
        mine = r.dq_s.at[to]
        remote(mine, mine, r.s_dq.at[to], r.r_dq.at[c, 0], ctx=to).wait_send()

    each(nc - ((nc - 1 - c) // (nc - 1) if split else 0), parts_sent, c + 1)
    if split:

        @pl.when(last)
        def _():
            mine = r.kv.at[0]
            remote(mine, mine, r.s_q.at[0], r.r_q.at[nc - 1, 0], ctx=0).wait_send()

    def query_sent(to):
        for src, sems, recv in (
            (r.qd.at[:, :, 0:LANES], r.s_q.at[to], r.r_q.at[c, 0]),
            (r.qd.at[:, :, LANES : z.kvw], r.s_do.at[to], r.r_do.at[c, 0]),
            (r.lse.at[c], r.s_st.at[0, to], r.r_st.at[0, c, 0]),
            (r.delta.at[c], r.s_st.at[1, to], r.r_st.at[1, c, 0]),
        ):
            remote(src, src, sems, recv, ctx=to).wait_send()

    each(c, query_sent, skip)
    for cp in outs:
        cp.wait()


def finish_kernel(z, *refs):
    ins, outs, refs = refs[:6], refs[6:15], refs[15:]
    held, stage, sems = refs[:6], refs[6:15], refs[15]
    hw = z.hw
    fetches = [
        pltpu.make_async_copy(src, dst, sems.at[i]) for i, (src, dst) in enumerate(zip(ins, held))
    ]
    for i in (2, 3, 1, 0, 4, 5):
        fetches[i].start()
    ga, gb, emb, mg, res, gtok = held
    copies = []

    def put(i, value):
        stage[i][...] = value
        cp = pltpu.make_async_copy(stage[i], outs[i], sems.at[6 + i])
        cp.start()
        copies.append(cp)

    def through(i, src):
        cp = pltpu.make_async_copy(src, outs[i], sems.at[6 + i])
        cp.start()
        copies.append(cp)

    fetches[2].wait()
    fetches[3].wait()
    rest = mg[...].reshape(z.nc * 16, z.half)
    terms = []
    for _ in range(3):
        terms.append(rest.astype(BF16))
        rest = rest - terms[-1].astype(F32)
    terms = jnp.concatenate(terms, axis=0)
    row = lax.broadcasted_iota(jnp.int32, (8, z.half), 0)
    columns = []
    for k in range(z.thirds):
        left = []
        for c in range(z.nc):
            for d in range(2):
                one, two = emb[c, 2 * d : 2 * d + 1, :], emb[c, 2 * d + 1 : 2 * d + 2, :]
                left.append(
                    jnp.where(row == k, one, jnp.where(row == z.thirds + k, two, 0.0))
                )
        left = jnp.concatenate(left, axis=0).astype(BF16)
        columns.append(mm(jnp.concatenate([left] * 3, axis=0), terms, TN))
    put(8, jnp.concatenate(columns, axis=1))
    fetches[0].wait()
    put(6, ga[:, 0 : z.ff].astype(F32))
    put(7, ga[:, z.ff : 2 * z.ff].astype(F32))
    fetches[1].wait()
    for i in range(4):
        put(2 + i, gb[i * hw : (i + 1) * hw, :].astype(F32))
    fetches[4].wait()
    through(0, res)
    fetches[5].wait()
    through(1, gtok)
    for cp in copies:
        cp.wait()


IN_NAMES = (
    "tok_in",
    "ts_in",
    "wq_in",
    "wk_in",
    "wv_in",
    "wo_in",
    "wu_in",
    "wd_in",
    "wm_in",
    "cot_in",
)
OUT_NAMES = ("res_out", "gtok_out", "ga_out", "gb_out", "emb_out", "mg_out")


def solution(mesh):
    def shards(tokens, steps, wq, wk, wv, wo, wu, wd, wm, cot):
        wq, wk, wv, wo = wq.T, wk.T, wv.T, wo.T
        z = Dims(mesh, tokens.shape, wq.shape, wu.shape, wm.shape)
        table = scratch_table(z)
        names = list(IN_NAMES) + list(OUT_NAMES) + list(table)
        hbm = pl.BlockSpec(memory_space=pl.ANY)
        smem = pl.BlockSpec(memory_space=pltpu.SMEM)
        own = (z.seqs, z.rows, z.width)
        shape = jax.ShapeDtypeStruct
        outs = pl.pallas_call(
            functools.partial(layer_kernel, z, names),
            out_shape=(
                shape(own, BF16),
                shape(own, F32),
                shape((z.half, z.wide), BF16),
                shape((z.heads_rows, z.half), BF16),
                shape((z.nc, 8, z.half), F32),
                shape((z.nc, 2, 8, z.half), F32),
            ),
            in_specs=[hbm, smem] + [hbm] * 8,
            out_specs=[hbm] * 6,
            scratch_shapes=list(table.values()),
            compiler_params=pltpu.CompilerParams(
                collective_id=0, has_side_effects=True, vmem_limit_bytes=VMEM_BYTES
            ),
            name="layer",
        )(tokens, steps.T, wq, wk, wv, wo, wu, wd, wm, cot)
        outs = outs[2:] + outs[:2]
        shapes = (
            (own, BF16),
            (own, F32),
            ((z.hw, z.half), F32),
            ((z.hw, z.half), F32),
            ((z.hw, z.half), F32),
            ((z.hw, z.half), F32),
            ((z.half, z.ff), F32),
            ((z.half, z.ff), F32),
            ((z.half, z.mcols), F32),
        )
        done = pl.pallas_call(
            functools.partial(finish_kernel, z),
            out_shape=tuple(shape(*o) for o in shapes),
            in_specs=[hbm] * 6,
            out_specs=[hbm] * 9,
            scratch_shapes=[pltpu.VMEM(o.shape, o.dtype) for o in outs]
            + [pltpu.VMEM(*o) for o in shapes]
            + [pltpu.SemaphoreType.DMA((15,))],
            compiler_params=pltpu.CompilerParams(vmem_limit_bytes=VMEM_BYTES),
            name="finish",
        )(*outs)
        return done[:2] + tuple(g.T for g in done[2:6]) + done[6:]

    rows = P("dp", ("ctx", "tp"), None)
    cols = P("dp", "tp")
    return jax.shard_map(
        shards,
        mesh=mesh,
        in_specs=(rows, P("dp", "ctx")) + (cols,) * 6 + (P("dp", None), rows),
        out_specs=(rows, rows) + (cols,) * 7,
        check_vma=False,
    )
```
